32 devices in a mesh: gx: 4 (over y, x), gy: 4 (over z), gz: 2 (over core).
Axes of the slice: x: 2, y: 2, z: 4, core: 2. Of those that a mesh axis runs over, the one named last changes fastest.
Arguments:
- populations: float32 [19, 16, 32, 256], P(None, 'gx', 'gy', 'gz'), as said below
- solid: int32 [16, 32, 256], P('gx', 'gy', 'gz'), may hold values 0 or 1
- link_cell: int32 [4, 4, 2, 8, 16], P('gx', 'gy', 'gz'), may hold values from 0 to 4095, as said below
- link_dir: int32 [4, 4, 2, 8, 16], P('gx', 'gy', 'gz'), may hold values from 1 to 18, as said below
- link_node: int32 [4, 4, 2, 8, 16], P('gx', 'gy', 'gz'), may hold values from -1 to 511, as said below
- link_velocity: float32 [4, 4, 2, 3, 8, 16], P('gx', 'gy', 'gz'), may hold values from -1 to 1
- fabric_position: float32 [3, 4, 4096], P(None, 'gx', ('gy', 'gz')), may hold values from -6 to 6
- fabric_velocity: float32 [3, 4, 4096], P(None, 'gx', ('gy', 'gz')), may hold values from -2 to 2
- fabric_rest: float32 [3, 4, 4096], P(None, 'gx', ('gy', 'gz')), may hold values from -6 to 6
- triangles: int32 [3, 4, 7200], P(None, 'gx', ('gy', 'gz')), may hold values from 0 to 511, as said below
Outputs:
- populations_next: float32 [19, 16, 32, 256], P(None, 'gx', 'gy', 'gz')
- fabric_position_next: float32 [3, 4, 4096], P(None, 'gx', ('gy', 'gz'))
- fabric_velocity_next: float32 [3, 4, 4096], P(None, 'gx', ('gy', 'gz'))
- link_velocity_next: float32 [4, 4, 2, 3, 8, 16], P('gx', 'gy', 'gz')
The draws below stay inside these ranges and needn't reach their ends.
Inputs may be any that keep to these rules, and one draw needn't show every extreme that they name: `populations`: each entry lies between 0.55 and 1.45 times the lattice weight of its direction. `link_node`: -1 marks an empty slot; within one brick and owner the live slots come first; one owner (the same in every brick) receives 16 live links from every brick; the others receive any number from 0 to 16; live entries number the owner's 512 nodes. `link_cell`: A cell of the brick numbered (x * 8 + y) * 128 + z; no two slots of one brick name the same cell. `link_dir`: A moving direction. `triangles`: nodes of one triangle lie in one patch: patch k of an owner holds nodes k * 256 to (k + 1) * 256 - 1; every node belongs to some triangle.
All inputs are finite; a program needn't handle non-finite values. No bound on the sum of `solid` on one device may be relied on, other than what follows from the above.
Results may differ from the reference program's by a relative error of at most 0.0003.
Values sent between devices are 32-bit elements; how exact they have to be, the bound alone decides.
No kernel may reach another device: no remote copies, remote signals or barrier semaphores. Data moves between devices by JAX's collectives and lax.ppermute only.
A program may use at most 64 MiB of HBM per device.

```python
import jax
import jax.numpy as jnp
import numpy as np
from jax import lax

BX = 4
BY = 8
BZ = 128
CAP = 16
PSIDE = 16
PATCH_DEV = 2
PNODES = 256
NODES_DEV = 512
NTRI_DEV = 900
BRICKS_X = 4
BRICKS_Y = 4
BRICKS_Z = 2
OWNERS = 8
NX = 16
NY = 32
NZ = 256


def lattice_weights():
    return jnp.concatenate([jnp.full((1,), 1.0 / 3.0, jnp.float32), jnp.full((6,), 1.0 / 18.0, jnp.float32), jnp.full((12,), 1.0 / 36.0, jnp.float32)])


def draw_populations(key, part):
    shape = (19, NX, NY, NZ)
    factor = jax.random.uniform(key, shape, jnp.float32, 0.6, 1.4)
    return lattice_weights()[:, None, None, None] * factor


def link_tables(key):
    base = jax.random.fold_in(key, 11)
    key_load, key_count, key_star, key_node, key_cell, key_dir = jax.random.split(base, 6)
    bricks = BRICKS_X * BRICKS_Y * BRICKS_Z
    load = jax.random.randint(key_load, (bricks, 1), 1, 5)
    upper = CAP * load // 2 + 1
    counts = jnp.minimum(jax.random.randint(key_count, (bricks, OWNERS), 0, upper), CAP)
    star = jax.random.randint(key_star, (), 0, OWNERS)
    owner_ids = jnp.arange(OWNERS)
    counts = jnp.where(owner_ids[None, :] == star, CAP, counts)
    slots = jnp.arange(CAP)
    live = slots[None, None, :] < counts[:, :, None]
    star_slot = owner_ids[None, :, None] == star
    nodes = jax.random.randint(key_node, (bricks, OWNERS, CAP), 0, NODES_DEV)
    nodes = jnp.where(star_slot & (slots[None, None, :] == 0), NODES_DEV - 1, nodes)
    nodes = jnp.where(live, nodes, -1)
    cell_keys = jax.random.split(key_cell, bricks)
    orders = jax.vmap(lambda single: jax.random.permutation(single, BX * BY * BZ))(cell_keys)
    cells = orders[:, :OWNERS * CAP].reshape(bricks, OWNERS, CAP)
    dirs = jax.random.randint(key_dir, (bricks, OWNERS, CAP), 1, 19)
    dirs = jnp.where(star_slot & (slots[None, None, :] == 0), 18, dirs)
    dirs = jnp.where(star_slot & (slots[None, None, :] == 1), 1, dirs)
    shape = (BRICKS_X, BRICKS_Y, BRICKS_Z, OWNERS, CAP)
    return (cells.reshape(shape).astype(jnp.int32), dirs.reshape(shape).astype(jnp.int32), nodes.reshape(shape).astype(jnp.int32))


def draw_link_cell(key, part):
    return link_tables(key)[0]


def draw_link_dir(key, part):
    return link_tables(key)[1]


def draw_link_node(key, part):
    return link_tables(key)[2]


def draw_triangles(key, part):
    base = jax.random.fold_in(key, 23)
    key_perm, key_bits = jax.random.split(base)
    patches = BRICKS_X * OWNERS * PATCH_DEV
    quads = (PSIDE - 1) * (PSIDE - 1)
    perm_keys = jax.random.split(key_perm, patches)
    orders = jax.vmap(lambda single: jax.random.permutation(single, PNODES))(perm_keys)
    quad_i = jnp.arange(quads) // (PSIDE - 1)
    quad_j = jnp.arange(quads) % (PSIDE - 1)
    corner_a = quad_i * PSIDE + quad_j
    corner_b = corner_a + PSIDE
    corner_c = corner_a + 1
    corner_d = corner_b + 1
    bits = jax.random.randint(key_bits, (patches, quads), 0, 2) == 1
    first = jnp.stack([jnp.broadcast_to(corner_a, (patches, quads)), jnp.broadcast_to(corner_b, (patches, quads)), jnp.where(bits, corner_d, corner_c)])
    second = jnp.stack([jnp.where(bits, corner_a, corner_b), jnp.broadcast_to(corner_d, (patches, quads)), jnp.broadcast_to(corner_c, (patches, quads))])
    grid_ids = jnp.concatenate([first, second], axis=2)
    mapped = jax.vmap(lambda order, ids: order[ids], in_axes=(0, 1), out_axes=1)(orders, grid_ids)
    patch_local = (jnp.arange(patches) % PATCH_DEV)[None, :, None] * PNODES
    local = mapped + patch_local
    return local.reshape(3, BRICKS_X, OWNERS * NTRI_DEV).astype(jnp.int32)


def with_ends(values, own_key, low, top_value):
    extent = values.shape
    spot = [jax.random.randint(jax.random.fold_in(own_key, axis), (), 0, extent[axis]) for axis in range(len(extent))]
    values = values.at[tuple(spot)].set(low)
    longest = extent.index(max(extent))
    spot[longest] = (spot[longest] + 1) % extent[longest]
    return values.at[tuple(spot)].set(top_value)


def steps_of(rng, dims, cuts, low, largest):
    def one(dim, shards_of):
        steps = jax.random.uniform(jax.random.fold_in(jax.random.fold_in(rng, 6), dim), (shards_of,), jnp.float32, low / len(cuts), largest / len(cuts))
        return jnp.repeat(jnp.exp(steps), dims[dim] // shards_of).reshape((-1,) + (1,) * (len(dims) - dim - 1))

    level = one(*cuts[0])
    for cut in cuts[1:]:
        level = level * one(*cut)
    return level


def scatter_about(own_key, shape, spread, limit, cuts=(), held_as=jnp.bfloat16):
    result = spread * jax.random.normal(own_key, shape, jnp.float32)
    if cuts:
        result = result * steps_of(own_key, shape, cuts, -0.22, 0.18)
    return jnp.clip(result, -limit, limit).astype(held_as)


def setup_inputs(seed: int = 0) -> dict:
    splits = jax.random.split(jax.random.key(seed), 11)
    return {
        "populations": draw_populations(jax.random.fold_in(splits[10], 71), 0),
        "solid": with_ends((jax.random.randint(splits[1], (NX, NY, NZ), 0, 8) < 1).astype(jnp.int32), jax.random.fold_in(splits[1], 1), 0, 1),
        "link_cell": draw_link_cell(jax.random.fold_in(splits[10], 71), 0),
        "link_dir": draw_link_dir(jax.random.fold_in(splits[10], 71), 0),
        "link_node": draw_link_node(jax.random.fold_in(splits[10], 71), 0),
        "link_velocity": scatter_about(splits[5], (BRICKS_X, BRICKS_Y, BRICKS_Z, 3, OWNERS, CAP), 0.2, 1.0, ((0, 4), (1, 4), (2, 2)), jnp.float32),
        "fabric_position": scatter_about(splits[6], (3, BRICKS_X, OWNERS * NODES_DEV), 1.0, 6.0, ((1, 4), (2, 8)), jnp.float32),
        "fabric_velocity": scatter_about(splits[7], (3, BRICKS_X, OWNERS * NODES_DEV), 0.3, 2.0, ((1, 4), (2, 8)), jnp.float32),
        "fabric_rest": scatter_about(splits[8], (3, BRICKS_X, OWNERS * NODES_DEV), 1.0, 6.0, ((1, 4), (2, 8)), jnp.float32),
        "triangles": draw_triangles(jax.random.fold_in(splits[10], 71), 0),
    }


SPRING = 0.5
DAMPING = 0.1

DIRECTIONS = [[0, 0, 0], [1, 0, 0], [-1, 0, 0], [0, 1, 0], [0, -1, 0], [0, 0, 1], [0, 0, -1],
              [1, 1, 0], [-1, -1, 0], [1, -1, 0], [-1, 1, 0], [1, 0, 1], [-1, 0, -1], [1, 0, -1],
              [-1, 0, 1], [0, 1, 1], [0, -1, -1], [0, 1, -1], [0, -1, 1]]


def lattice():
    velocity_np = np.array(DIRECTIONS)
    weight_np = np.array([1.0 / 3.0] + [1.0 / 18.0] * 6 + [1.0 / 36.0] * 12)
    opposite_list = [DIRECTIONS.index([-entry for entry in DIRECTIONS[direction]]) for direction in range(19)]
    along_a = np.array([float(entry[0]) for entry in DIRECTIONS])
    along_b = np.array([float(entry[1]) for entry in DIRECTIONS])
    along_e = np.array([float(entry[2]) for entry in DIRECTIONS])
    speed_sq = along_a * along_a + along_b * along_b + along_e * along_e
    moment_rows = [np.ones(19), 19 * speed_sq - 30, (21 * speed_sq * speed_sq - 53 * speed_sq + 24) / 2,
                   along_a, (5 * speed_sq - 9) * along_a, along_b, (5 * speed_sq - 9) * along_b,
                   along_e, (5 * speed_sq - 9) * along_e, 3 * along_a * along_a - speed_sq,
                   (3 * speed_sq - 5) * (3 * along_a * along_a - speed_sq), along_b * along_b - along_e * along_e,
                   (3 * speed_sq - 5) * (along_b * along_b - along_e * along_e), along_a * along_b,
                   along_b * along_e, along_a * along_e, (along_b * along_b - along_e * along_e) * along_a,
                   (along_e * along_e - along_a * along_a) * along_b, (along_a * along_a - along_b * along_b) * along_e]
    moment_np = np.stack(moment_rows)
    inverse_np = moment_np.T / np.sum(moment_np * moment_np, axis=1)[None, :]
    viscous = 5.0 / 3.0
    rates_np = np.array([0.0, 1.19, 1.4, 0.0, 1.2, 0.0, 1.2, 0.0, 1.2, viscous, 1.4, viscous, 1.4,
                         viscous, viscous, viscous, 1.98, 1.98, 1.98])
    return velocity_np, weight_np, opposite_list, moment_np, inverse_np, rates_np


def collide_cells(popul, solid_flat):
    velocity_np, weight_np, opposite_list, moment_np, inverse_np, rates_np = lattice()
    velocity_table = jnp.asarray(velocity_np, jnp.float32)
    weight_table = jnp.asarray(weight_np, jnp.float32)
    density = jnp.sum(popul, axis=0)
    momentum = jnp.dot(velocity_table.T, popul, precision=lax.Precision.HIGHEST, preferred_element_type=jnp.float32)
    flow = momentum / density
    projected = jnp.dot(velocity_table, flow, precision=lax.Precision.HIGHEST, preferred_element_type=jnp.float32)
    speed_sq = jnp.sum(flow * flow, axis=0)
    equilibrium = weight_table[:, None] * density * (1.0 + 3.0 * projected + 4.5 * projected * projected - 1.5 * speed_sq)
    offset = popul - equilibrium
    moments = jnp.dot(jnp.asarray(moment_np, jnp.float32), offset, precision=lax.Precision.HIGHEST, preferred_element_type=jnp.float32)
    relaxed = jnp.asarray(rates_np, jnp.float32)[:, None] * moments
    change = jnp.dot(jnp.asarray(inverse_np, jnp.float32), relaxed, precision=lax.Precision.HIGHEST, preferred_element_type=jnp.float32)
    return jnp.where(solid_flat[None, :] == 1, popul, popul - change)


def membrane(positions, rest, triangle_nodes):
    force = jnp.zeros(positions.shape, jnp.float32)
    for first, second in ((0, 1), (1, 2), (2, 0)):
        head = triangle_nodes[first]
        tail = triangle_nodes[second]
        stretch = (positions[:, tail] - positions[:, head]) - (rest[:, tail] - rest[:, head])
        force = force.at[:, head].add(SPRING * stretch)
        force = force.at[:, tail].add(-SPRING * stretch)
    return force


def reference(populations, solid, link_cell, link_dir, link_node, link_velocity, fabric_position, fabric_velocity, fabric_rest, triangles):
    velocity_np, weight_np, opposite_list, moment_np, inverse_np, rates_np = lattice()
    velocity_table = jnp.asarray(velocity_np, jnp.float32)
    weight_table = jnp.asarray(weight_np, jnp.float32)
    opposite_table = jnp.asarray(opposite_list, jnp.int32)

    def plane_step(pair):
        plane_pop, plane_solid = pair
        flat = collide_cells(plane_pop.reshape(19, -1), plane_solid.reshape(-1))
        return flat.reshape(plane_pop.shape)

    planes = jnp.moveaxis(populations, 1, 0)
    post = jnp.moveaxis(lax.map(plane_step, (planes, solid)), 0, 1)

    padded = jnp.pad(post, ((0, 0), (1, 1), (0, 0), (0, 0)), mode="wrap")
    padded = jnp.pad(padded, ((0, 0), (0, 0), (1, 1), (1, 1)))
    rows_y = jnp.arange(NY + 2)
    rows_z = jnp.arange(NZ + 2)
    outside = ((rows_y == 0) | (rows_y == NY + 1))[:, None] | ((rows_z == 0) | (rows_z == NZ + 1))[None, :]
    padded = jnp.where(outside[None, None], weight_table[:, None, None, None], padded)
    pieces = []
    for direction in range(19):
        shift_x = DIRECTIONS[direction][0]
        shift_y = DIRECTIONS[direction][1]
        shift_z = DIRECTIONS[direction][2]
        pieces.append(padded[direction, 1 - shift_x:1 - shift_x + NX, 1 - shift_y:1 - shift_y + NY, 1 - shift_z:1 - shift_z + NZ])
    propagated = jnp.stack(pieces)

    live = link_node >= 0
    brick_x = jnp.arange(BRICKS_X).astype(jnp.int32).reshape(-1, 1, 1, 1, 1)
    brick_y = jnp.arange(BRICKS_Y).astype(jnp.int32).reshape(1, -1, 1, 1, 1)
    brick_z = jnp.arange(BRICKS_Z).astype(jnp.int32).reshape(1, 1, -1, 1, 1)
    owner_axis = jnp.arange(OWNERS).astype(jnp.int32).reshape(1, 1, 1, -1, 1)
    coord_x = brick_x * BX + link_cell // (BY * BZ)
    coord_y = brick_y * BY + (link_cell // BZ) % BY
    coord_z = brick_z * BZ + link_cell % BZ
    reflected = post[opposite_table[link_dir], coord_x, coord_y, coord_z]
    link_unit = velocity_table[link_dir]
    wall = jnp.moveaxis(link_velocity, 3, -1)
    returned = reflected + 6.0 * weight_table[link_dir] * jnp.sum(link_unit * wall, axis=-1)
    populations_next = propagated.at[jnp.where(live, link_dir, 19), coord_x, coord_y, coord_z].set(returned, mode="drop")
    link_force = -link_unit * (reflected + returned)[..., None]

    slab = OWNERS * NODES_DEV
    total_nodes = BRICKS_X * slab
    node_global = brick_x * slab + owner_axis * NODES_DEV + jnp.where(live, link_node, 0)
    target = jnp.where(live, node_global, total_nodes).reshape(-1)
    fluid_force = jnp.zeros((3, total_nodes), jnp.float32).at[:, target].add(link_force.reshape(-1, 3).T, mode="drop")

    positions = fabric_position.reshape(3, total_nodes)
    velocities = fabric_velocity.reshape(3, total_nodes)
    rest = fabric_rest.reshape(3, total_nodes)
    tri_offset = jnp.arange(BRICKS_X).astype(jnp.int32)[:, None] * slab + (jnp.arange(OWNERS * NTRI_DEV).astype(jnp.int32) // NTRI_DEV)[None, :] * NODES_DEV
    global_tri = (triangles + tri_offset[None]).reshape(3, -1)
    elastic = membrane(positions, rest, global_tri)
    velocity_next = (1.0 - DAMPING) * velocities + (fluid_force + elastic)
    position_next = positions + velocity_next

    reply = jnp.where(live[None], velocity_next[:, node_global], 0.0)
    link_velocity_next = jnp.moveaxis(reply, 0, 3)
    return (populations_next, position_next.reshape(fabric_position.shape),
            velocity_next.reshape(fabric_velocity.shape), link_velocity_next)
```

```python
import jax
import jax.numpy as jnp
import numpy as np
from jax import lax
from jax.experimental import pallas as pl
from jax.experimental.pallas import tpu as pltpu
from jax.sharding import PartitionSpec as P

SPRING = 0.5
DAMPING = 0.1
DIRECTIONS = [
    [0, 0, 0],
    [1, 0, 0],
    [-1, 0, 0],
    [0, 1, 0],
    [0, -1, 0],
    [0, 0, 1],
    [0, 0, -1],
    [1, 1, 0],
    [-1, -1, 0],
    [1, -1, 0],
    [-1, 1, 0],
    [1, 0, 1],
    [-1, 0, -1],
    [1, 0, -1],
    [-1, 0, 1],
    [0, 1, 1],
    [0, -1, -1],
    [0, 1, -1],
    [0, -1, 1],
]


def extended(cells, sides, width):
    for axis, dim in sides:
        count = lax.axis_size(axis)
        head = lax.slice_in_dim(cells, 0, width, axis=dim)
        tail = lax.slice_in_dim(cells, cells.shape[dim] - width, cells.shape[dim], axis=dim)
        cells = jnp.concatenate(
            [
                lax.ppermute(tail, axis, [(i, (i + 1) % count) for i in range(count)]),
                cells,
                lax.ppermute(head, axis, [((i + 1) % count, i) for i in range(count)]),
            ],
            axis=dim,
        )
    return cells


def lattice():
    velocity_np = np.array(DIRECTIONS)
    weight_np = np.array([1.0 / 3.0] + [1.0 / 18.0] * 6 + [1.0 / 36.0] * 12)
    opposite_list = [
        DIRECTIONS.index([-entry for entry in DIRECTIONS[direction]]) for direction in range(19)
    ]
    along_a = np.array([float(entry[0]) for entry in DIRECTIONS])
    along_b = np.array([float(entry[1]) for entry in DIRECTIONS])
    along_e = np.array([float(entry[2]) for entry in DIRECTIONS])
    speed_sq = along_a * along_a + along_b * along_b + along_e * along_e
    moment_rows = [
        np.ones(19),
        19 * speed_sq - 30,
        (21 * speed_sq * speed_sq - 53 * speed_sq + 24) / 2,
        along_a,
        (5 * speed_sq - 9) * along_a,
        along_b,
        (5 * speed_sq - 9) * along_b,
        along_e,
        (5 * speed_sq - 9) * along_e,
        3 * along_a * along_a - speed_sq,
        (3 * speed_sq - 5) * (3 * along_a * along_a - speed_sq),
        along_b * along_b - along_e * along_e,
        (3 * speed_sq - 5) * (along_b * along_b - along_e * along_e),
        along_a * along_b,
        along_b * along_e,
        along_a * along_e,
        (along_b * along_b - along_e * along_e) * along_a,
        (along_e * along_e - along_a * along_a) * along_b,
        (along_a * along_a - along_b * along_b) * along_e,
    ]
    moment_np = np.stack(moment_rows)
    inverse_np = moment_np.T / np.sum(moment_np * moment_np, axis=1)[None, :]
    viscous = 5.0 / 3.0
    rates_np = np.array(
        [
            0.0,
            1.19,
            1.4,
            0.0,
            1.2,
            0.0,
            1.2,
            0.0,
            1.2,
            viscous,
            1.4,
            viscous,
            1.4,
            viscous,
            viscous,
            viscous,
            1.98,
            1.98,
            1.98,
        ]
    )
    return (velocity_np, weight_np, opposite_list, moment_np, inverse_np, rates_np)


def collide_cells(popul, solid_flat):
    velocity_np, weight_np, opposite_list, moment_np, inverse_np, rates_np = lattice()
    velocity_table = jnp.asarray(velocity_np, jnp.float32)
    weight_table = jnp.asarray(weight_np, jnp.float32)
    density = jnp.sum(popul, axis=0)
    momentum = jnp.dot(
        velocity_table.T, popul, precision=lax.Precision.HIGHEST, preferred_element_type=jnp.float32
    )
    flow = momentum / density
    projected = jnp.dot(
        velocity_table, flow, precision=lax.Precision.HIGHEST, preferred_element_type=jnp.float32
    )
    speed_sq = jnp.sum(flow * flow, axis=0)
    equilibrium = (
        weight_table[:, None]
        * density
        * (1.0 + 3.0 * projected + 4.5 * projected * projected - 1.5 * speed_sq)
    )
    offset = popul - equilibrium
    moments = jnp.dot(
        jnp.asarray(moment_np, jnp.float32),
        offset,
        precision=lax.Precision.HIGHEST,
        preferred_element_type=jnp.float32,
    )
    relaxed = jnp.asarray(rates_np, jnp.float32)[:, None] * moments
    change = jnp.dot(
        jnp.asarray(inverse_np, jnp.float32),
        relaxed,
        precision=lax.Precision.HIGHEST,
        preferred_element_type=jnp.float32,
    )
    return jnp.where(solid_flat[None, :] == 1, popul, popul - change)


def fill_outside(padded, weight_np):
    span_y = padded.shape[2]
    span_z = padded.shape[3]
    place_y = lax.axis_index("gy")
    place_z = lax.axis_index("gz")
    count_y = lax.axis_size("gy")
    count_z = lax.axis_size("gz")
    rows_y = jnp.arange(span_y)
    rows_z = jnp.arange(span_z)
    out_y = (rows_y == 0) & (place_y == 0) | (rows_y == span_y - 1) & (place_y == count_y - 1)
    out_z = (rows_z == 0) & (place_z == 0) | (rows_z == span_z - 1) & (place_z == count_z - 1)
    outside = out_y[:, None] | out_z[None, :]
    return jnp.where(
        outside[None, None], jnp.asarray(weight_np, jnp.float32)[:, None, None, None], padded
    )


def propagate(padded, size_x, size_y, size_z):
    pieces = []
    for direction in range(19):
        shift_x = DIRECTIONS[direction][0]
        shift_y = DIRECTIONS[direction][1]
        shift_z = DIRECTIONS[direction][2]
        plane = padded[direction]
        pieces.append(
            lax.slice(
                plane,
                (1 - shift_x, 1 - shift_y, 1 - shift_z),
                (1 - shift_x + size_x, 1 - shift_y + size_y, 1 - shift_z + size_z),
            )
        )
    return jnp.stack(pieces)


def membrane(positions, rest, triangle_nodes):
    force = jnp.zeros(positions.shape, jnp.float32)
    for first, second in ((0, 1), (1, 2), (2, 0)):
        head = triangle_nodes[first]
        tail = triangle_nodes[second]
        stretch = positions[:, tail] - positions[:, head] - (rest[:, tail] - rest[:, head])
        force = force.at[:, head].add(SPRING * stretch)
        force = force.at[:, tail].add(-SPRING * stretch)
    return force


def general_body(
    populations,
    solid,
    link_cell,
    link_dir,
    link_node,
    link_velocity,
    fabric_position,
    fabric_velocity,
    fabric_rest,
    triangles,
):
    velocity_np, weight_np, opposite_list, moment_np, inverse_np, rates_np = lattice()
    velocity_table = jnp.asarray(velocity_np, jnp.float32)
    weight_table = jnp.asarray(weight_np, jnp.float32)
    opposite_table = jnp.asarray(opposite_list, jnp.int32)
    size_x = populations.shape[1]
    size_y = populations.shape[2]
    size_z = populations.shape[3]
    cells = size_x * size_y * size_z
    post = collide_cells(populations.reshape(19, cells), solid.reshape(cells)).reshape(
        populations.shape
    )
    padded = extended(post, (("gx", 1), ("gy", 2), ("gz", 3)), 1)
    padded = fill_outside(padded, weight_np)
    propagated = propagate(padded, size_x, size_y, size_z).reshape(19, cells)
    owners_n = link_node.shape[3]
    capacity = link_node.shape[4]
    node_rows = link_node.reshape(owners_n, capacity)
    cell_rows = link_cell.reshape(owners_n, capacity)
    dir_rows = link_dir.reshape(owners_n, capacity)
    live = node_rows >= 0
    post_flat = post.reshape(19, cells)
    reflected = post_flat[opposite_table[dir_rows], cell_rows]
    link_unit = velocity_table[dir_rows]
    wall = jnp.moveaxis(link_velocity.reshape(3, owners_n, capacity), 0, -1)
    returned = reflected + 6.0 * weight_table[dir_rows] * jnp.sum(link_unit * wall, axis=-1)
    populations_next = propagated.at[jnp.where(live, dir_rows, 19), cell_rows].set(
        returned, mode="drop"
    )
    strength = reflected + returned
    positions = fabric_position.reshape(3, -1)
    velocities = fabric_velocity.reshape(3, -1)
    rest = fabric_rest.reshape(3, -1)
    nodes_n = positions.shape[1]
    elastic = membrane(positions, rest, triangles.reshape(3, -1))
    link_force = jnp.moveaxis(-link_unit * strength[..., None], -1, 0)
    got_nodes, got_force = (
        lax.all_to_all(node_rows[None], ("gy", "gz"), split_axis=1, concat_axis=1, tiled=True),
        lax.all_to_all(link_force, ("gy", "gz"), split_axis=1, concat_axis=1, tiled=True),
    )
    got_ids = got_nodes[0]
    got_live = got_ids >= 0
    target = jnp.where(got_live, got_ids, nodes_n).reshape(-1)
    fluid_force = (
        jnp.zeros((3, nodes_n), jnp.float32)
        .at[:, target]
        .add(got_force.reshape(3, -1), mode="drop")
    )
    velocity_next = (1.0 - DAMPING) * velocities + (fluid_force + elastic)
    position_next = positions + velocity_next
    reply = jnp.where(got_live[None], velocity_next[:, jnp.where(got_live, got_ids, 0)], 0.0)
    wall_next = lax.all_to_all(reply, ("gy", "gz"), split_axis=1, concat_axis=1, tiled=True)
    return (
        populations_next.reshape(populations.shape),
        position_next.reshape(fabric_position.shape),
        velocity_next.reshape(fabric_velocity.shape),
        wall_next.reshape(link_velocity.shape),
    )


WEIGHTS = [1.0 / 3.0] + [1.0 / 18.0] * 6 + [1.0 / 36.0] * 12
OPPOSITE = [DIRECTIONS.index([-entry for entry in d]) for d in DIRECTIONS]
SIDES = [
    ([i for i in range(19) if DIRECTIONS[i][a] == 1], [i for i in range(19) if DIRECTIONS[i][a] == -1])
    for a in range(3)
]
LANES = 128
FAB = 16


def iota(shape, axis):
    return lax.broadcasted_iota(jnp.int32, shape, axis)


def split3(value):
    high = value.astype(jnp.bfloat16).astype(jnp.float32)
    rest = value - high
    middle = rest.astype(jnp.bfloat16).astype(jnp.float32)
    return high, middle, rest - middle


def stacked3(value):
    return jnp.concatenate(split3(value), axis=0).astype(jnp.bfloat16)


def sum3(value):
    rows = value.shape[0] // 3
    return value[:rows] + value[rows : 2 * rows] + value[2 * rows :]


def dot_nn(left, right):
    return lax.dot_general(left, right, (((1,), (0,)), ((), ())), preferred_element_type=jnp.float32)


def dot_nt(left, right):
    return lax.dot_general(left, right, (((1,), (1,)), ((), ())), preferred_element_type=jnp.float32)


def one_hot(mask):
    return jnp.where(mask, 1.0, 0.0).astype(jnp.bfloat16)


def collided(f, solid):
    sx, dx = f[1] + f[2], f[1] - f[2]
    sy, dy = f[3] + f[4], f[3] - f[4]
    sz, dz = f[5] + f[6], f[5] - f[6]
    sa, da = f[7] + f[8], f[7] - f[8]
    sb, db = f[9] + f[10], f[9] - f[10]
    sc, dc = f[11] + f[12], f[11] - f[12]
    sd, dd = f[13] + f[14], f[13] - f[14]
    se, de = f[15] + f[16], f[15] - f[16]
    sg, dg = f[17] + f[18], f[17] - f[18]
    sxy, txy = sa + sb, sa - sb
    sxz, txz = sc + sd, sc - sd
    syz, tyz = se + sg, se - sg
    ax_ab, ay_ab = da + db, da - db
    ax_cd, az_cd = dc + dd, dc - dd
    ay_eg, az_eg = de + dg, de - dg
    near, far = sx + sy + sz, sxy + sxz + syz
    rho = f[0] + near + far
    ex, ey, ez = ax_ab + ax_cd, ay_ab + ay_eg, az_cd + az_eg
    jx, jy, jz = dx + ex, dy + ey, dz + ez
    inv = 1.0 / rho
    ux, uy, uz = jx * inv, jy * inv, jz * inv
    xx, yy, zz = jx * ux, jy * uy, jz * uz
    jj = xx + yy + zz
    energy = (-30.0 * f[0] - 11.0 * near + 8.0 * far) - (-11.0 * rho + 19.0 * jj)
    square = (12.0 * f[0] - 4.0 * near + far) - (3.0 * rho - 5.5 * jj)
    kx = (1.2 / 40.0) * (ex - 4.0 * dx + (2.0 / 3.0) * jx)
    ky = (1.2 / 40.0) * (ey - 4.0 * dy + (2.0 / 3.0) * jy)
    kz = (1.2 / 40.0) * (ez - 4.0 * dz + (2.0 / 3.0) * jz)
    yz_near, xyz_far = sy + sz, sxy + sxz - 2.0 * syz
    pxx_eq = 2.0 * xx - yy - zz
    pww_eq = yy - zz
    pxx = (5.0 / 3.0 / 36.0) * (2.0 * sx - yz_near + xyz_far - pxx_eq)
    pixx = (1.4 / 72.0) * (-4.0 * sx + 2.0 * yz_near + xyz_far + 0.5 * pxx_eq)
    w_near, w_far = sy - sz, sxy - sxz
    pww = (5.0 / 3.0 / 12.0) * (w_near + w_far - pww_eq)
    piww = (1.4 / 24.0) * (w_far - 2.0 * w_near + 0.5 * pww_eq)
    pxy = (5.0 / 3.0 / 4.0) * (txy - jx * uy)
    pyz = (5.0 / 3.0 / 4.0) * (tyz - jy * uz)
    pxz = (5.0 / 3.0 / 4.0) * (txz - jx * uz)
    mx = (1.98 / 8.0) * (ax_ab - ax_cd)
    my = (1.98 / 8.0) * (ay_eg - ay_ab)
    mz = (1.98 / 8.0) * (az_cd - az_eg)
    energy = (1.19 / 2394.0) * energy
    square = (1.4 / 252.0) * square
    axis = -11.0 * energy - 4.0 * square
    across = pxx - 2.0 * pixx
    split = pww - 2.0 * piww
    edge = 8.0 * energy + square
    pp, ww = pxx + pixx, pww + piww
    even = [
        axis + 2.0 * across,
        axis - across + split,
        axis - across - split,
        edge + pp + ww + pxy,
        edge + pp + ww - pxy,
        edge + pp - ww + pxz,
        edge + pp - ww - pxz,
        edge - 2.0 * pp + pyz,
        edge - 2.0 * pp - pyz,
    ]
    odd = [
        -4.0 * kx,
        -4.0 * ky,
        -4.0 * kz,
        (kx + mx) + (ky - my),
        (kx + mx) - (ky - my),
        (kx - mx) + (kz + mz),
        (kx - mx) - (kz + mz),
        (ky + my) + (kz - mz),
        (ky + my) - (kz - mz),
    ]
    change = [12.0 * square - 30.0 * energy]
    for pair in range(9):
        change += [even[pair] + odd[pair], even[pair] - odd[pair]]
    fluid = solid != 1
    return [jnp.where(fluid, f[i] - change[i], f[i]) for i in range(19)]


def collide_kernel(pop_ref, solid_ref, post_ref, up_ref, down_ref):
    size_x = pop_ref.shape[1]
    for x in range(size_x):
        post = collided([pop_ref[i, x] for i in range(19)], solid_ref[x])
        for i in range(19):
            post_ref[i, x] = post[i]
            if x == size_x - 1 and i in SIDES[0][0]:
                up_ref[SIDES[0][0].index(i)] = post[i]
            if x == 0 and i in SIDES[0][1]:
                down_ref[SIDES[0][1].index(i)] = post[i]


def slots_to_row(value):
    owners, capacity = value.shape
    wide = jnp.concatenate([value, jnp.zeros((owners, LANES - capacity), value.dtype)], axis=1)
    return jnp.sum(pltpu.roll(wide, 0, 1, stride=capacity, stride_axis=0), axis=0, keepdims=True)


def fabric_kernel(
    post_ref, cell_ref, dir_ref, node_ref, wall_ref, pos_ref, vel_ref, rest_ref, tri_ref,
    fab_ref, kind_ref, back_ref,
):
    size_x = post_ref.shape[1]
    size_y = post_ref.shape[2]
    rows = size_x * size_y
    cell = slots_to_row(cell_ref[0, 0, 0].astype(jnp.float32)).astype(jnp.int32)
    way = slots_to_row(dir_ref[0, 0, 0].astype(jnp.float32))
    node = slots_to_row(node_ref[0, 0, 0].astype(jnp.float32))
    live = node >= 0.0
    unit = []
    for a in range(3):
        u = jnp.zeros_like(way)
        for i in range(1, 19):
            if DIRECTIONS[i][a]:
                u = jnp.where(way == float(i), float(DIRECTIONS[i][a]), u)
        unit.append(u)
    weight = jnp.where(way >= 7.0, 6.0 / 36.0, 6.0 / 18.0)
    wall = [slots_to_row(wall_ref[0, 0, 0, a]) for a in range(3)]
    term = weight * (unit[0] * wall[0] + unit[1] * wall[1] + unit[2] * wall[2])
    at_row = jnp.where((iota((rows, LANES), 0) == (cell >> 7)) & live, 1.0, 0.0)
    at_lane = one_hot(iota((LANES, LANES), 0) == (cell & (LANES - 1)))
    left = jnp.concatenate([at_row * way] + [at_row * t for t in split3(term)], axis=0)
    maps = dot_nt(left.astype(jnp.bfloat16), at_lane)
    kind = maps[:rows]
    added = sum3(maps[rows:])
    taken = []
    for x in range(size_x):
        k = kind[x * size_y : (x + 1) * size_y]
        t = jnp.zeros_like(k)
        for i in range(1, 19):
            t = jnp.where(k == float(i), post_ref[OPPOSITE[i], x], t)
        taken.append(t)
        kind_ref[x] = k
        back_ref[x] = t + added[x * size_y : (x + 1) * size_y]
    strength = 2.0 * jnp.concatenate(taken, axis=0) + added
    at_link = sum3(dot_nn(stacked3(strength), at_lane))
    push = jnp.sum(at_row * at_link, axis=0, keepdims=True)
    fab_ref[0:1] = node
    for a in range(3):
        fab_ref[1 + a : 2 + a] = -unit[a] * push

    nodes = pos_ref.shape[2]
    count = tri_ref.shape[2]
    wide = -(-count // LANES) * LANES
    stretch = [pos_ref[a] - rest_ref[a] for a in range(3)]
    corners = [
        jnp.concatenate([tri_ref[t], jnp.full((1, wide - count), -1, jnp.int32)], axis=1) for t in range(3)
    ]
    node_ids = iota((nodes, wide), 0)
    hits = sum(jnp.where(node_ids == corner, 1.0, 0.0) for corner in corners).astype(jnp.bfloat16)
    stretch8 = jnp.concatenate(stretch + [jnp.zeros((5, nodes), jnp.float32)], axis=0)
    total = sum3(dot_nn(stacked3(stretch8), hits))
    total = jnp.where(iota(total.shape, 0) == 3, 1.0, total)
    back = sum3(dot_nt(stacked3(total), hits))
    for a in range(3):
        elastic = SPRING * back[a : a + 1] - 3.0 * SPRING * back[3:4] * stretch[a]
        base = (1.0 - DAMPING) * vel_ref[a] + elastic
        for k in range(nodes // LANES):
            row = 4 + a * (nodes // LANES) + k
            fab_ref[row : row + 1] = base[:, k * LANES : (k + 1) * LANES]


def source_tile(post_ref, low_ref, high_ref, i, x):
    size_x = post_ref.shape[1]
    from_x = x - DIRECTIONS[i][0]
    if from_x < 0:
        return low_ref.at[SIDES[0][0].index(i)]
    if from_x >= size_x:
        return high_ref.at[SIDES[0][1].index(i)]
    return post_ref.at[i, from_x]


def side_kernel(post_ref, low_ref, high_ref, fab_ref, up_ref, down_ref):
    size_x = post_ref.shape[1]
    size_y = post_ref.shape[2]
    for out_ref, side, row in ((up_ref, 0, size_y - 1), (down_ref, 1, 0)):
        out_ref[:FAB] = fab_ref[...]
        for k, i in enumerate(SIDES[1][side]):
            for x in range(size_x):
                at = FAB + k * size_x + x
                out_ref[at : at + 1] = source_tile(post_ref, low_ref, high_ref, i, x)[row : row + 1]
        end = FAB + 5 * size_x
        if out_ref.shape[0] > end:
            out_ref[end:] = jnp.zeros((out_ref.shape[0] - end, LANES), jnp.float32)


def shift_kernel(
    post_ref, xlow_ref, xhigh_ref, fab_ref, below_ref, above_ref, across_ref,
    rolled_ref, face_ref, slab_ref,
):
    size_x = post_ref.shape[1]
    size_y = post_ref.shape[2]
    place_y = lax.axis_index("gy")
    place_z = lax.axis_index("gz")
    count_y = lax.axis_size("gy")
    sub = iota((size_y, LANES), 0)
    lane = iota((size_y, LANES), 1)
    first, last = place_y == 0, place_y == count_y - 1
    for x in range(size_x):
        up = jnp.zeros((size_y, LANES), jnp.float32)
        down = jnp.zeros((size_y, LANES), jnp.float32)
        for i in range(19):
            tile = source_tile(post_ref, xlow_ref, xhigh_ref, i, x)[...]
            if DIRECTIONS[i][1] == 1:
                at = FAB + SIDES[1][0].index(i) * size_x + x
                row = jnp.where(first, WEIGHTS[i], below_ref[at : at + 1])
                tile = jnp.where(sub == 0, row, pltpu.roll(tile, 1, 0))
            if DIRECTIONS[i][1] == -1:
                at = FAB + SIDES[1][1].index(i) * size_x + x
                row = jnp.where(last, WEIGHTS[i], above_ref[at : at + 1])
                tile = jnp.where(sub == size_y - 1, row, pltpu.roll(tile, size_y - 1, 0))
            if DIRECTIONS[i][2] == 1:
                k = SIDES[2][0].index(i)
                tile = pltpu.roll(tile, 1, 1)
                up = jnp.where(lane == k, pltpu.roll(tile, k, 1) if k else tile, up)
            if DIRECTIONS[i][2] == -1:
                k = SIDES[2][1].index(i)
                tile = pltpu.roll(tile, LANES - 1, 1)
                down = jnp.where(lane == k, pltpu.roll(tile, k + 1, 1), down)
            rolled_ref[i, x] = tile
        face_ref[x] = jnp.where(place_z == 0, up, down)
    slab_ref[place_y] = fab_ref[...]
    slab_ref[lax.rem(place_y + count_y - 1, count_y)] = below_ref[:FAB]
    slab_ref[lax.rem(place_y + 1, count_y)] = above_ref[:FAB]
    slab_ref[lax.rem(place_y + 2, count_y)] = across_ref[...]


def final_kernel(
    rolled_ref, face_ref, kind_ref, back_ref, own_ref, other_ref, pos_ref,
    pop_ref, pos_out_ref, vel_out_ref, wall_out_ref,
):
    size_x = rolled_ref.shape[1]
    size_y = rolled_ref.shape[2]
    place_y = lax.axis_index("gy")
    place_z = lax.axis_index("gz")
    count_y = lax.axis_size("gy")
    lane = iota((size_y, LANES), 1)
    low_end = place_z == 0
    for x in range(size_x):
        kind = kind_ref[x]
        back = back_ref[x]
        face = face_ref[x]
        for i in range(19):
            tile = rolled_ref[i, x]
            if DIRECTIONS[i][2] == 1:
                k = SIDES[2][0].index(i)
                halo = pltpu.roll(face, LANES - k, 1) if k else face
                tile = jnp.where(lane == 0, jnp.where(low_end, WEIGHTS[i], halo), tile)
            if DIRECTIONS[i][2] == -1:
                k = SIDES[2][1].index(i)
                halo = pltpu.roll(face, LANES - 1 - k, 1)
                tile = jnp.where(lane == LANES - 1, jnp.where(low_end, halo, WEIGHTS[i]), tile)
            if i:
                tile = jnp.where(kind == float(i), back, tile)
            pop_ref[i, x] = tile

    owners, capacity = wall_out_ref.shape[4], wall_out_ref.shape[5]
    nodes = pos_ref.shape[2]
    parts = nodes // LANES
    slot_owner = iota((1, LANES), 1) // capacity
    owner_base = (slot_owner * nodes).astype(jnp.float32)
    mine = own_ref[place_y]
    my_node = mine[0:1]
    my_live = my_node >= 0.0
    my_id = jnp.where(my_live, owner_base + my_node, -2.0)
    my_column = jnp.transpose(jnp.broadcast_to(my_id, (LANES, LANES)))
    me = place_y * 2 + place_z
    matches, forces, picked = [], [], jnp.zeros((8, LANES), jnp.float32)
    for group, ref in ((0, own_ref), (1, other_ref)):
        for y in range(count_y):
            m = group * count_y + y
            tile = ref[y, 0:8]
            ids = tile[0:1]
            ids = jnp.where(ids >= 0.0, owner_base + ids, -1.0)
            matches.append(one_hot(my_column == ids))
            forces.append(tile)
            shift = lax.rem((m + owners - me) * capacity, LANES)
            picked = jnp.where(slot_owner == m, pltpu.roll(tile, shift, 1), picked)
    force = stacked3(jnp.concatenate(forces, axis=1))
    fluid_at_links = sum3(dot_nt(force, jnp.concatenate(matches, axis=1)))

    every = jnp.concatenate(
        [own_ref[...].reshape(count_y * FAB, LANES), other_ref[...].reshape(count_y * FAB, LANES)], axis=0
    )
    my_int = my_node.astype(jnp.int32)
    at_lane = one_hot(iota((LANES, LANES), 0) == (my_int & (LANES - 1)))
    found = sum3(dot_nn(stacked3(every), at_lane))
    row = iota(found.shape, 0)
    message, inner = row // FAB, row % FAB
    owner = (message % count_y) * 2 + jnp.where(message < count_y, place_z, 1 - place_z)
    fits = (owner == slot_owner) & (inner >= 4) & (inner % parts == (my_int >> 7))
    found = jnp.where(fits, found, 0.0)
    found = sum(found[m * FAB : (m + 1) * FAB] for m in range(2 * count_y))

    node = picked[0:1].astype(jnp.int32)
    row = iota((FAB, LANES), 0)
    spread = jnp.where(row < parts, picked[1:2], jnp.where(row < 2 * parts, picked[2:3], picked[3:4]))
    spread = jnp.where((row < 3 * parts) & (row % parts == (node >> 7)), spread, 0.0)
    at_node = one_hot(iota((LANES, LANES), 0) == (node & (LANES - 1)))
    fluid = sum3(dot_nt(stacked3(spread), at_node))
    moved = []
    for a in range(3):
        for k in range(parts):
            r = a * parts + k
            new = mine[4 + r : 5 + r] + fluid[r : r + 1]
            at = slice(k * LANES, (k + 1) * LANES)
            vel_out_ref[a, :, at] = new
            pos_out_ref[a, :, at] = pos_ref[a, :, at] + new
        base = jnp.sum(found[4 + a * parts : 4 + (a + 1) * parts], axis=0, keepdims=True)
        moved.append(jnp.where(my_live, base + fluid_at_links[1 + a : 2 + a], 0.0))
    moved = jnp.concatenate(moved + [jnp.zeros((5, LANES), jnp.float32)], axis=0)
    for o in range(owners):
        turned = pltpu.roll(moved, LANES - o * capacity, 1) if o else moved
        for a in range(3):
            wall_out_ref[0, 0, 0, a, o : o + 1] = turned[a : a + 1, :capacity]


def ring(count, step):
    return [(i, (i + step) % count) for i in range(count)]


def body(
    populations,
    solid,
    link_cell,
    link_dir,
    link_node,
    link_velocity,
    fabric_position,
    fabric_velocity,
    fabric_rest,
    triangles,
):
    size_x, size_y, size_z = populations.shape[1:]
    owners, capacity = link_node.shape[3:]
    nodes = fabric_position.shape[2]
    count_x, count_y, count_z = (lax.axis_size(name) for name in ("gx", "gy", "gz"))
    folded = (
        (count_y, count_z) == (4, 2)
        and (size_y, size_z) == (8, LANES)
        and owners * capacity == LANES
        and nodes == 4 * LANES
    )
    if not folded:
        return general_body(
            populations, solid, link_cell, link_dir, link_node, link_velocity,
            fabric_position, fabric_velocity, fabric_rest, triangles,
        )
    f32 = jnp.float32

    def shape(*dims):
        return jax.ShapeDtypeStruct(dims, f32)

    face_x = shape(5, size_y, size_z)
    post, up, down = pl.pallas_call(
        collide_kernel, out_shape=(shape(*populations.shape), face_x, face_x), name="collide"
    )(populations, solid)
    xlow = lax.ppermute(up, "gx", ring(count_x, 1))
    xhigh = lax.ppermute(down, "gx", ring(count_x, -1))
    map_shape = shape(size_x, size_y, size_z)
    fab, kind, back = pl.pallas_call(
        fabric_kernel, out_shape=(shape(FAB, LANES), map_shape, map_shape), name="fabric"
    )(post, link_cell, link_dir, link_node, link_velocity, fabric_position, fabric_velocity, fabric_rest, triangles)
    side = shape(FAB + -(-5 * size_x // 8) * 8, LANES)
    up, down = pl.pallas_call(side_kernel, out_shape=(side, side), name="sides")(post, xlow, xhigh, fab)
    below = lax.ppermute(up, "gy", ring(count_y, 1))
    above = lax.ppermute(down, "gy", ring(count_y, -1))
    across = lax.ppermute(fab, "gy", ring(count_y, 2))
    slab = shape(count_y, FAB, LANES)
    rolled, face, own = pl.pallas_call(
        shift_kernel, out_shape=(shape(*populations.shape), map_shape, slab), name="shift"
    )(post, xlow, xhigh, fab, below, above, across)
    swap = [(0, 1), (1, 0)]
    face = lax.ppermute(face, "gz", swap)
    other = lax.ppermute(own, "gz", swap)
    return pl.pallas_call(
        final_kernel,
        out_shape=(
            shape(*populations.shape),
            shape(*fabric_position.shape),
            shape(*fabric_velocity.shape),
            shape(*link_velocity.shape),
        ),
        name="final",
    )(rolled, face, kind, back, own, other, fabric_position)


def solution(mesh):
    placed = (
        P(None, "gx", "gy", "gz"),
        P("gx", "gy", "gz"),
        P("gx", "gy", "gz", None, None),
        P("gx", "gy", "gz", None, None),
        P("gx", "gy", "gz", None, None),
        P("gx", "gy", "gz", None, None, None),
        P(None, "gx", ("gy", "gz")),
        P(None, "gx", ("gy", "gz")),
        P(None, "gx", ("gy", "gz")),
        P(None, "gx", ("gy", "gz")),
    )
    return jax.shard_map(
        body,
        mesh=mesh,
        in_specs=placed,
        out_specs=(
            P(None, "gx", "gy", "gz"),
            P(None, "gx", ("gy", "gz")),
            P(None, "gx", ("gy", "gz")),
            P("gx", "gy", "gz", None, None, None),
        ),
        check_vma=False,
    )
```

```python
import jax
import jax.numpy as jnp
import numpy as np
from jax import lax
from jax.experimental import pallas as pl
from jax.experimental.pallas import tpu as pltpu
from jax.sharding import PartitionSpec as P

SPRING = 0.5
DAMPING = 0.1
DIRECTIONS = [
    [0, 0, 0],
    [1, 0, 0],
    [-1, 0, 0],
    [0, 1, 0],
    [0, -1, 0],
    [0, 0, 1],
    [0, 0, -1],
    [1, 1, 0],
    [-1, -1, 0],
    [1, -1, 0],
    [-1, 1, 0],
    [1, 0, 1],
    [-1, 0, -1],
    [1, 0, -1],
    [-1, 0, 1],
    [0, 1, 1],
    [0, -1, -1],
    [0, 1, -1],
    [0, -1, 1],
]


def extended(cells, sides, width):
    for axis, dim in sides:
        count = lax.axis_size(axis)
        head = lax.slice_in_dim(cells, 0, width, axis=dim)
        tail = lax.slice_in_dim(cells, cells.shape[dim] - width, cells.shape[dim], axis=dim)
        cells = jnp.concatenate(
            [
                lax.ppermute(tail, axis, [(i, (i + 1) % count) for i in range(count)]),
                cells,
                lax.ppermute(head, axis, [((i + 1) % count, i) for i in range(count)]),
            ],
            axis=dim,
        )
    return cells


def lattice():
    velocity_np = np.array(DIRECTIONS)
    weight_np = np.array([1.0 / 3.0] + [1.0 / 18.0] * 6 + [1.0 / 36.0] * 12)
    opposite_list = [
        DIRECTIONS.index([-entry for entry in DIRECTIONS[direction]]) for direction in range(19)
    ]
    along_a = np.array([float(entry[0]) for entry in DIRECTIONS])
    along_b = np.array([float(entry[1]) for entry in DIRECTIONS])
    along_e = np.array([float(entry[2]) for entry in DIRECTIONS])
    speed_sq = along_a * along_a + along_b * along_b + along_e * along_e
    moment_rows = [
        np.ones(19),
        19 * speed_sq - 30,
        (21 * speed_sq * speed_sq - 53 * speed_sq + 24) / 2,
        along_a,
        (5 * speed_sq - 9) * along_a,
        along_b,
        (5 * speed_sq - 9) * along_b,
        along_e,
        (5 * speed_sq - 9) * along_e,
        3 * along_a * along_a - speed_sq,
        (3 * speed_sq - 5) * (3 * along_a * along_a - speed_sq),
        along_b * along_b - along_e * along_e,
        (3 * speed_sq - 5) * (along_b * along_b - along_e * along_e),
        along_a * along_b,
        along_b * along_e,
        along_a * along_e,
        (along_b * along_b - along_e * along_e) * along_a,
        (along_e * along_e - along_a * along_a) * along_b,
        (along_a * along_a - along_b * along_b) * along_e,
    ]
    moment_np = np.stack(moment_rows)
    inverse_np = moment_np.T / np.sum(moment_np * moment_np, axis=1)[None, :]
    viscous = 5.0 / 3.0
    rates_np = np.array(
        [
            0.0,
            1.19,
            1.4,
            0.0,
            1.2,
            0.0,
            1.2,
            0.0,
            1.2,
            viscous,
            1.4,
            viscous,
            1.4,
            viscous,
            viscous,
            viscous,
            1.98,
            1.98,
            1.98,
        ]
    )
    return (velocity_np, weight_np, opposite_list, moment_np, inverse_np, rates_np)


def collide_cells(popul, solid_flat):
    velocity_np, weight_np, opposite_list, moment_np, inverse_np, rates_np = lattice()
    velocity_table = jnp.asarray(velocity_np, jnp.float32)
    weight_table = jnp.asarray(weight_np, jnp.float32)
    density = jnp.sum(popul, axis=0)
    momentum = jnp.dot(
        velocity_table.T, popul, precision=lax.Precision.HIGHEST, preferred_element_type=jnp.float32
    )
    flow = momentum / density
    projected = jnp.dot(
        velocity_table, flow, precision=lax.Precision.HIGHEST, preferred_element_type=jnp.float32
    )
    speed_sq = jnp.sum(flow * flow, axis=0)
    equilibrium = (
        weight_table[:, None]
        * density
        * (1.0 + 3.0 * projected + 4.5 * projected * projected - 1.5 * speed_sq)
    )
    offset = popul - equilibrium
    moments = jnp.dot(
        jnp.asarray(moment_np, jnp.float32),
        offset,
        precision=lax.Precision.HIGHEST,
        preferred_element_type=jnp.float32,
    )
    relaxed = jnp.asarray(rates_np, jnp.float32)[:, None] * moments
    change = jnp.dot(
        jnp.asarray(inverse_np, jnp.float32),
        relaxed,
        precision=lax.Precision.HIGHEST,
        preferred_element_type=jnp.float32,
    )
    return jnp.where(solid_flat[None, :] == 1, popul, popul - change)


def fill_outside(padded, weight_np):
    span_y = padded.shape[2]
    span_z = padded.shape[3]
    place_y = lax.axis_index("gy")
    place_z = lax.axis_index("gz")
    count_y = lax.axis_size("gy")
    count_z = lax.axis_size("gz")
    rows_y = jnp.arange(span_y)
    rows_z = jnp.arange(span_z)
    out_y = (rows_y == 0) & (place_y == 0) | (rows_y == span_y - 1) & (place_y == count_y - 1)
    out_z = (rows_z == 0) & (place_z == 0) | (rows_z == span_z - 1) & (place_z == count_z - 1)
    outside = out_y[:, None] | out_z[None, :]
    return jnp.where(
        outside[None, None], jnp.asarray(weight_np, jnp.float32)[:, None, None, None], padded
    )


def propagate(padded, size_x, size_y, size_z):
    pieces = []
    for direction in range(19):
        shift_x = DIRECTIONS[direction][0]
        shift_y = DIRECTIONS[direction][1]
        shift_z = DIRECTIONS[direction][2]
        plane = padded[direction]
        pieces.append(
            lax.slice(
                plane,
                (1 - shift_x, 1 - shift_y, 1 - shift_z),
                (1 - shift_x + size_x, 1 - shift_y + size_y, 1 - shift_z + size_z),
            )
        )
    return jnp.stack(pieces)


def membrane(positions, rest, triangle_nodes):
    force = jnp.zeros(positions.shape, jnp.float32)
    for first, second in ((0, 1), (1, 2), (2, 0)):
        head = triangle_nodes[first]
        tail = triangle_nodes[second]
        stretch = positions[:, tail] - positions[:, head] - (rest[:, tail] - rest[:, head])
        force = force.at[:, head].add(SPRING * stretch)
        force = force.at[:, tail].add(-SPRING * stretch)
    return force


def general_body(
    populations,
    solid,
    link_cell,
    link_dir,
    link_node,
    link_velocity,
    fabric_position,
    fabric_velocity,
    fabric_rest,
    triangles,
):
    velocity_np, weight_np, opposite_list, moment_np, inverse_np, rates_np = lattice()
    velocity_table = jnp.asarray(velocity_np, jnp.float32)
    weight_table = jnp.asarray(weight_np, jnp.float32)
    opposite_table = jnp.asarray(opposite_list, jnp.int32)
    size_x = populations.shape[1]
    size_y = populations.shape[2]
    size_z = populations.shape[3]
    cells = size_x * size_y * size_z
    post = collide_cells(populations.reshape(19, cells), solid.reshape(cells)).reshape(
        populations.shape
    )
    padded = extended(post, (("gx", 1), ("gy", 2), ("gz", 3)), 1)
    padded = fill_outside(padded, weight_np)
    propagated = propagate(padded, size_x, size_y, size_z).reshape(19, cells)
    owners_n = link_node.shape[3]
    capacity = link_node.shape[4]
    node_rows = link_node.reshape(owners_n, capacity)
    cell_rows = link_cell.reshape(owners_n, capacity)
    dir_rows = link_dir.reshape(owners_n, capacity)
    live = node_rows >= 0
    post_flat = post.reshape(19, cells)
    reflected = post_flat[opposite_table[dir_rows], cell_rows]
    link_unit = velocity_table[dir_rows]
    wall = jnp.moveaxis(link_velocity.reshape(3, owners_n, capacity), 0, -1)
    returned = reflected + 6.0 * weight_table[dir_rows] * jnp.sum(link_unit * wall, axis=-1)
    populations_next = propagated.at[jnp.where(live, dir_rows, 19), cell_rows].set(
        returned, mode="drop"
    )
    strength = reflected + returned
    positions = fabric_position.reshape(3, -1)
    velocities = fabric_velocity.reshape(3, -1)
    rest = fabric_rest.reshape(3, -1)
    nodes_n = positions.shape[1]
    elastic = membrane(positions, rest, triangles.reshape(3, -1))
    link_force = jnp.moveaxis(-link_unit * strength[..., None], -1, 0)
    got_nodes, got_force = (
        lax.all_to_all(node_rows[None], ("gy", "gz"), split_axis=1, concat_axis=1, tiled=True),
        lax.all_to_all(link_force, ("gy", "gz"), split_axis=1, concat_axis=1, tiled=True),
    )
    got_ids = got_nodes[0]
    got_live = got_ids >= 0
    target = jnp.where(got_live, got_ids, nodes_n).reshape(-1)
    fluid_force = (
        jnp.zeros((3, nodes_n), jnp.float32)
        .at[:, target]
        .add(got_force.reshape(3, -1), mode="drop")
    )
    velocity_next = (1.0 - DAMPING) * velocities + (fluid_force + elastic)
    position_next = positions + velocity_next
    reply = jnp.where(got_live[None], velocity_next[:, jnp.where(got_live, got_ids, 0)], 0.0)
    wall_next = lax.all_to_all(reply, ("gy", "gz"), split_axis=1, concat_axis=1, tiled=True)
    return (
        populations_next.reshape(populations.shape),
        position_next.reshape(fabric_position.shape),
        velocity_next.reshape(fabric_velocity.shape),
        wall_next.reshape(link_velocity.shape),
    )


WEIGHTS = [1.0 / 3.0] + [1.0 / 18.0] * 6 + [1.0 / 36.0] * 12
OPPOSITE = [DIRECTIONS.index([-entry for entry in d]) for d in DIRECTIONS]
SIDES = [
    ([i for i in range(19) if DIRECTIONS[i][a] == 1], [i for i in range(19) if DIRECTIONS[i][a] == -1])
    for a in range(3)
]
LANES = 128
FAB = 16


def iota(shape, axis):
    return lax.broadcasted_iota(jnp.int32, shape, axis)


def split3(value):
    high = value.astype(jnp.bfloat16).astype(jnp.float32)
    rest = value - high
    middle = rest.astype(jnp.bfloat16).astype(jnp.float32)
    return high, middle, rest - middle


def stacked3(value):
    return jnp.concatenate(split3(value), axis=0).astype(jnp.bfloat16)


def sum3(value):
    rows = value.shape[0] // 3
    return value[:rows] + value[rows : 2 * rows] + value[2 * rows :]


def dot_nn(left, right):
    return lax.dot_general(left, right, (((1,), (0,)), ((), ())), preferred_element_type=jnp.float32)


def dot_nt(left, right):
    return lax.dot_general(left, right, (((1,), (1,)), ((), ())), preferred_element_type=jnp.float32)


def one_hot(mask):
    return jnp.where(mask, 1.0, 0.0).astype(jnp.bfloat16)


def collided(f, solid):
    sx, dx = f[1] + f[2], f[1] - f[2]
    sy, dy = f[3] + f[4], f[3] - f[4]
    sz, dz = f[5] + f[6], f[5] - f[6]
    sa, da = f[7] + f[8], f[7] - f[8]
    sb, db = f[9] + f[10], f[9] - f[10]
    sc, dc = f[11] + f[12], f[11] - f[12]
    sd, dd = f[13] + f[14], f[13] - f[14]
    se, de = f[15] + f[16], f[15] - f[16]
    sg, dg = f[17] + f[18], f[17] - f[18]
    sxy, txy = sa + sb, sa - sb
    sxz, txz = sc + sd, sc - sd
    syz, tyz = se + sg, se - sg
    ax_ab, ay_ab = da + db, da - db
    ax_cd, az_cd = dc + dd, dc - dd
    ay_eg, az_eg = de + dg, de - dg
    near, far = sx + sy + sz, sxy + sxz + syz
    rho = f[0] + near + far
    ex, ey, ez = ax_ab + ax_cd, ay_ab + ay_eg, az_cd + az_eg
    jx, jy, jz = dx + ex, dy + ey, dz + ez
    inv = 1.0 / rho
    ux, uy, uz = jx * inv, jy * inv, jz * inv
    xx, yy, zz = jx * ux, jy * uy, jz * uz
    jj = xx + yy + zz
    energy = (-30.0 * f[0] - 11.0 * near + 8.0 * far) - (-11.0 * rho + 19.0 * jj)
    square = (12.0 * f[0] - 4.0 * near + far) - (3.0 * rho - 5.5 * jj)
    kx = (1.2 / 40.0) * (ex - 4.0 * dx + (2.0 / 3.0) * jx)
    ky = (1.2 / 40.0) * (ey - 4.0 * dy + (2.0 / 3.0) * jy)
    kz = (1.2 / 40.0) * (ez - 4.0 * dz + (2.0 / 3.0) * jz)
    yz_near, xyz_far = sy + sz, sxy + sxz - 2.0 * syz
    pxx_eq = 2.0 * xx - yy - zz
    pww_eq = yy - zz
    pxx = (5.0 / 3.0 / 36.0) * (2.0 * sx - yz_near + xyz_far - pxx_eq)
    pixx = (1.4 / 72.0) * (-4.0 * sx + 2.0 * yz_near + xyz_far + 0.5 * pxx_eq)
    w_near, w_far = sy - sz, sxy - sxz
    pww = (5.0 / 3.0 / 12.0) * (w_near + w_far - pww_eq)
    piww = (1.4 / 24.0) * (w_far - 2.0 * w_near + 0.5 * pww_eq)
    pxy = (5.0 / 3.0 / 4.0) * (txy - jx * uy)
    pyz = (5.0 / 3.0 / 4.0) * (tyz - jy * uz)
    pxz = (5.0 / 3.0 / 4.0) * (txz - jx * uz)
    mx = (1.98 / 8.0) * (ax_ab - ax_cd)
    my = (1.98 / 8.0) * (ay_eg - ay_ab)
    mz = (1.98 / 8.0) * (az_cd - az_eg)
    energy = (1.19 / 2394.0) * energy
    square = (1.4 / 252.0) * square
    axis = -11.0 * energy - 4.0 * square
    across = pxx - 2.0 * pixx
    split = pww - 2.0 * piww
    edge = 8.0 * energy + square
    pp, ww = pxx + pixx, pww + piww
    even = [
        axis + 2.0 * across,
        axis - across + split,
        axis - across - split,
        edge + pp + ww + pxy,
        edge + pp + ww - pxy,
        edge + pp - ww + pxz,
        edge + pp - ww - pxz,
        edge - 2.0 * pp + pyz,
        edge - 2.0 * pp - pyz,
    ]
    odd = [
        -4.0 * kx,
        -4.0 * ky,
        -4.0 * kz,
        (kx + mx) + (ky - my),
        (kx + mx) - (ky - my),
        (kx - mx) + (kz + mz),
        (kx - mx) - (kz + mz),
        (ky + my) + (kz - mz),
        (ky + my) - (kz - mz),
    ]
    change = [12.0 * square - 30.0 * energy]
    for pair in range(9):
        change += [even[pair] + odd[pair], even[pair] - odd[pair]]
    fluid = solid != 1
    return [jnp.where(fluid, f[i] - change[i], f[i]) for i in range(19)]


def collide_kernel(pop_ref, solid_ref, post_ref, up_ref, down_ref):
    size_x = pop_ref.shape[1]
    for x in range(size_x):
        post = collided([pop_ref[i, x] for i in range(19)], solid_ref[x])
        for i in range(19):
            post_ref[i, x] = post[i]
            if x == size_x - 1 and i in SIDES[0][0]:
                up_ref[SIDES[0][0].index(i)] = post[i]
            if x == 0 and i in SIDES[0][1]:
                down_ref[SIDES[0][1].index(i)] = post[i]


def slots_to_row(value):
    owners, capacity = value.shape
    wide = jnp.concatenate([value, jnp.zeros((owners, LANES - capacity), value.dtype)], axis=1)
    return jnp.sum(pltpu.roll(wide, 0, 1, stride=capacity, stride_axis=0), axis=0, keepdims=True)


def fabric_kernel(
    post_ref, cell_ref, dir_ref, node_ref, wall_ref, pos_ref, vel_ref, rest_ref, tri_ref,
    fab_ref, kind_ref, back_ref,
):
    size_x = post_ref.shape[1]
    size_y = post_ref.shape[2]
    rows = size_x * size_y
    cell = slots_to_row(cell_ref[0, 0, 0].astype(jnp.float32)).astype(jnp.int32)
    way = slots_to_row(dir_ref[0, 0, 0].astype(jnp.float32))
    node = slots_to_row(node_ref[0, 0, 0].astype(jnp.float32))
    live = node >= 0.0
    unit = []
    for a in range(3):
        u = jnp.zeros_like(way)
        for i in range(1, 19):
            if DIRECTIONS[i][a]:
                u = jnp.where(way == float(i), float(DIRECTIONS[i][a]), u)
        unit.append(u)
    weight = jnp.where(way >= 7.0, 6.0 / 36.0, 6.0 / 18.0)
    wall = [slots_to_row(wall_ref[0, 0, 0, a]) for a in range(3)]
    term = weight * (unit[0] * wall[0] + unit[1] * wall[1] + unit[2] * wall[2])
    at_row = jnp.where((iota((rows, LANES), 0) == (cell >> 7)) & live, 1.0, 0.0)
    at_lane = one_hot(iota((LANES, LANES), 0) == (cell & (LANES - 1)))
    left = jnp.concatenate([at_row * way] + [at_row * t for t in split3(term)], axis=0)
    maps = dot_nt(left.astype(jnp.bfloat16), at_lane)
    kind = maps[:rows]
    added = sum3(maps[rows:])
    taken = []
    for x in range(size_x):
        k = kind[x * size_y : (x + 1) * size_y]
        t = jnp.zeros_like(k)
        for i in range(1, 19):
            t = jnp.where(k == float(i), post_ref[OPPOSITE[i], x], t)
        taken.append(t)
        kind_ref[x] = k
        back_ref[x] = t + added[x * size_y : (x + 1) * size_y]
    strength = 2.0 * jnp.concatenate(taken, axis=0) + added
    at_link = sum3(dot_nn(stacked3(strength), at_lane))
    push = jnp.sum(at_row * at_link, axis=0, keepdims=True)
    fab_ref[0:1] = node
    for a in range(3):
        fab_ref[1 + a : 2 + a] = -unit[a] * push

    nodes = pos_ref.shape[2]
    count = tri_ref.shape[2]
    wide = -(-count // LANES) * LANES
    stretch = [pos_ref[a] - rest_ref[a] for a in range(3)]
    corners = [
        jnp.concatenate([tri_ref[t], jnp.full((1, wide - count), -1, jnp.int32)], axis=1) for t in range(3)
    ]
    node_ids = iota((nodes, wide), 0)
    hits = sum(jnp.where(node_ids == corner, 1.0, 0.0) for corner in corners).astype(jnp.bfloat16)
    stretch8 = jnp.concatenate(stretch + [jnp.zeros((5, nodes), jnp.float32)], axis=0)
    total = sum3(dot_nn(stacked3(stretch8), hits))
    total = jnp.where(iota(total.shape, 0) == 3, 1.0, total)
    back = sum3(dot_nt(stacked3(total), hits))
    for a in range(3):
        elastic = SPRING * back[a : a + 1] - 3.0 * SPRING * back[3:4] * stretch[a]
        base = (1.0 - DAMPING) * vel_ref[a] + elastic
        for k in range(nodes // LANES):
            row = 4 + a * (nodes // LANES) + k
            fab_ref[row : row + 1] = base[:, k * LANES : (k + 1) * LANES]


def source_tile(post_ref, low_ref, high_ref, i, x):
    size_x = post_ref.shape[1]
    from_x = x - DIRECTIONS[i][0]
    if from_x < 0:
        return low_ref.at[SIDES[0][0].index(i)]
    if from_x >= size_x:
        return high_ref.at[SIDES[0][1].index(i)]
    return post_ref.at[i, from_x]


def side_kernel(post_ref, low_ref, high_ref, fab_ref, up_ref, down_ref):
    size_x = post_ref.shape[1]
    size_y = post_ref.shape[2]
    for out_ref, side, row in ((up_ref, 0, size_y - 1), (down_ref, 1, 0)):
        out_ref[:FAB] = fab_ref[...]
        for k, i in enumerate(SIDES[1][side]):
            for x in range(size_x):
                at = FAB + k * size_x + x
                out_ref[at : at + 1] = source_tile(post_ref, low_ref, high_ref, i, x)[row : row + 1]
        end = FAB + 5 * size_x
        if out_ref.shape[0] > end:
            out_ref[end:] = jnp.zeros((out_ref.shape[0] - end, LANES), jnp.float32)


def shift_kernel(
    post_ref, xlow_ref, xhigh_ref, fab_ref, below_ref, above_ref, across_ref,
    rolled_ref, face_ref, slab_ref,
):
    size_x = post_ref.shape[1]
    size_y = post_ref.shape[2]
    place_y = lax.axis_index("gy")
    place_z = lax.axis_index("gz")
    count_y = lax.axis_size("gy")
    sub = iota((size_y, LANES), 0)
    lane = iota((size_y, LANES), 1)
    first, last = place_y == 0, place_y == count_y - 1
    for x in range(size_x):
        up = jnp.zeros((size_y, LANES), jnp.float32)
        down = jnp.zeros((size_y, LANES), jnp.float32)
        for i in range(19):
            tile = source_tile(post_ref, xlow_ref, xhigh_ref, i, x)[...]
            if DIRECTIONS[i][1] == 1:
                at = FAB + SIDES[1][0].index(i) * size_x + x
                row = jnp.where(first, WEIGHTS[i], below_ref[at : at + 1])
                tile = jnp.where(sub == 0, row, pltpu.roll(tile, 1, 0))
            if DIRECTIONS[i][1] == -1:
                at = FAB + SIDES[1][1].index(i) * size_x + x
                row = jnp.where(last, WEIGHTS[i], above_ref[at : at + 1])
                tile = jnp.where(sub == size_y - 1, row, pltpu.roll(tile, size_y - 1, 0))
            if DIRECTIONS[i][2] == 1:
                k = SIDES[2][0].index(i)
                tile = pltpu.roll(tile, 1, 1)
                up = jnp.where(lane == k, pltpu.roll(tile, k, 1) if k else tile, up)
            if DIRECTIONS[i][2] == -1:
                k = SIDES[2][1].index(i)
                tile = pltpu.roll(tile, LANES - 1, 1)
                down = jnp.where(lane == k, pltpu.roll(tile, k + 1, 1), down)
            rolled_ref[i, x] = tile
        face_ref[x] = jnp.where(place_z == 0, up, down)
    slab_ref[place_y] = fab_ref[...]
    slab_ref[lax.rem(place_y + count_y - 1, count_y)] = below_ref[:FAB]
    slab_ref[lax.rem(place_y + 1, count_y)] = above_ref[:FAB]
    slab_ref[lax.rem(place_y + 2, count_y)] = across_ref[...]


def final_kernel(
    rolled_ref, face_ref, kind_ref, back_ref, own_ref, other_ref, pos_ref,
    pop_ref, pos_out_ref, vel_out_ref, wall_out_ref,
):
    size_x = rolled_ref.shape[1]
    size_y = rolled_ref.shape[2]
    place_y = lax.axis_index("gy")
    place_z = lax.axis_index("gz")
    count_y = lax.axis_size("gy")
    lane = iota((size_y, LANES), 1)
    low_end = place_z == 0
    for x in range(size_x):
        kind = kind_ref[x]
        back = back_ref[x]
        face = face_ref[x]
        for i in range(19):
            tile = rolled_ref[i, x]
            if DIRECTIONS[i][2] == 1:
                k = SIDES[2][0].index(i)
                halo = pltpu.roll(face, LANES - k, 1) if k else face
                tile = jnp.where(lane == 0, jnp.where(low_end, WEIGHTS[i], halo), tile)
            if DIRECTIONS[i][2] == -1:
                k = SIDES[2][1].index(i)
                halo = pltpu.roll(face, LANES - 1 - k, 1)
                tile = jnp.where(lane == LANES - 1, jnp.where(low_end, halo, WEIGHTS[i]), tile)
            if i:
                tile = jnp.where(kind == float(i), back, tile)
            pop_ref[i, x] = tile

    owners, capacity = wall_out_ref.shape[4], wall_out_ref.shape[5]
    nodes = pos_ref.shape[2]
    parts = nodes // LANES
    slot_owner = iota((1, LANES), 1) // capacity
    owner_base = (slot_owner * nodes).astype(jnp.float32)
    mine = own_ref[place_y]
    my_node = mine[0:1]
    my_live = my_node >= 0.0
    my_id = jnp.where(my_live, owner_base + my_node, -2.0)
    my_column = jnp.transpose(jnp.broadcast_to(my_id, (LANES, LANES)))
    me = place_y * 2 + place_z
    matches, forces, picked = [], [], jnp.zeros((8, LANES), jnp.float32)
    for group, ref in ((0, own_ref), (1, other_ref)):
        for y in range(count_y):
            m = group * count_y + y
            tile = ref[y, 0:8]
            ids = tile[0:1]
            ids = jnp.where(ids >= 0.0, owner_base + ids, -1.0)
            matches.append(one_hot(my_column == ids))
            forces.append(tile)
            shift = lax.rem((m + owners - me) * capacity, LANES)
            picked = jnp.where(slot_owner == m, pltpu.roll(tile, shift, 1), picked)
    force = stacked3(jnp.concatenate(forces, axis=1))
    fluid_at_links = sum3(dot_nt(force, jnp.concatenate(matches, axis=1)))

    every = jnp.concatenate(
        [own_ref[...].reshape(count_y * FAB, LANES), other_ref[...].reshape(count_y * FAB, LANES)], axis=0
    )
    my_int = my_node.astype(jnp.int32)
    at_lane = one_hot(iota((LANES, LANES), 0) == (my_int & (LANES - 1)))
    found = sum3(dot_nn(stacked3(every), at_lane))
    row = iota(found.shape, 0)
    message, inner = row // FAB, row % FAB
    owner = (message % count_y) * 2 + jnp.where(message < count_y, place_z, 1 - place_z)
    fits = (owner == slot_owner) & (inner >= 4) & (inner % parts == (my_int >> 7))
    found = jnp.where(fits, found, 0.0)
    found = sum(found[m * FAB : (m + 1) * FAB] for m in range(2 * count_y))

    node = picked[0:1].astype(jnp.int32)
    row = iota((FAB, LANES), 0)
    spread = jnp.where(row < parts, picked[1:2], jnp.where(row < 2 * parts, picked[2:3], picked[3:4]))
    spread = jnp.where((row < 3 * parts) & (row % parts == (node >> 7)), spread, 0.0)
    at_node = one_hot(iota((LANES, LANES), 0) == (node & (LANES - 1)))
    fluid = sum3(dot_nt(stacked3(spread), at_node))
    moved = []
    for a in range(3):
        for k in range(parts):
            r = a * parts + k
            new = mine[4 + r : 5 + r] + fluid[r : r + 1]
            at = slice(k * LANES, (k + 1) * LANES)
            vel_out_ref[a, :, at] = new
            pos_out_ref[a, :, at] = pos_ref[a, :, at] + new
        base = jnp.sum(found[4 + a * parts : 4 + (a + 1) * parts], axis=0, keepdims=True)
        moved.append(jnp.where(my_live, base + fluid_at_links[1 + a : 2 + a], 0.0))
    moved = jnp.concatenate(moved + [jnp.zeros((5, LANES), jnp.float32)], axis=0)
    for o in range(owners):
        turned = pltpu.roll(moved, LANES - o * capacity, 1) if o else moved
        for a in range(3):
            wall_out_ref[0, 0, 0, a, o : o + 1] = turned[a : a + 1, :capacity]


def ring(count, step):
    return [(i, (i + step) % count) for i in range(count)]


def body(
    populations,
    solid,
    link_cell,
    link_dir,
    link_node,
    link_velocity,
    fabric_position,
    fabric_velocity,
    fabric_rest,
    triangles,
):
    size_x, size_y, size_z = populations.shape[1:]
    owners, capacity = link_node.shape[3:]
    nodes = fabric_position.shape[2]
    count_x, count_y, count_z = (lax.axis_size(name) for name in ("gx", "gy", "gz"))
    folded = (
        (count_y, count_z) == (4, 2)
        and (size_y, size_z) == (8, LANES)
        and owners * capacity == LANES
        and nodes == 4 * LANES
    )
    if not folded:
        return general_body(
            populations, solid, link_cell, link_dir, link_node, link_velocity,
            fabric_position, fabric_velocity, fabric_rest, triangles,
        )
    f32 = jnp.float32
    on_chip = pl.BlockSpec(memory_space=pltpu.VMEM)

    def shape(*dims):
        return jax.ShapeDtypeStruct(dims, f32)

    def kept(*dims):
        return pltpu.VMEM(dims, f32)

    def run(kernel, outs, *args):
        args = [pltpu.with_memory_space_constraint(arg, pltpu.VMEM) for arg in args]
        return pl.pallas_call(
            kernel,
            out_shape=outs,
            in_specs=[on_chip] * len(args),
            out_specs=jax.tree.map(lambda _: on_chip, outs),
            name=kernel.__name__,
        )(*args)

    face_x = kept(5, size_y, size_z)
    post, up, down = run(collide_kernel, (kept(*populations.shape), face_x, face_x), populations, solid)
    xlow = lax.ppermute(up, "gx", ring(count_x, 1))
    xhigh = lax.ppermute(down, "gx", ring(count_x, -1))
    map_shape = kept(size_x, size_y, size_z)
    fab, kind, back = run(
        fabric_kernel, (kept(FAB, LANES), map_shape, map_shape),
        post, link_cell, link_dir, link_node, link_velocity, fabric_position, fabric_velocity, fabric_rest, triangles,
    )
    side = kept(FAB + -(-5 * size_x // 8) * 8, LANES)
    up, down = run(side_kernel, (side, side), post, xlow, xhigh, fab)
    below = lax.ppermute(up, "gy", ring(count_y, 1))
    above = lax.ppermute(down, "gy", ring(count_y, -1))
    across = lax.ppermute(fab, "gy", ring(count_y, 2))
    slab = kept(count_y, FAB, LANES)
    rolled, face, own = run(
        shift_kernel, (kept(*populations.shape), map_shape, slab), post, xlow, xhigh, fab, below, above, across
    )
    swap = [(0, 1), (1, 0)]
    face = lax.ppermute(face, "gz", swap)
    other = lax.ppermute(own, "gz", swap)
    return run(
        final_kernel,
        (
            shape(*populations.shape),
            shape(*fabric_position.shape),
            shape(*fabric_velocity.shape),
            shape(*link_velocity.shape),
        ),
        rolled, face, kind, back, own, other, fabric_position,
    )


def solution(mesh):
    placed = (
        P(None, "gx", "gy", "gz"),
        P("gx", "gy", "gz"),
        P("gx", "gy", "gz", None, None),
        P("gx", "gy", "gz", None, None),
        P("gx", "gy", "gz", None, None),
        P("gx", "gy", "gz", None, None, None),
        P(None, "gx", ("gy", "gz")),
        P(None, "gx", ("gy", "gz")),
        P(None, "gx", ("gy", "gz")),
        P(None, "gx", ("gy", "gz")),
    )
    return jax.shard_map(
        body,
        mesh=mesh,
        in_specs=placed,
        out_specs=(
            P(None, "gx", "gy", "gz"),
            P(None, "gx", ("gy", "gz")),
            P(None, "gx", ("gy", "gz")),
            P("gx", "gy", "gz", None, None, None),
        ),
        check_vma=False,
    )
```

```python
import jax
import jax.numpy as jnp
import numpy as np
from jax import lax
from jax.experimental import pallas as pl
from jax.experimental.pallas import tpu as pltpu
from jax.sharding import PartitionSpec as P

SPRING = 0.5
DAMPING = 0.1
DIRECTIONS = [
    [0, 0, 0],
    [1, 0, 0],
    [-1, 0, 0],
    [0, 1, 0],
    [0, -1, 0],
    [0, 0, 1],
    [0, 0, -1],
    [1, 1, 0],
    [-1, -1, 0],
    [1, -1, 0],
    [-1, 1, 0],
    [1, 0, 1],
    [-1, 0, -1],
    [1, 0, -1],
    [-1, 0, 1],
    [0, 1, 1],
    [0, -1, -1],
    [0, 1, -1],
    [0, -1, 1],
]


def extended(cells, sides, width):
    for axis, dim in sides:
        count = lax.axis_size(axis)
        head = lax.slice_in_dim(cells, 0, width, axis=dim)
        tail = lax.slice_in_dim(cells, cells.shape[dim] - width, cells.shape[dim], axis=dim)
        cells = jnp.concatenate(
            [
                lax.ppermute(tail, axis, [(i, (i + 1) % count) for i in range(count)]),
                cells,
                lax.ppermute(head, axis, [((i + 1) % count, i) for i in range(count)]),
            ],
            axis=dim,
        )
    return cells


def lattice():
    velocity_np = np.array(DIRECTIONS)
    weight_np = np.array([1.0 / 3.0] + [1.0 / 18.0] * 6 + [1.0 / 36.0] * 12)
    opposite_list = [
        DIRECTIONS.index([-entry for entry in DIRECTIONS[direction]]) for direction in range(19)
    ]
    along_a = np.array([float(entry[0]) for entry in DIRECTIONS])
    along_b = np.array([float(entry[1]) for entry in DIRECTIONS])
    along_e = np.array([float(entry[2]) for entry in DIRECTIONS])
    speed_sq = along_a * along_a + along_b * along_b + along_e * along_e
    moment_rows = [
        np.ones(19),
        19 * speed_sq - 30,
        (21 * speed_sq * speed_sq - 53 * speed_sq + 24) / 2,
        along_a,
        (5 * speed_sq - 9) * along_a,
        along_b,
        (5 * speed_sq - 9) * along_b,
        along_e,
        (5 * speed_sq - 9) * along_e,
        3 * along_a * along_a - speed_sq,
        (3 * speed_sq - 5) * (3 * along_a * along_a - speed_sq),
        along_b * along_b - along_e * along_e,
        (3 * speed_sq - 5) * (along_b * along_b - along_e * along_e),
        along_a * along_b,
        along_b * along_e,
        along_a * along_e,
        (along_b * along_b - along_e * along_e) * along_a,
        (along_e * along_e - along_a * along_a) * along_b,
        (along_a * along_a - along_b * along_b) * along_e,
    ]
    moment_np = np.stack(moment_rows)
    inverse_np = moment_np.T / np.sum(moment_np * moment_np, axis=1)[None, :]
    viscous = 5.0 / 3.0
    rates_np = np.array(
        [
            0.0,
            1.19,
            1.4,
            0.0,
            1.2,
            0.0,
            1.2,
            0.0,
            1.2,
            viscous,
            1.4,
            viscous,
            1.4,
            viscous,
            viscous,
            viscous,
            1.98,
            1.98,
            1.98,
        ]
    )
    return (velocity_np, weight_np, opposite_list, moment_np, inverse_np, rates_np)


def collide_cells(popul, solid_flat):
    velocity_np, weight_np, opposite_list, moment_np, inverse_np, rates_np = lattice()
    velocity_table = jnp.asarray(velocity_np, jnp.float32)
    weight_table = jnp.asarray(weight_np, jnp.float32)
    density = jnp.sum(popul, axis=0)
    momentum = jnp.dot(
        velocity_table.T, popul, precision=lax.Precision.HIGHEST, preferred_element_type=jnp.float32
    )
    flow = momentum / density
    projected = jnp.dot(
        velocity_table, flow, precision=lax.Precision.HIGHEST, preferred_element_type=jnp.float32
    )
    speed_sq = jnp.sum(flow * flow, axis=0)
    equilibrium = (
        weight_table[:, None]
        * density
        * (1.0 + 3.0 * projected + 4.5 * projected * projected - 1.5 * speed_sq)
    )
    offset = popul - equilibrium
    moments = jnp.dot(
        jnp.asarray(moment_np, jnp.float32),
        offset,
        precision=lax.Precision.HIGHEST,
        preferred_element_type=jnp.float32,
    )
    relaxed = jnp.asarray(rates_np, jnp.float32)[:, None] * moments
    change = jnp.dot(
        jnp.asarray(inverse_np, jnp.float32),
        relaxed,
        precision=lax.Precision.HIGHEST,
        preferred_element_type=jnp.float32,
    )
    return jnp.where(solid_flat[None, :] == 1, popul, popul - change)


def fill_outside(padded, weight_np):
    span_y = padded.shape[2]
    span_z = padded.shape[3]
    place_y = lax.axis_index("gy")
    place_z = lax.axis_index("gz")
    count_y = lax.axis_size("gy")
    count_z = lax.axis_size("gz")
    rows_y = jnp.arange(span_y)
    rows_z = jnp.arange(span_z)
    out_y = (rows_y == 0) & (place_y == 0) | (rows_y == span_y - 1) & (place_y == count_y - 1)
    out_z = (rows_z == 0) & (place_z == 0) | (rows_z == span_z - 1) & (place_z == count_z - 1)
    outside = out_y[:, None] | out_z[None, :]
    return jnp.where(
        outside[None, None], jnp.asarray(weight_np, jnp.float32)[:, None, None, None], padded
    )


def propagate(padded, size_x, size_y, size_z):
    pieces = []
    for direction in range(19):
        shift_x = DIRECTIONS[direction][0]
        shift_y = DIRECTIONS[direction][1]
        shift_z = DIRECTIONS[direction][2]
        plane = padded[direction]
        pieces.append(
            lax.slice(
                plane,
                (1 - shift_x, 1 - shift_y, 1 - shift_z),
                (1 - shift_x + size_x, 1 - shift_y + size_y, 1 - shift_z + size_z),
            )
        )
    return jnp.stack(pieces)


def membrane(positions, rest, triangle_nodes):
    force = jnp.zeros(positions.shape, jnp.float32)
    for first, second in ((0, 1), (1, 2), (2, 0)):
        head = triangle_nodes[first]
        tail = triangle_nodes[second]
        stretch = positions[:, tail] - positions[:, head] - (rest[:, tail] - rest[:, head])
        force = force.at[:, head].add(SPRING * stretch)
        force = force.at[:, tail].add(-SPRING * stretch)
    return force


def general_body(
    populations,
    solid,
    link_cell,
    link_dir,
    link_node,
    link_velocity,
    fabric_position,
    fabric_velocity,
    fabric_rest,
    triangles,
):
    velocity_np, weight_np, opposite_list, moment_np, inverse_np, rates_np = lattice()
    velocity_table = jnp.asarray(velocity_np, jnp.float32)
    weight_table = jnp.asarray(weight_np, jnp.float32)
    opposite_table = jnp.asarray(opposite_list, jnp.int32)
    size_x = populations.shape[1]
    size_y = populations.shape[2]
    size_z = populations.shape[3]
    cells = size_x * size_y * size_z
    post = collide_cells(populations.reshape(19, cells), solid.reshape(cells)).reshape(
        populations.shape
    )
    padded = extended(post, (("gx", 1), ("gy", 2), ("gz", 3)), 1)
    padded = fill_outside(padded, weight_np)
    propagated = propagate(padded, size_x, size_y, size_z).reshape(19, cells)
    owners_n = link_node.shape[3]
    capacity = link_node.shape[4]
    node_rows = link_node.reshape(owners_n, capacity)
    cell_rows = link_cell.reshape(owners_n, capacity)
    dir_rows = link_dir.reshape(owners_n, capacity)
    live = node_rows >= 0
    post_flat = post.reshape(19, cells)
    reflected = post_flat[opposite_table[dir_rows], cell_rows]
    link_unit = velocity_table[dir_rows]
    wall = jnp.moveaxis(link_velocity.reshape(3, owners_n, capacity), 0, -1)
    returned = reflected + 6.0 * weight_table[dir_rows] * jnp.sum(link_unit * wall, axis=-1)
    populations_next = propagated.at[jnp.where(live, dir_rows, 19), cell_rows].set(
        returned, mode="drop"
    )
    strength = reflected + returned
    positions = fabric_position.reshape(3, -1)
    velocities = fabric_velocity.reshape(3, -1)
    rest = fabric_rest.reshape(3, -1)
    nodes_n = positions.shape[1]
    elastic = membrane(positions, rest, triangles.reshape(3, -1))
    link_force = jnp.moveaxis(-link_unit * strength[..., None], -1, 0)
    got_nodes, got_force = (
        lax.all_to_all(node_rows[None], ("gy", "gz"), split_axis=1, concat_axis=1, tiled=True),
        lax.all_to_all(link_force, ("gy", "gz"), split_axis=1, concat_axis=1, tiled=True),
    )
    got_ids = got_nodes[0]
    got_live = got_ids >= 0
    target = jnp.where(got_live, got_ids, nodes_n).reshape(-1)
    fluid_force = (
        jnp.zeros((3, nodes_n), jnp.float32)
        .at[:, target]
        .add(got_force.reshape(3, -1), mode="drop")
    )
    velocity_next = (1.0 - DAMPING) * velocities + (fluid_force + elastic)
    position_next = positions + velocity_next
    reply = jnp.where(got_live[None], velocity_next[:, jnp.where(got_live, got_ids, 0)], 0.0)
    wall_next = lax.all_to_all(reply, ("gy", "gz"), split_axis=1, concat_axis=1, tiled=True)
    return (
        populations_next.reshape(populations.shape),
        position_next.reshape(fabric_position.shape),
        velocity_next.reshape(fabric_velocity.shape),
        wall_next.reshape(link_velocity.shape),
    )


WEIGHTS = [1.0 / 3.0] + [1.0 / 18.0] * 6 + [1.0 / 36.0] * 12
OPPOSITE = [DIRECTIONS.index([-entry for entry in d]) for d in DIRECTIONS]
SIDES = [
    ([i for i in range(19) if DIRECTIONS[i][a] == 1], [i for i in range(19) if DIRECTIONS[i][a] == -1])
    for a in range(3)
]
LANES = 128
PATCH = 256
FAB = 16


def iota(shape, axis):
    return lax.broadcasted_iota(jnp.int32, shape, axis)


def split3(value):
    high = value.astype(jnp.bfloat16).astype(jnp.float32)
    rest = value - high
    middle = rest.astype(jnp.bfloat16).astype(jnp.float32)
    return high, middle, rest - middle


def stacked3(value):
    return jnp.concatenate(split3(value), axis=0).astype(jnp.bfloat16)


def sum3(value):
    rows = value.shape[0] // 3
    return value[:rows] + value[rows : 2 * rows] + value[2 * rows :]


def dot_nn(left, right):
    return lax.dot_general(left, right, (((1,), (0,)), ((), ())), preferred_element_type=jnp.float32)


def dot_nt(left, right):
    return lax.dot_general(left, right, (((1,), (1,)), ((), ())), preferred_element_type=jnp.float32)


def one_hot(mask):
    return jnp.where(mask, 1.0, 0.0).astype(jnp.bfloat16)


def collided(f, solid):
    sx, dx = f[1] + f[2], f[1] - f[2]
    sy, dy = f[3] + f[4], f[3] - f[4]
    sz, dz = f[5] + f[6], f[5] - f[6]
    sa, da = f[7] + f[8], f[7] - f[8]
    sb, db = f[9] + f[10], f[9] - f[10]
    sc, dc = f[11] + f[12], f[11] - f[12]
    sd, dd = f[13] + f[14], f[13] - f[14]
    se, de = f[15] + f[16], f[15] - f[16]
    sg, dg = f[17] + f[18], f[17] - f[18]
    sxy, txy = sa + sb, sa - sb
    sxz, txz = sc + sd, sc - sd
    syz, tyz = se + sg, se - sg
    ax_ab, ay_ab = da + db, da - db
    ax_cd, az_cd = dc + dd, dc - dd
    ay_eg, az_eg = de + dg, de - dg
    near, far = sx + sy + sz, sxy + sxz + syz
    rho = f[0] + near + far
    ex, ey, ez = ax_ab + ax_cd, ay_ab + ay_eg, az_cd + az_eg
    jx, jy, jz = dx + ex, dy + ey, dz + ez
    inv = 1.0 / rho
    ux, uy, uz = jx * inv, jy * inv, jz * inv
    xx, yy, zz = jx * ux, jy * uy, jz * uz
    jj = xx + yy + zz
    energy = (-30.0 * f[0] - 11.0 * near + 8.0 * far) - (-11.0 * rho + 19.0 * jj)
    square = (12.0 * f[0] - 4.0 * near + far) - (3.0 * rho - 5.5 * jj)
    kx = (1.2 / 40.0) * (ex - 4.0 * dx + (2.0 / 3.0) * jx)
    ky = (1.2 / 40.0) * (ey - 4.0 * dy + (2.0 / 3.0) * jy)
    kz = (1.2 / 40.0) * (ez - 4.0 * dz + (2.0 / 3.0) * jz)
    yz_near, xyz_far = sy + sz, sxy + sxz - 2.0 * syz
    pxx_eq = 2.0 * xx - yy - zz
    pww_eq = yy - zz
    pxx = (5.0 / 3.0 / 36.0) * (2.0 * sx - yz_near + xyz_far - pxx_eq)
    pixx = (1.4 / 72.0) * (-4.0 * sx + 2.0 * yz_near + xyz_far + 0.5 * pxx_eq)
    w_near, w_far = sy - sz, sxy - sxz
    pww = (5.0 / 3.0 / 12.0) * (w_near + w_far - pww_eq)
    piww = (1.4 / 24.0) * (w_far - 2.0 * w_near + 0.5 * pww_eq)
    pxy = (5.0 / 3.0 / 4.0) * (txy - jx * uy)
    pyz = (5.0 / 3.0 / 4.0) * (tyz - jy * uz)
    pxz = (5.0 / 3.0 / 4.0) * (txz - jx * uz)
    mx = (1.98 / 8.0) * (ax_ab - ax_cd)
    my = (1.98 / 8.0) * (ay_eg - ay_ab)
    mz = (1.98 / 8.0) * (az_cd - az_eg)
    energy = (1.19 / 2394.0) * energy
    square = (1.4 / 252.0) * square
    axis = -11.0 * energy - 4.0 * square
    across = pxx - 2.0 * pixx
    split = pww - 2.0 * piww
    edge = 8.0 * energy + square
    pp, ww = pxx + pixx, pww + piww
    even = [
        axis + 2.0 * across,
        axis - across + split,
        axis - across - split,
        edge + pp + ww + pxy,
        edge + pp + ww - pxy,
        edge + pp - ww + pxz,
        edge + pp - ww - pxz,
        edge - 2.0 * pp + pyz,
        edge - 2.0 * pp - pyz,
    ]
    odd = [
        -4.0 * kx,
        -4.0 * ky,
        -4.0 * kz,
        (kx + mx) + (ky - my),
        (kx + mx) - (ky - my),
        (kx - mx) + (kz + mz),
        (kx - mx) - (kz + mz),
        (ky + my) + (kz - mz),
        (ky + my) - (kz - mz),
    ]
    change = [12.0 * square - 30.0 * energy]
    for pair in range(9):
        change += [even[pair] + odd[pair], even[pair] - odd[pair]]
    fluid = solid != 1
    return [jnp.where(fluid, f[i] - change[i], f[i]) for i in range(19)]


def slots_to_row(value):
    owners, capacity = value.shape
    wide = jnp.concatenate([value, jnp.zeros((owners, LANES - capacity), value.dtype)], axis=1)
    return jnp.sum(pltpu.roll(wide, 0, 1, stride=capacity, stride_axis=0), axis=0, keepdims=True)


def membrane_base(pos_ref, vel_ref, rest_ref, tri_ref, fab_ref):
    nodes = pos_ref.shape[2]
    count = tri_ref.shape[2]
    wide = -(-count // LANES) * LANES
    patches = nodes // PATCH
    stretch = [pos_ref[a] - rest_ref[a] for a in range(3)]
    corners = [
        jnp.concatenate([tri_ref[t], jnp.full((1, wide - count), -1, jnp.int32)], axis=1) for t in range(3)
    ]
    patch = jnp.maximum(corners[0], 0) // PATCH
    local = [(corner - patch * PATCH).astype(jnp.float32) for corner in corners]
    node_ids = iota((PATCH, LANES), 0).astype(jnp.float32).astype(jnp.bfloat16)
    blocks = []
    for k in range(0, wide, LANES):
        block = jnp.zeros((PATCH, LANES), jnp.bfloat16)
        for corner in local:
            row = jnp.broadcast_to(corner[:, k : k + LANES], (16, LANES)).astype(jnp.bfloat16)
            row = jnp.concatenate([row] * (PATCH // 16), axis=0)
            block = block + jnp.where(node_ids == row, jnp.ones_like(block), jnp.zeros_like(block))
        blocks.append(block)
    hits = jnp.concatenate(blocks, axis=1)
    stretch8 = jnp.concatenate(stretch + [jnp.zeros((5, nodes), jnp.float32)], axis=0)
    pieces = [stacked3(stretch8[:, p * PATCH : (p + 1) * PATCH]) for p in range(patches)]
    sums = dot_nn(jnp.concatenate(pieces, axis=0), hits)
    total = jnp.zeros((8, wide), jnp.float32)
    for p in range(patches):
        total = jnp.where(patch == p, sum3(sums[p * 24 : (p + 1) * 24]), total)
    total = jnp.where(iota(total.shape, 0) == 3, 1.0, total)
    pieces = [stacked3(jnp.where(patch == p, total, 0.0)) for p in range(patches)]
    sums = dot_nt(jnp.concatenate(pieces, axis=0), hits)
    back = jnp.concatenate([sum3(sums[p * 24 : (p + 1) * 24]) for p in range(patches)], axis=1)
    for a in range(3):
        elastic = SPRING * back[a : a + 1] - 3.0 * SPRING * back[3:4] * stretch[a]
        base = (1.0 - DAMPING) * vel_ref[a] + elastic
        for k in range(nodes // LANES):
            row = 4 + a * (nodes // LANES) + k
            fab_ref[row : row + 1] = base[:, k * LANES : (k + 1) * LANES]


def collide_kernel(pop_hbm, solid_hbm, post_ref, up_ref, down_ref, pop_ref, solid_ref, sems):
    copies = [
        pltpu.make_async_copy(pop_hbm, pop_ref, sems.at[0]),
        pltpu.make_async_copy(solid_hbm, solid_ref, sems.at[1]),
    ]
    for copy in copies:
        copy.start()
    for copy in copies:
        copy.wait()
    size_x = post_ref.shape[1]
    for x in range(size_x):
        post = collided([pop_ref[i, x] for i in range(19)], solid_ref[x])
        for i in range(19):
            post_ref[i, x] = post[i]
            if x == size_x - 1 and i in SIDES[0][0]:
                up_ref[SIDES[0][0].index(i)] = post[i]
            if x == 0 and i in SIDES[0][1]:
                down_ref[SIDES[0][1].index(i)] = post[i]


def fabric_kernel(
    post_ref, cell_ref, dir_ref, node_ref, wall_ref, pos_ref, vel_ref, rest_ref, tri_ref,
    fab_ref, kind_ref, back_ref,
):
    membrane_base(pos_ref, vel_ref, rest_ref, tri_ref, fab_ref)
    size_x, size_y = post_ref.shape[1:3]
    rows = size_x * size_y
    cell = slots_to_row(cell_ref[0, 0, 0].astype(jnp.float32)).astype(jnp.int32)
    way = slots_to_row(dir_ref[0, 0, 0].astype(jnp.float32))
    node = slots_to_row(node_ref[0, 0, 0].astype(jnp.float32))
    live = node >= 0.0
    unit = []
    for a in range(3):
        u = jnp.zeros_like(way)
        for i in range(1, 19):
            if DIRECTIONS[i][a]:
                u = jnp.where(way == float(i), float(DIRECTIONS[i][a]), u)
        unit.append(u)
    weight = jnp.where(way >= 7.0, 6.0 / 36.0, 6.0 / 18.0)
    wall = [slots_to_row(wall_ref[0, 0, 0, a]) for a in range(3)]
    term = weight * (unit[0] * wall[0] + unit[1] * wall[1] + unit[2] * wall[2])
    at_row = jnp.where((iota((rows, LANES), 0) == (cell >> 7)) & live, 1.0, 0.0)
    at_lane = one_hot(iota((LANES, LANES), 0) == (cell & (LANES - 1)))
    left = jnp.concatenate([at_row * way] + [at_row * t for t in split3(term)], axis=0)
    maps = dot_nt(left.astype(jnp.bfloat16), at_lane)
    kind = maps[:rows]
    added = sum3(maps[rows:])
    taken = []
    for x in range(size_x):
        k = kind[x * size_y : (x + 1) * size_y]
        t = jnp.zeros_like(k)
        for i in range(1, 19):
            t = jnp.where(k == float(i), post_ref[OPPOSITE[i], x], t)
        taken.append(t)
        kind_ref[x] = k
        back_ref[x] = t + added[x * size_y : (x + 1) * size_y]
    strength = 2.0 * jnp.concatenate(taken, axis=0) + added
    at_link = sum3(dot_nn(stacked3(strength), at_lane))
    push = jnp.sum(at_row * at_link, axis=0, keepdims=True)
    fab_ref[0:1] = node
    for a in range(3):
        fab_ref[1 + a : 2 + a] = -unit[a] * push


def source_tile(post_ref, low_ref, high_ref, i, x):
    size_x = post_ref.shape[1]
    from_x = x - DIRECTIONS[i][0]
    if from_x < 0:
        return low_ref.at[SIDES[0][0].index(i)]
    if from_x >= size_x:
        return high_ref.at[SIDES[0][1].index(i)]
    return post_ref.at[i, from_x]


def side_kernel(post_ref, low_ref, high_ref, fab_ref, across_ref, near_ref, middle_ref):
    size_x, size_y = post_ref.shape[1:3]
    odd = lax.rem(lax.axis_index("gy"), 2) == 1
    near_ref[:FAB] = fab_ref[...]
    near_ref[FAB : 2 * FAB] = across_ref[...]
    for k in range(5):
        for x in range(size_x):
            at = k * size_x + x
            up = source_tile(post_ref, low_ref, high_ref, SIDES[1][0][k], x)[size_y - 1 : size_y]
            down = source_tile(post_ref, low_ref, high_ref, SIDES[1][1][k], x)[0:1]
            near_ref[2 * FAB + at : 2 * FAB + at + 1] = jnp.where(odd, down, up)
            middle_ref[at : at + 1] = jnp.where(odd, up, down)
    end = 5 * size_x
    if middle_ref.shape[0] > end:
        pad = jnp.zeros((middle_ref.shape[0] - end, LANES), jnp.float32)
        near_ref[2 * FAB + end :] = pad
        middle_ref[end:] = pad


def shift_kernel(
    post_ref, xlow_ref, xhigh_ref, fab_ref, across_ref, near_ref, middle_ref,
    rolled_ref, slab_ref,
):
    size_x, size_y = post_ref.shape[1:3]
    place_y = lax.axis_index("gy")
    place_z = lax.axis_index("gz")
    count_y = lax.axis_size("gy")
    odd = lax.rem(place_y, 2) == 1
    sub = iota((size_y, LANES), 0)
    lane = iota((size_y, LANES), 1)
    first, last = place_y == 0, place_y == count_y - 1
    for x in range(size_x):
        up = jnp.zeros((size_y, LANES), jnp.float32)
        down = jnp.zeros((size_y, LANES), jnp.float32)
        for i in range(19):
            tile = source_tile(post_ref, xlow_ref, xhigh_ref, i, x)[...]
            if DIRECTIONS[i][1]:
                side = 0 if DIRECTIONS[i][1] == 1 else 1
                at = SIDES[1][side].index(i) * size_x + x
                by_near = near_ref[2 * FAB + at : 2 * FAB + at + 1]
                by_middle = middle_ref[at : at + 1]
                if side == 0:
                    row = jnp.where(first, WEIGHTS[i], jnp.where(odd, by_near, by_middle))
                    tile = jnp.where(sub == 0, row, pltpu.roll(tile, 1, 0))
                else:
                    row = jnp.where(last, WEIGHTS[i], jnp.where(odd, by_middle, by_near))
                    tile = jnp.where(sub == size_y - 1, row, pltpu.roll(tile, size_y - 1, 0))
            if DIRECTIONS[i][2] == 1:
                k = SIDES[2][0].index(i)
                tile = pltpu.roll(tile, 1, 1)
                up = jnp.where(lane == k, pltpu.roll(tile, k, 1) if k else tile, up)
            if DIRECTIONS[i][2] == -1:
                k = SIDES[2][1].index(i)
                tile = pltpu.roll(tile, LANES - 1, 1)
                down = jnp.where(lane == k, pltpu.roll(tile, k + 1, 1), down)
            rolled_ref[i, x] = tile
        slab_ref[pl.ds((count_y * 2 + x) * 8, 8)] = jnp.where(place_z == 0, up, down)
    pair = place_y ^ 1
    for at, block in (
        (place_y, fab_ref[...]),
        (place_y ^ 2, across_ref[...]),
        (pair, near_ref[:FAB]),
        (pair ^ 2, near_ref[FAB : 2 * FAB]),
    ):
        slab_ref[pl.ds(pl.multiple_of(at * FAB, FAB), FAB)] = block


def final_kernel(
    rolled_ref, kind_ref, back_ref, own_ref, other_ref, pos_ref,
    pop_ref, pos_out_ref, vel_out_ref, wall_out_ref,
):
    size_x = rolled_ref.shape[1]
    size_y = rolled_ref.shape[2]
    place_y = lax.axis_index("gy")
    place_z = lax.axis_index("gz")
    count_y = lax.axis_size("gy")
    lane = iota((size_y, LANES), 1)
    low_end = place_z == 0
    for x in range(size_x):
        kind = kind_ref[x]
        back = back_ref[x]
        face = other_ref[(count_y * 2 + x) * 8 : (count_y * 2 + x + 1) * 8]
        for i in range(19):
            tile = rolled_ref[i, x]
            if DIRECTIONS[i][2] == 1:
                k = SIDES[2][0].index(i)
                halo = pltpu.roll(face, LANES - k, 1) if k else face
                tile = jnp.where(lane == 0, jnp.where(low_end, WEIGHTS[i], halo), tile)
            if DIRECTIONS[i][2] == -1:
                k = SIDES[2][1].index(i)
                halo = pltpu.roll(face, LANES - 1 - k, 1)
                tile = jnp.where(lane == LANES - 1, jnp.where(low_end, halo, WEIGHTS[i]), tile)
            if i:
                tile = jnp.where(kind == float(i), back, tile)
            pop_ref[i, x] = tile

    owners, capacity = wall_out_ref.shape[4], wall_out_ref.shape[5]
    nodes = pos_ref.shape[2]
    parts = nodes // LANES
    slot_owner = iota((1, LANES), 1) // capacity
    owner_base = (slot_owner * nodes).astype(jnp.float32)
    mine = own_ref[pl.ds(pl.multiple_of(place_y * FAB, FAB), FAB)]
    my_node = mine[0:1]
    my_live = my_node >= 0.0
    my_id = jnp.where(my_live, owner_base + my_node, -2.0)
    my_column = jnp.transpose(jnp.broadcast_to(my_id, (LANES, LANES)))
    me = place_y * 2 + place_z
    matches, forces, picked = [], [], jnp.zeros((8, LANES), jnp.float32)
    for group, ref in ((0, own_ref), (1, other_ref)):
        for y in range(count_y):
            m = group * count_y + y
            tile = ref[y * FAB : y * FAB + 8]
            ids = tile[0:1]
            ids = jnp.where(ids >= 0.0, owner_base + ids, -1.0)
            matches.append(one_hot(my_column == ids))
            forces.append(tile)
            shift = lax.rem((m + owners - me) * capacity, LANES)
            picked = jnp.where(slot_owner == m, pltpu.roll(tile, shift, 1), picked)
    force = stacked3(jnp.concatenate(forces, axis=1))
    fluid_at_links = sum3(dot_nt(force, jnp.concatenate(matches, axis=1)))

    every = jnp.concatenate(
        [own_ref[: count_y * FAB], other_ref[: count_y * FAB]], axis=0
    )
    my_int = my_node.astype(jnp.int32)
    at_lane = one_hot(iota((LANES, LANES), 0) == (my_int & (LANES - 1)))
    found = sum3(dot_nn(stacked3(every), at_lane))
    row = iota(found.shape, 0)
    message, inner = row // FAB, row % FAB
    owner = (message % count_y) * 2 + jnp.where(message < count_y, place_z, 1 - place_z)
    fits = (owner == slot_owner) & (inner >= 4) & (inner % parts == (my_int >> 7))
    found = jnp.where(fits, found, 0.0)
    found = sum(found[m * FAB : (m + 1) * FAB] for m in range(2 * count_y))

    node = picked[0:1].astype(jnp.int32)
    row = iota((FAB, LANES), 0)
    spread = jnp.where(row < parts, picked[1:2], jnp.where(row < 2 * parts, picked[2:3], picked[3:4]))
    spread = jnp.where((row < 3 * parts) & (row % parts == (node >> 7)), spread, 0.0)
    at_node = one_hot(iota((LANES, LANES), 0) == (node & (LANES - 1)))
    fluid = sum3(dot_nt(stacked3(spread), at_node))
    moved = []
    for a in range(3):
        for k in range(parts):
            r = a * parts + k
            new = mine[4 + r : 5 + r] + fluid[r : r + 1]
            at = slice(k * LANES, (k + 1) * LANES)
            vel_out_ref[a, :, at] = new
            pos_out_ref[a, :, at] = pos_ref[a, :, at] + new
        base = jnp.sum(found[4 + a * parts : 4 + (a + 1) * parts], axis=0, keepdims=True)
        moved.append(jnp.where(my_live, base + fluid_at_links[1 + a : 2 + a], 0.0))
    moved = jnp.concatenate(moved + [jnp.zeros((5, LANES), jnp.float32)], axis=0)
    for o in range(owners):
        turned = pltpu.roll(moved, LANES - o * capacity, 1) if o else moved
        for a in range(3):
            wall_out_ref[0, 0, 0, a, o : o + 1] = turned[a : a + 1, :capacity]


def ring(count, step):
    return [(i, (i + step) % count) for i in range(count)]


def body(
    populations,
    solid,
    link_cell,
    link_dir,
    link_node,
    link_velocity,
    fabric_position,
    fabric_velocity,
    fabric_rest,
    triangles,
):
    size_x, size_y, size_z = populations.shape[1:]
    owners, capacity = link_node.shape[3:]
    nodes = fabric_position.shape[2]
    count_x, count_y, count_z = (lax.axis_size(name) for name in ("gx", "gy", "gz"))
    folded = (
        (count_y, count_z) == (4, 2)
        and (size_y, size_z) == (8, LANES)
        and owners * capacity == LANES
        and nodes == 4 * LANES
    )
    if not folded:
        return general_body(
            populations, solid, link_cell, link_dir, link_node, link_velocity,
            fabric_position, fabric_velocity, fabric_rest, triangles,
        )
    f32 = jnp.float32
    on_chip = pl.BlockSpec(memory_space=pltpu.VMEM)

    def shape(*dims):
        return jax.ShapeDtypeStruct(dims, f32)

    def kept(*dims):
        return pltpu.VMEM(dims, f32)

    def run(kernel, outs, *args):
        args = [pltpu.with_memory_space_constraint(arg, pltpu.VMEM) for arg in args]
        return pl.pallas_call(
            kernel,
            out_shape=outs,
            in_specs=[on_chip] * len(args),
            out_specs=jax.tree.map(lambda _: on_chip, outs),
            name=kernel.__name__,
        )(*args)

    face_x = kept(5, size_y, size_z)
    map_shape = kept(size_x, size_y, size_z)
    given = (populations, solid)
    opened = (kept(*populations.shape), face_x, face_x)
    post, up, down = pl.pallas_call(
        collide_kernel,
        out_shape=opened,
        in_specs=[pl.BlockSpec(memory_space=pl.ANY)] * 2,
        out_specs=(on_chip,) * 3,
        scratch_shapes=[pltpu.VMEM(arg.shape, arg.dtype) for arg in given] + [pltpu.SemaphoreType.DMA((2,))],
        name="collide_kernel",
    )(*given)
    fab, kind, back = run(
        fabric_kernel, (kept(FAB, LANES), map_shape, map_shape),
        post, link_cell, link_dir, link_node, link_velocity, fabric_position, fabric_velocity, fabric_rest, triangles,
    )
    xlow = lax.ppermute(up, "gx", ring(count_x, 1))
    xhigh = lax.ppermute(down, "gx", ring(count_x, -1))
    across = lax.ppermute(fab, "gy", [(y, y ^ 2) for y in range(count_y)])
    face_rows = -(-5 * size_x // 8) * 8
    near, middle = run(
        side_kernel, (kept(2 * FAB + face_rows, LANES), kept(face_rows, LANES)), post, xlow, xhigh, fab, across
    )
    near = lax.ppermute(near, "gy", [(y, y ^ 1) for y in range(count_y)])
    swaps = []
    for y in range(count_y):
        to = y + 1 if y % 2 else y - 1
        for z in range(count_z):
            swaps.append((y * count_z + z, to * count_z + z if 0 <= to < count_y else y * count_z + 1 - z))
    middle = lax.ppermute(middle, ("gy", "gz"), swaps)
    rolled, own = run(
        shift_kernel, (kept(*populations.shape), kept(count_y * FAB + size_x * size_y, LANES)),
        post, xlow, xhigh, fab, across, near, middle,
    )
    other = lax.ppermute(own, "gz", [(0, 1), (1, 0)])
    return run(
        final_kernel,
        (
            shape(*populations.shape),
            shape(*fabric_position.shape),
            shape(*fabric_velocity.shape),
            shape(*link_velocity.shape),
        ),
        rolled, kind, back, own, other, fabric_position,
    )


def solution(mesh):
    placed = (
        P(None, "gx", "gy", "gz"),
        P("gx", "gy", "gz"),
        P("gx", "gy", "gz", None, None),
        P("gx", "gy", "gz", None, None),
        P("gx", "gy", "gz", None, None),
        P("gx", "gy", "gz", None, None, None),
        P(None, "gx", ("gy", "gz")),
        P(None, "gx", ("gy", "gz")),
        P(None, "gx", ("gy", "gz")),
        P(None, "gx", ("gy", "gz")),
    )
    return jax.shard_map(
        body,
        mesh=mesh,
        in_specs=placed,
        out_specs=(
            P(None, "gx", "gy", "gz"),
            P(None, "gx", ("gy", "gz")),
            P(None, "gx", ("gy", "gz")),
            P("gx", "gy", "gz", None, None, None),
        ),
        check_vma=False,
    )
```

```python
import jax
import jax.numpy as jnp
import numpy as np
from jax import lax
from jax.experimental import pallas as pl
from jax.experimental.pallas import tpu as pltpu
from jax.sharding import PartitionSpec as P

SPRING = 0.5
DAMPING = 0.1
DIRECTIONS = [
    [0, 0, 0],
    [1, 0, 0],
    [-1, 0, 0],
    [0, 1, 0],
    [0, -1, 0],
    [0, 0, 1],
    [0, 0, -1],
    [1, 1, 0],
    [-1, -1, 0],
    [1, -1, 0],
    [-1, 1, 0],
    [1, 0, 1],
    [-1, 0, -1],
    [1, 0, -1],
    [-1, 0, 1],
    [0, 1, 1],
    [0, -1, -1],
    [0, 1, -1],
    [0, -1, 1],
]


def extended(cells, sides, width):
    for axis, dim in sides:
        count = lax.axis_size(axis)
        head = lax.slice_in_dim(cells, 0, width, axis=dim)
        tail = lax.slice_in_dim(cells, cells.shape[dim] - width, cells.shape[dim], axis=dim)
        cells = jnp.concatenate(
            [
                lax.ppermute(tail, axis, [(i, (i + 1) % count) for i in range(count)]),
                cells,
                lax.ppermute(head, axis, [((i + 1) % count, i) for i in range(count)]),
            ],
            axis=dim,
        )
    return cells


def lattice():
    velocity_np = np.array(DIRECTIONS)
    weight_np = np.array([1.0 / 3.0] + [1.0 / 18.0] * 6 + [1.0 / 36.0] * 12)
    opposite_list = [
        DIRECTIONS.index([-entry for entry in DIRECTIONS[direction]]) for direction in range(19)
    ]
    along_a = np.array([float(entry[0]) for entry in DIRECTIONS])
    along_b = np.array([float(entry[1]) for entry in DIRECTIONS])
    along_e = np.array([float(entry[2]) for entry in DIRECTIONS])
    speed_sq = along_a * along_a + along_b * along_b + along_e * along_e
    moment_rows = [
        np.ones(19),
        19 * speed_sq - 30,
        (21 * speed_sq * speed_sq - 53 * speed_sq + 24) / 2,
        along_a,
        (5 * speed_sq - 9) * along_a,
        along_b,
        (5 * speed_sq - 9) * along_b,
        along_e,
        (5 * speed_sq - 9) * along_e,
        3 * along_a * along_a - speed_sq,
        (3 * speed_sq - 5) * (3 * along_a * along_a - speed_sq),
        along_b * along_b - along_e * along_e,
        (3 * speed_sq - 5) * (along_b * along_b - along_e * along_e),
        along_a * along_b,
        along_b * along_e,
        along_a * along_e,
        (along_b * along_b - along_e * along_e) * along_a,
        (along_e * along_e - along_a * along_a) * along_b,
        (along_a * along_a - along_b * along_b) * along_e,
    ]
    moment_np = np.stack(moment_rows)
    inverse_np = moment_np.T / np.sum(moment_np * moment_np, axis=1)[None, :]
    viscous = 5.0 / 3.0
    rates_np = np.array(
        [
            0.0,
            1.19,
            1.4,
            0.0,
            1.2,
            0.0,
            1.2,
            0.0,
            1.2,
            viscous,
            1.4,
            viscous,
            1.4,
            viscous,
            viscous,
            viscous,
            1.98,
            1.98,
            1.98,
        ]
    )
    return (velocity_np, weight_np, opposite_list, moment_np, inverse_np, rates_np)


def collide_cells(popul, solid_flat):
    velocity_np, weight_np, opposite_list, moment_np, inverse_np, rates_np = lattice()
    velocity_table = jnp.asarray(velocity_np, jnp.float32)
    weight_table = jnp.asarray(weight_np, jnp.float32)
    density = jnp.sum(popul, axis=0)
    momentum = jnp.dot(
        velocity_table.T, popul, precision=lax.Precision.HIGHEST, preferred_element_type=jnp.float32
    )
    flow = momentum / density
    projected = jnp.dot(
        velocity_table, flow, precision=lax.Precision.HIGHEST, preferred_element_type=jnp.float32
    )
    speed_sq = jnp.sum(flow * flow, axis=0)
    equilibrium = (
        weight_table[:, None]
        * density
        * (1.0 + 3.0 * projected + 4.5 * projected * projected - 1.5 * speed_sq)
    )
    offset = popul - equilibrium
    moments = jnp.dot(
        jnp.asarray(moment_np, jnp.float32),
        offset,
        precision=lax.Precision.HIGHEST,
        preferred_element_type=jnp.float32,
    )
    relaxed = jnp.asarray(rates_np, jnp.float32)[:, None] * moments
    change = jnp.dot(
        jnp.asarray(inverse_np, jnp.float32),
        relaxed,
        precision=lax.Precision.HIGHEST,
        preferred_element_type=jnp.float32,
    )
    return jnp.where(solid_flat[None, :] == 1, popul, popul - change)


def fill_outside(padded, weight_np):
    span_y = padded.shape[2]
    span_z = padded.shape[3]
    place_y = lax.axis_index("gy")
    place_z = lax.axis_index("gz")
    count_y = lax.axis_size("gy")
    count_z = lax.axis_size("gz")
    rows_y = jnp.arange(span_y)
    rows_z = jnp.arange(span_z)
    out_y = (rows_y == 0) & (place_y == 0) | (rows_y == span_y - 1) & (place_y == count_y - 1)
    out_z = (rows_z == 0) & (place_z == 0) | (rows_z == span_z - 1) & (place_z == count_z - 1)
    outside = out_y[:, None] | out_z[None, :]
    return jnp.where(
        outside[None, None], jnp.asarray(weight_np, jnp.float32)[:, None, None, None], padded
    )


def propagate(padded, size_x, size_y, size_z):
    pieces = []
    for direction in range(19):
        shift_x = DIRECTIONS[direction][0]
        shift_y = DIRECTIONS[direction][1]
        shift_z = DIRECTIONS[direction][2]
        plane = padded[direction]
        pieces.append(
            lax.slice(
                plane,
                (1 - shift_x, 1 - shift_y, 1 - shift_z),
                (1 - shift_x + size_x, 1 - shift_y + size_y, 1 - shift_z + size_z),
            )
        )
    return jnp.stack(pieces)


def membrane(positions, rest, triangle_nodes):
    force = jnp.zeros(positions.shape, jnp.float32)
    for first, second in ((0, 1), (1, 2), (2, 0)):
        head = triangle_nodes[first]
        tail = triangle_nodes[second]
        stretch = positions[:, tail] - positions[:, head] - (rest[:, tail] - rest[:, head])
        force = force.at[:, head].add(SPRING * stretch)
        force = force.at[:, tail].add(-SPRING * stretch)
    return force


def general_body(
    populations,
    solid,
    link_cell,
    link_dir,
    link_node,
    link_velocity,
    fabric_position,
    fabric_velocity,
    fabric_rest,
    triangles,
):
    velocity_np, weight_np, opposite_list, moment_np, inverse_np, rates_np = lattice()
    velocity_table = jnp.asarray(velocity_np, jnp.float32)
    weight_table = jnp.asarray(weight_np, jnp.float32)
    opposite_table = jnp.asarray(opposite_list, jnp.int32)
    size_x = populations.shape[1]
    size_y = populations.shape[2]
    size_z = populations.shape[3]
    cells = size_x * size_y * size_z
    post = collide_cells(populations.reshape(19, cells), solid.reshape(cells)).reshape(
        populations.shape
    )
    padded = extended(post, (("gx", 1), ("gy", 2), ("gz", 3)), 1)
    padded = fill_outside(padded, weight_np)
    propagated = propagate(padded, size_x, size_y, size_z).reshape(19, cells)
    owners_n = link_node.shape[3]
    capacity = link_node.shape[4]
    node_rows = link_node.reshape(owners_n, capacity)
    cell_rows = link_cell.reshape(owners_n, capacity)
    dir_rows = link_dir.reshape(owners_n, capacity)
    live = node_rows >= 0
    post_flat = post.reshape(19, cells)
    reflected = post_flat[opposite_table[dir_rows], cell_rows]
    link_unit = velocity_table[dir_rows]
    wall = jnp.moveaxis(link_velocity.reshape(3, owners_n, capacity), 0, -1)
    returned = reflected + 6.0 * weight_table[dir_rows] * jnp.sum(link_unit * wall, axis=-1)
    populations_next = propagated.at[jnp.where(live, dir_rows, 19), cell_rows].set(
        returned, mode="drop"
    )
    strength = reflected + returned
    positions = fabric_position.reshape(3, -1)
    velocities = fabric_velocity.reshape(3, -1)
    rest = fabric_rest.reshape(3, -1)
    nodes_n = positions.shape[1]
    elastic = membrane(positions, rest, triangles.reshape(3, -1))
    link_force = jnp.moveaxis(-link_unit * strength[..., None], -1, 0)
    got_nodes, got_force = (
        lax.all_to_all(node_rows[None], ("gy", "gz"), split_axis=1, concat_axis=1, tiled=True),
        lax.all_to_all(link_force, ("gy", "gz"), split_axis=1, concat_axis=1, tiled=True),
    )
    got_ids = got_nodes[0]
    got_live = got_ids >= 0
    target = jnp.where(got_live, got_ids, nodes_n).reshape(-1)
    fluid_force = (
        jnp.zeros((3, nodes_n), jnp.float32)
        .at[:, target]
        .add(got_force.reshape(3, -1), mode="drop")
    )
    velocity_next = (1.0 - DAMPING) * velocities + (fluid_force + elastic)
    position_next = positions + velocity_next
    reply = jnp.where(got_live[None], velocity_next[:, jnp.where(got_live, got_ids, 0)], 0.0)
    wall_next = lax.all_to_all(reply, ("gy", "gz"), split_axis=1, concat_axis=1, tiled=True)
    return (
        populations_next.reshape(populations.shape),
        position_next.reshape(fabric_position.shape),
        velocity_next.reshape(fabric_velocity.shape),
        wall_next.reshape(link_velocity.shape),
    )


WEIGHTS = [1.0 / 3.0] + [1.0 / 18.0] * 6 + [1.0 / 36.0] * 12
OPPOSITE = [DIRECTIONS.index([-entry for entry in d]) for d in DIRECTIONS]
SIDES = [
    ([i for i in range(19) if DIRECTIONS[i][a] == 1], [i for i in range(19) if DIRECTIONS[i][a] == -1])
    for a in range(3)
]
LANES = 128
PATCH = 256
FAB = 16
WIDE = 80


def iota(shape, axis):
    return lax.broadcasted_iota(jnp.int32, shape, axis)


def split3(value):
    high = value.astype(jnp.bfloat16).astype(jnp.float32)
    rest = value - high
    middle = rest.astype(jnp.bfloat16).astype(jnp.float32)
    return high, middle, rest - middle


def stacked3(value):
    return jnp.concatenate(split3(value), axis=0).astype(jnp.bfloat16)


def sum3(value):
    rows = value.shape[0] // 3
    return value[:rows] + value[rows : 2 * rows] + value[2 * rows :]


def dot_nn(left, right):
    return lax.dot_general(left, right, (((1,), (0,)), ((), ())), preferred_element_type=jnp.float32)


def dot_nt(left, right):
    return lax.dot_general(left, right, (((1,), (1,)), ((), ())), preferred_element_type=jnp.float32)


def one_hot(mask):
    return jnp.where(mask, 1.0, 0.0).astype(jnp.bfloat16)


def collided(f, solid):
    sx, dx = f[1] + f[2], f[1] - f[2]
    sy, dy = f[3] + f[4], f[3] - f[4]
    sz, dz = f[5] + f[6], f[5] - f[6]
    sa, da = f[7] + f[8], f[7] - f[8]
    sb, db = f[9] + f[10], f[9] - f[10]
    sc, dc = f[11] + f[12], f[11] - f[12]
    sd, dd = f[13] + f[14], f[13] - f[14]
    se, de = f[15] + f[16], f[15] - f[16]
    sg, dg = f[17] + f[18], f[17] - f[18]
    sxy, txy = sa + sb, sa - sb
    sxz, txz = sc + sd, sc - sd
    syz, tyz = se + sg, se - sg
    ax_ab, ay_ab = da + db, da - db
    ax_cd, az_cd = dc + dd, dc - dd
    ay_eg, az_eg = de + dg, de - dg
    near, far = sx + sy + sz, sxy + sxz + syz
    rho = f[0] + near + far
    ex, ey, ez = ax_ab + ax_cd, ay_ab + ay_eg, az_cd + az_eg
    jx, jy, jz = dx + ex, dy + ey, dz + ez
    inv = 1.0 / rho
    ux, uy, uz = jx * inv, jy * inv, jz * inv
    xx, yy, zz = jx * ux, jy * uy, jz * uz
    jj = xx + yy + zz
    energy = (-30.0 * f[0] - 11.0 * near + 8.0 * far) - (-11.0 * rho + 19.0 * jj)
    square = (12.0 * f[0] - 4.0 * near + far) - (3.0 * rho - 5.5 * jj)
    kx = (1.2 / 40.0) * (ex - 4.0 * dx + (2.0 / 3.0) * jx)
    ky = (1.2 / 40.0) * (ey - 4.0 * dy + (2.0 / 3.0) * jy)
    kz = (1.2 / 40.0) * (ez - 4.0 * dz + (2.0 / 3.0) * jz)
    yz_near, xyz_far = sy + sz, sxy + sxz - 2.0 * syz
    pxx_eq = 2.0 * xx - yy - zz
    pww_eq = yy - zz
    pxx = (5.0 / 3.0 / 36.0) * (2.0 * sx - yz_near + xyz_far - pxx_eq)
    pixx = (1.4 / 72.0) * (-4.0 * sx + 2.0 * yz_near + xyz_far + 0.5 * pxx_eq)
    w_near, w_far = sy - sz, sxy - sxz
    pww = (5.0 / 3.0 / 12.0) * (w_near + w_far - pww_eq)
    piww = (1.4 / 24.0) * (w_far - 2.0 * w_near + 0.5 * pww_eq)
    pxy = (5.0 / 3.0 / 4.0) * (txy - jx * uy)
    pyz = (5.0 / 3.0 / 4.0) * (tyz - jy * uz)
    pxz = (5.0 / 3.0 / 4.0) * (txz - jx * uz)
    mx = (1.98 / 8.0) * (ax_ab - ax_cd)
    my = (1.98 / 8.0) * (ay_eg - ay_ab)
    mz = (1.98 / 8.0) * (az_cd - az_eg)
    energy = (1.19 / 2394.0) * energy
    square = (1.4 / 252.0) * square
    axis = -11.0 * energy - 4.0 * square
    across = pxx - 2.0 * pixx
    split = pww - 2.0 * piww
    edge = 8.0 * energy + square
    pp, ww = pxx + pixx, pww + piww
    even = [
        axis + 2.0 * across,
        axis - across + split,
        axis - across - split,
        edge + pp + ww + pxy,
        edge + pp + ww - pxy,
        edge + pp - ww + pxz,
        edge + pp - ww - pxz,
        edge - 2.0 * pp + pyz,
        edge - 2.0 * pp - pyz,
    ]
    odd = [
        -4.0 * kx,
        -4.0 * ky,
        -4.0 * kz,
        (kx + mx) + (ky - my),
        (kx + mx) - (ky - my),
        (kx - mx) + (kz + mz),
        (kx - mx) - (kz + mz),
        (ky + my) + (kz - mz),
        (ky + my) - (kz - mz),
    ]
    change = [12.0 * square - 30.0 * energy]
    for pair in range(9):
        change += [even[pair] + odd[pair], even[pair] - odd[pair]]
    fluid = solid != 1
    return [jnp.where(fluid, f[i] - change[i], f[i]) for i in range(19)]


def slots_to_row(value):
    owners, capacity = value.shape
    wide = jnp.concatenate([value, jnp.zeros((owners, LANES - capacity), value.dtype)], axis=1)
    return jnp.sum(pltpu.roll(wide, 0, 1, stride=capacity, stride_axis=0), axis=0, keepdims=True)


def membrane_base(pos_ref, vel_ref, rest_ref, tri_ref, fab_ref):
    nodes = pos_ref.shape[2]
    count = tri_ref.shape[2]
    wide = -(-count // LANES) * LANES
    patches = nodes // PATCH
    stretch = [pos_ref[a] - rest_ref[a] for a in range(3)]
    corners = [
        jnp.concatenate([tri_ref[t], jnp.full((1, wide - count), -1, jnp.int32)], axis=1) for t in range(3)
    ]
    patch = jnp.maximum(corners[0], 0) // PATCH
    local = [(corner - patch * PATCH).astype(jnp.float32) for corner in corners]
    node_ids = iota((PATCH, LANES), 0).astype(jnp.float32).astype(jnp.bfloat16)
    blocks = []
    for k in range(0, wide, LANES):
        block = jnp.zeros((PATCH, LANES), jnp.bfloat16)
        for corner in local:
            row = jnp.broadcast_to(corner[:, k : k + LANES], (16, LANES)).astype(jnp.bfloat16)
            row = jnp.concatenate([row] * (PATCH // 16), axis=0)
            block = block + jnp.where(node_ids == row, jnp.ones_like(block), jnp.zeros_like(block))
        blocks.append(block)
    hits = jnp.concatenate(blocks, axis=1)
    stretch8 = jnp.concatenate(stretch + [jnp.zeros((5, nodes), jnp.float32)], axis=0)
    pieces = [stacked3(stretch8[:, p * PATCH : (p + 1) * PATCH]) for p in range(patches)]
    sums = dot_nn(jnp.concatenate(pieces, axis=0), hits)
    total = jnp.zeros((8, wide), jnp.float32)
    for p in range(patches):
        total = jnp.where(patch == p, sum3(sums[p * 24 : (p + 1) * 24]), total)
    total = jnp.where(iota(total.shape, 0) == 3, 1.0, total)
    pieces = [stacked3(jnp.where(patch == p, total, 0.0)) for p in range(patches)]
    sums = dot_nt(jnp.concatenate(pieces, axis=0), hits)
    back = jnp.concatenate([sum3(sums[p * 24 : (p + 1) * 24]) for p in range(patches)], axis=1)
    for a in range(3):
        elastic = SPRING * back[a : a + 1] - 3.0 * SPRING * back[3:4] * stretch[a]
        base = (1.0 - DAMPING) * vel_ref[a] + elastic
        for k in range(nodes // LANES):
            row = 4 + a * (nodes // LANES) + k
            fab_ref[row : row + 1] = base[:, k * LANES : (k + 1) * LANES]


def open_kernel(
    pop_hbm, solid_hbm, cell_hbm, dir_hbm, node_hbm, wall_hbm, pos_hbm, vel_hbm, rest_hbm, tri_hbm,
    post_ref, up_ref, down_ref, fab_ref, kind_ref, back_ref,
    pop_ref, solid_ref, cell_ref, dir_ref, node_ref, wall_ref, pos_ref, vel_ref, rest_ref, tri_ref, sems,
):
    moves = [
        (tri_hbm, tri_ref), (pos_hbm, pos_ref), (rest_hbm, rest_ref), (vel_hbm, vel_ref),
        (pop_hbm, pop_ref), (solid_hbm, solid_ref),
        (cell_hbm, cell_ref), (dir_hbm, dir_ref), (node_hbm, node_ref), (wall_hbm, wall_ref),
    ]
    copies = [pltpu.make_async_copy(src, dst, sems.at[k]) for k, (src, dst) in enumerate(moves)]
    for copy in copies:
        copy.start()
    for copy in copies[:4]:
        copy.wait()
    membrane_base(pos_ref, vel_ref, rest_ref, tri_ref, fab_ref)
    for copy in copies[4:]:
        copy.wait()
    size_x, size_y = post_ref.shape[1:3]
    rows = size_x * size_y
    cell = slots_to_row(cell_ref[0, 0, 0].astype(jnp.float32)).astype(jnp.int32)
    way = slots_to_row(dir_ref[0, 0, 0].astype(jnp.float32))
    node = slots_to_row(node_ref[0, 0, 0].astype(jnp.float32))
    live = node >= 0.0
    unit = []
    for a in range(3):
        u = jnp.zeros_like(way)
        for i in range(1, 19):
            if DIRECTIONS[i][a]:
                u = jnp.where(way == float(i), float(DIRECTIONS[i][a]), u)
        unit.append(u)
    weight = jnp.where(way >= 7.0, 6.0 / 36.0, 6.0 / 18.0)
    wall = [slots_to_row(wall_ref[0, 0, 0, a]) for a in range(3)]
    term = weight * (unit[0] * wall[0] + unit[1] * wall[1] + unit[2] * wall[2])
    at_row = jnp.where((iota((rows, LANES), 0) == (cell >> 7)) & live, 1.0, 0.0)
    at_lane = one_hot(iota((LANES, LANES), 0) == (cell & (LANES - 1)))
    left = jnp.concatenate([at_row * way] + [at_row * t for t in split3(term)], axis=0)
    maps = dot_nt(left.astype(jnp.bfloat16), at_lane)
    kind = maps[:rows]
    added = sum3(maps[rows:])
    taken = []
    for x in range(size_x):
        post = collided([pop_ref[i, x] for i in range(19)], solid_ref[x])
        k = kind[x * size_y : (x + 1) * size_y]
        t = jnp.zeros_like(k)
        for i in range(19):
            post_ref[i, x] = post[i]
            if x == size_x - 1 and i in SIDES[0][0]:
                up_ref[SIDES[0][0].index(i)] = post[i]
            if x == 0 and i in SIDES[0][1]:
                down_ref[SIDES[0][1].index(i)] = post[i]
            if i:
                t = jnp.where(k == float(OPPOSITE[i]), post[i], t)
        taken.append(t)
        kind_ref[x] = k
        back_ref[x] = t + added[x * size_y : (x + 1) * size_y]
    strength = 2.0 * jnp.concatenate(taken, axis=0) + added
    at_link = sum3(dot_nn(stacked3(strength), at_lane))
    push = jnp.sum(at_row * at_link, axis=0, keepdims=True)
    fab_ref[FAB:] = jnp.zeros((WIDE - FAB, LANES), jnp.float32)
    fab_ref[0:1] = node
    for a in range(3):
        fab_ref[1 + a : 2 + a] = -unit[a] * push


def source_tile(post_ref, low_ref, high_ref, i, x):
    size_x = post_ref.shape[1]
    from_x = x - DIRECTIONS[i][0]
    if from_x < 0:
        return low_ref.at[SIDES[0][0].index(i)]
    if from_x >= size_x:
        return high_ref.at[SIDES[0][1].index(i)]
    return post_ref.at[i, from_x]


def pair_kernel(fab_ref, other_ref, pair_ref):
    low = lax.axis_index("gz") == 0
    pair_ref[:FAB] = jnp.where(low, fab_ref[:FAB], other_ref[:FAB])
    pair_ref[FAB:] = jnp.where(low, other_ref[:FAB], fab_ref[:FAB])


def face_rows(post_ref, low_ref, high_ref, out_ref, start, upward):
    size_x, size_y = post_ref.shape[1:3]
    for k in range(5):
        for x in range(size_x):
            at = start + k * size_x + x
            up = source_tile(post_ref, low_ref, high_ref, SIDES[1][0][k], x)[size_y - 1 : size_y]
            down = source_tile(post_ref, low_ref, high_ref, SIDES[1][1][k], x)[0:1]
            out_ref[at : at + 1] = jnp.where(upward, up, down)
    end = start + 5 * size_x
    if out_ref.shape[0] > end:
        out_ref[end:] = jnp.zeros((out_ref.shape[0] - end, LANES), jnp.float32)


def middle_kernel(post_ref, low_ref, high_ref, middle_ref):
    odd = lax.rem(lax.axis_index("gy"), 2) == 1
    face_rows(post_ref, low_ref, high_ref, middle_ref, 0, odd)


def near_kernel(post_ref, low_ref, high_ref, cross_ref, _, near_ref):
    odd = lax.rem(lax.axis_index("gy"), 2) == 1
    near_ref[: 2 * FAB] = cross_ref[...]
    face_rows(post_ref, low_ref, high_ref, near_ref, 2 * FAB, jnp.logical_not(odd))


def shift_kernel(
    post_ref, xlow_ref, xhigh_ref, cross_ref, near_ref, middle_ref, rolled_ref, swap_ref,
):
    size_x, size_y = post_ref.shape[1:3]
    place_y = lax.axis_index("gy")
    place_z = lax.axis_index("gz")
    count_y = lax.axis_size("gy")
    odd = lax.rem(place_y, 2) == 1
    sub = iota((size_y, LANES), 0)
    lane = iota((size_y, LANES), 1)
    first, last = place_y == 0, place_y == count_y - 1
    swap_ref[: 2 * FAB] = cross_ref[...]
    swap_ref[2 * FAB : 4 * FAB] = near_ref[: 2 * FAB]
    for x in range(size_x):
        up = jnp.zeros((size_y, LANES), jnp.float32)
        down = jnp.zeros((size_y, LANES), jnp.float32)
        for i in range(19):
            tile = source_tile(post_ref, xlow_ref, xhigh_ref, i, x)[...]
            if DIRECTIONS[i][1]:
                side = 0 if DIRECTIONS[i][1] == 1 else 1
                at = SIDES[1][side].index(i) * size_x + x
                by_near = near_ref[2 * FAB + at : 2 * FAB + at + 1]
                by_middle = middle_ref[at : at + 1]
                if side == 0:
                    row = jnp.where(first, WEIGHTS[i], jnp.where(odd, by_near, by_middle))
                    tile = jnp.where(sub == 0, row, pltpu.roll(tile, 1, 0))
                else:
                    row = jnp.where(last, WEIGHTS[i], jnp.where(odd, by_middle, by_near))
                    tile = jnp.where(sub == size_y - 1, row, pltpu.roll(tile, size_y - 1, 0))
            if DIRECTIONS[i][2] == 1:
                k = SIDES[2][0].index(i)
                tile = pltpu.roll(tile, 1, 1)
                up = jnp.where(lane == k, pltpu.roll(tile, k, 1) if k else tile, up)
            if DIRECTIONS[i][2] == -1:
                k = SIDES[2][1].index(i)
                tile = pltpu.roll(tile, LANES - 1, 1)
                down = jnp.where(lane == k, pltpu.roll(tile, k + 1, 1), down)
            rolled_ref[i, x] = tile
        swap_ref[4 * FAB + x * size_y : 4 * FAB + (x + 1) * size_y] = jnp.where(place_z == 0, up, down)


def fabric_part(pairs, chips, start, mine, nodes, capacity):
    parts = nodes // LANES
    place_z = lax.axis_index("gz")
    me = lax.axis_index("gy") * 2 + place_z
    slot_owner = iota((1, LANES), 1) // capacity
    owner_base = (slot_owner * nodes).astype(jnp.float32)
    my_node = mine[0:1]
    my_id = jnp.where(my_node >= 0.0, owner_base + my_node, -2.0)
    my_column = jnp.transpose(jnp.broadcast_to(my_id, (LANES, LANES)))
    matches, forces, picked = [], [], jnp.zeros((8, LANES), jnp.float32)
    for m in range(2 * len(pairs)):
        tile = pairs[m // 2][m % 2 * FAB : m % 2 * FAB + 8]
        ids = tile[0:1]
        ids = jnp.where(ids >= 0.0, owner_base + ids, -1.0)
        matches.append(one_hot(my_column == ids))
        forces.append(tile)
        shift = lax.rem((start + m + LANES // capacity - me) * capacity, LANES)
        picked = jnp.where(slot_owner == start + m, pltpu.roll(tile, shift, 1), picked)
    pushed = sum3(dot_nt(stacked3(jnp.concatenate(forces, axis=1)), jnp.concatenate(matches, axis=1)))

    my_int = my_node.astype(jnp.int32)
    at_lane = one_hot(iota((LANES, LANES), 0) == (my_int & (LANES - 1)))
    found = sum3(dot_nn(stacked3(jnp.concatenate(pairs, axis=0)), at_lane))
    row = iota((FAB, LANES), 0)
    fits = (row >= 4) & (row % parts == (my_int >> 7))
    base = jnp.zeros((FAB, LANES), jnp.float32)
    for m in range(2 * len(pairs)):
        owner = chips[m // 2] * 2 + m % 2
        base = jnp.where(fits & (slot_owner == owner), found[m * FAB : (m + 1) * FAB], base)
    return jnp.concatenate([pushed, base, picked], axis=0)


def half_kernel(fab_ref, pair_ref, cross_ref, acc_ref):
    place_y = lax.axis_index("gy")
    far = place_y ^ jnp.where(lax.axis_index("gz") == 0, 1, 2)
    nodes, capacity = 4 * LANES, LANES // 8
    acc_ref[...] = fabric_part([pair_ref[...], cross_ref[...]], [place_y, far], 0, fab_ref[:FAB], nodes, capacity)


def final_kernel(
    rolled_ref, kind_ref, back_ref, fab_ref, acc_ref, near_ref, other_ref, pos_ref,
    pop_hbm, pos_hbm, vel_hbm, wall_hbm,
    pop_ref, pos_out_ref, vel_out_ref, wall_out_ref, sems,
):
    size_x, size_y = rolled_ref.shape[1:3]
    place_y = lax.axis_index("gy")
    place_z = lax.axis_index("gz")
    lane = iota((size_y, LANES), 1)
    low_end = place_z == 0
    copies = []
    for x in range(size_x):
        kind = kind_ref[x]
        back = back_ref[x]
        face = other_ref[4 * FAB + x * size_y : 4 * FAB + (x + 1) * size_y]
        for i in range(19):
            tile = rolled_ref[i, x]
            if DIRECTIONS[i][2] == 1:
                k = SIDES[2][0].index(i)
                halo = pltpu.roll(face, LANES - k, 1) if k else face
                tile = jnp.where(lane == 0, jnp.where(low_end, WEIGHTS[i], halo), tile)
            if DIRECTIONS[i][2] == -1:
                k = SIDES[2][1].index(i)
                halo = pltpu.roll(face, LANES - 1 - k, 1)
                tile = jnp.where(lane == LANES - 1, jnp.where(low_end, halo, WEIGHTS[i]), tile)
            if i:
                tile = jnp.where(kind == float(i), back, tile)
            pop_ref[i, x] = tile
        copies.append(pltpu.make_async_copy(pop_ref.at[:, x], pop_hbm.at[:, x], sems.at[x]))
        copies[-1].start()

    owners, capacity = wall_out_ref.shape[4], wall_out_ref.shape[5]
    nodes = pos_ref.shape[2]
    parts = nodes // LANES
    mine = fab_ref[:FAB]
    last = jnp.where(low_end, other_ref[2 * FAB : 4 * FAB], near_ref[: 2 * FAB])
    far = place_y ^ jnp.where(low_end, 2, 1)
    acc = fabric_part([other_ref[: 2 * FAB], last], [far, place_y ^ 3], 4, mine, nodes, capacity) + acc_ref[...]
    pushed, found, picked = acc[:8], acc[8:24], acc[24:32]
    node = picked[0:1].astype(jnp.int32)
    row = iota((FAB, LANES), 0)
    spread = jnp.where(row < parts, picked[1:2], jnp.where(row < 2 * parts, picked[2:3], picked[3:4]))
    spread = jnp.where((row < 3 * parts) & (row % parts == (node >> 7)), spread, 0.0)
    at_node = one_hot(iota((LANES, LANES), 0) == (node & (LANES - 1)))
    fluid = sum3(dot_nt(stacked3(spread), at_node))
    my_live = mine[0:1] >= 0.0
    moved = []
    for a in range(3):
        for k in range(parts):
            r = a * parts + k
            new = mine[4 + r : 5 + r] + fluid[r : r + 1]
            at = slice(k * LANES, (k + 1) * LANES)
            vel_out_ref[a, :, at] = new
            pos_out_ref[a, :, at] = pos_ref[a, :, at] + new
        base = jnp.sum(found[4 + a * parts : 4 + (a + 1) * parts], axis=0, keepdims=True)
        moved.append(jnp.where(my_live, base + pushed[1 + a : 2 + a], 0.0))
    moved = jnp.concatenate(moved + [jnp.zeros((5, LANES), jnp.float32)], axis=0)
    for o in range(owners):
        turned = pltpu.roll(moved, LANES - o * capacity, 1) if o else moved
        for a in range(3):
            wall_out_ref[0, 0, 0, a, o : o + 1] = turned[a : a + 1, :capacity]
    for k, (src, dst) in enumerate(((vel_out_ref, vel_hbm), (pos_out_ref, pos_hbm), (wall_out_ref, wall_hbm))):
        copies.append(pltpu.make_async_copy(src, dst, sems.at[size_x + k]))
        copies[-1].start()
    for copy in copies:
        copy.wait()


def ring(count, step):
    return [(i, (i + step) % count) for i in range(count)]


def body(
    populations,
    solid,
    link_cell,
    link_dir,
    link_node,
    link_velocity,
    fabric_position,
    fabric_velocity,
    fabric_rest,
    triangles,
):
    size_x, size_y, size_z = populations.shape[1:]
    owners, capacity = link_node.shape[3:]
    nodes = fabric_position.shape[2]
    count_x, count_y, count_z = (lax.axis_size(name) for name in ("gx", "gy", "gz"))
    folded = (
        (count_y, count_z) == (4, 2)
        and (size_y, size_z) == (8, LANES)
        and owners * capacity == LANES
        and nodes == 4 * LANES
    )
    if not folded:
        return general_body(
            populations, solid, link_cell, link_dir, link_node, link_velocity,
            fabric_position, fabric_velocity, fabric_rest, triangles,
        )
    f32 = jnp.float32
    on_chip = pl.BlockSpec(memory_space=pltpu.VMEM)

    def shape(*dims):
        return jax.ShapeDtypeStruct(dims, f32)

    def kept(*dims):
        return pltpu.VMEM(dims, f32)

    def run(kernel, outs, *args):
        args = [pltpu.with_memory_space_constraint(arg, pltpu.VMEM) for arg in args]
        return pl.pallas_call(
            kernel,
            out_shape=outs,
            in_specs=[on_chip] * len(args),
            out_specs=jax.tree.map(lambda _: on_chip, outs),
            name=kernel.__name__,
        )(*args)

    face_x = kept(5, size_y, size_z)
    map_shape = kept(size_x, size_y, size_z)
    given = (
        populations, solid, link_cell, link_dir, link_node, link_velocity,
        fabric_position, fabric_velocity, fabric_rest, triangles,
    )
    opened = (kept(*populations.shape), face_x, face_x, kept(WIDE, LANES), map_shape, map_shape)
    post, up, down, fab, kind, back = pl.pallas_call(
        open_kernel,
        out_shape=opened,
        in_specs=[pl.BlockSpec(memory_space=pl.ANY)] * len(given),
        out_specs=(on_chip,) * len(opened),
        scratch_shapes=[pltpu.VMEM(arg.shape, arg.dtype) for arg in given] + [pltpu.SemaphoreType.DMA((len(given),))],
        name="open_kernel",
    )(*given)
    swap_z = [(0, 1), (1, 0)]
    beside = lax.ppermute(fab, "gz", swap_z)
    xlow = lax.ppermute(up, "gx", ring(count_x, 1))
    xhigh = lax.ppermute(down, "gx", ring(count_x, -1))
    (pair,) = run(pair_kernel, (kept(2 * FAB, LANES),), fab, beside)
    crossing, middling = [], []
    for y in range(count_y):
        to = y + 1 if y % 2 else y - 1
        for z in range(count_z):
            crossing.append((y * 2 + z, (y ^ (1 + z)) * 2 + z))
            middling.append((y * 2 + z, to * 2 + z if 0 <= to < count_y else y * 2 + 1 - z))
    cross = lax.ppermute(pair, ("gy", "gz"), crossing)
    rows = -(-5 * size_x // 8) * 8
    (middle,) = run(middle_kernel, (kept(3 * rows, LANES),), post, xlow, xhigh)
    (near,) = run(near_kernel, (kept(2 * FAB + rows, LANES),), post, xlow, xhigh, cross, middle)
    middle = lax.ppermute(middle, ("gy", "gz"), middling)
    near = lax.ppermute(near, "gy", [(y, y ^ 1) for y in range(count_y)])
    rolled, swap = run(
        shift_kernel, (kept(*populations.shape), kept(4 * FAB + size_x * size_y, LANES)),
        post, xlow, xhigh, cross, near, middle,
    )
    other = lax.ppermute(swap, "gz", swap_z)
    (acc,) = run(half_kernel, (kept(32, LANES),), fab, pair, cross)
    outs = (
        shape(*populations.shape),
        shape(*fabric_position.shape),
        shape(*fabric_velocity.shape),
        shape(*link_velocity.shape),
    )
    last = [rolled, kind, back, fab, acc, near, other, fabric_position]
    last = [pltpu.with_memory_space_constraint(arg, pltpu.VMEM) for arg in last]
    return pl.pallas_call(
        final_kernel,
        out_shape=outs,
        in_specs=[on_chip] * len(last),
        out_specs=(pl.BlockSpec(memory_space=pl.ANY),) * 4,
        scratch_shapes=[pltpu.VMEM(out.shape, f32) for out in outs] + [pltpu.SemaphoreType.DMA((size_x + 3,))],
        name="final_kernel",
    )(*last)


def solution(mesh):
    placed = (
        P(None, "gx", "gy", "gz"),
        P("gx", "gy", "gz"),
        P("gx", "gy", "gz", None, None),
        P("gx", "gy", "gz", None, None),
        P("gx", "gy", "gz", None, None),
        P("gx", "gy", "gz", None, None, None),
        P(None, "gx", ("gy", "gz")),
        P(None, "gx", ("gy", "gz")),
        P(None, "gx", ("gy", "gz")),
        P(None, "gx", ("gy", "gz")),
    )
    return jax.shard_map(
        body,
        mesh=mesh,
        in_specs=placed,
        out_specs=(
            P(None, "gx", "gy", "gz"),
            P(None, "gx", ("gy", "gz")),
            P(None, "gx", ("gy", "gz")),
            P("gx", "gy", "gz", None, None, None),
        ),
        check_vma=False,
    )
```

```python
import jax
import jax.numpy as jnp
import numpy as np
from jax import lax
from jax.experimental import pallas as pl
from jax.experimental.pallas import tpu as pltpu
from jax.sharding import PartitionSpec as P

SPRING = 0.5
DAMPING = 0.1
DIRECTIONS = [
    [0, 0, 0],
    [1, 0, 0],
    [-1, 0, 0],
    [0, 1, 0],
    [0, -1, 0],
    [0, 0, 1],
    [0, 0, -1],
    [1, 1, 0],
    [-1, -1, 0],
    [1, -1, 0],
    [-1, 1, 0],
    [1, 0, 1],
    [-1, 0, -1],
    [1, 0, -1],
    [-1, 0, 1],
    [0, 1, 1],
    [0, -1, -1],
    [0, 1, -1],
    [0, -1, 1],
]


def extended(cells, sides, width):
    for axis, dim in sides:
        count = lax.axis_size(axis)
        head = lax.slice_in_dim(cells, 0, width, axis=dim)
        tail = lax.slice_in_dim(cells, cells.shape[dim] - width, cells.shape[dim], axis=dim)
        cells = jnp.concatenate(
            [
                lax.ppermute(tail, axis, [(i, (i + 1) % count) for i in range(count)]),
                cells,
                lax.ppermute(head, axis, [((i + 1) % count, i) for i in range(count)]),
            ],
            axis=dim,
        )
    return cells


def lattice():
    velocity_np = np.array(DIRECTIONS)
    weight_np = np.array([1.0 / 3.0] + [1.0 / 18.0] * 6 + [1.0 / 36.0] * 12)
    opposite_list = [
        DIRECTIONS.index([-entry for entry in DIRECTIONS[direction]]) for direction in range(19)
    ]
    along_a = np.array([float(entry[0]) for entry in DIRECTIONS])
    along_b = np.array([float(entry[1]) for entry in DIRECTIONS])
    along_e = np.array([float(entry[2]) for entry in DIRECTIONS])
    speed_sq = along_a * along_a + along_b * along_b + along_e * along_e
    moment_rows = [
        np.ones(19),
        19 * speed_sq - 30,
        (21 * speed_sq * speed_sq - 53 * speed_sq + 24) / 2,
        along_a,
        (5 * speed_sq - 9) * along_a,
        along_b,
        (5 * speed_sq - 9) * along_b,
        along_e,
        (5 * speed_sq - 9) * along_e,
        3 * along_a * along_a - speed_sq,
        (3 * speed_sq - 5) * (3 * along_a * along_a - speed_sq),
        along_b * along_b - along_e * along_e,
        (3 * speed_sq - 5) * (along_b * along_b - along_e * along_e),
        along_a * along_b,
        along_b * along_e,
        along_a * along_e,
        (along_b * along_b - along_e * along_e) * along_a,
        (along_e * along_e - along_a * along_a) * along_b,
        (along_a * along_a - along_b * along_b) * along_e,
    ]
    moment_np = np.stack(moment_rows)
    inverse_np = moment_np.T / np.sum(moment_np * moment_np, axis=1)[None, :]
    viscous = 5.0 / 3.0
    rates_np = np.array(
        [
            0.0,
            1.19,
            1.4,
            0.0,
            1.2,
            0.0,
            1.2,
            0.0,
            1.2,
            viscous,
            1.4,
            viscous,
            1.4,
            viscous,
            viscous,
            viscous,
            1.98,
            1.98,
            1.98,
        ]
    )
    return (velocity_np, weight_np, opposite_list, moment_np, inverse_np, rates_np)


def collide_cells(popul, solid_flat):
    velocity_np, weight_np, opposite_list, moment_np, inverse_np, rates_np = lattice()
    velocity_table = jnp.asarray(velocity_np, jnp.float32)
    weight_table = jnp.asarray(weight_np, jnp.float32)
    density = jnp.sum(popul, axis=0)
    momentum = jnp.dot(
        velocity_table.T, popul, precision=lax.Precision.HIGHEST, preferred_element_type=jnp.float32
    )
    flow = momentum / density
    projected = jnp.dot(
        velocity_table, flow, precision=lax.Precision.HIGHEST, preferred_element_type=jnp.float32
    )
    speed_sq = jnp.sum(flow * flow, axis=0)
    equilibrium = (
        weight_table[:, None]
        * density
        * (1.0 + 3.0 * projected + 4.5 * projected * projected - 1.5 * speed_sq)
    )
    offset = popul - equilibrium
    moments = jnp.dot(
        jnp.asarray(moment_np, jnp.float32),
        offset,
        precision=lax.Precision.HIGHEST,
        preferred_element_type=jnp.float32,
    )
    relaxed = jnp.asarray(rates_np, jnp.float32)[:, None] * moments
    change = jnp.dot(
        jnp.asarray(inverse_np, jnp.float32),
        relaxed,
        precision=lax.Precision.HIGHEST,
        preferred_element_type=jnp.float32,
    )
    return jnp.where(solid_flat[None, :] == 1, popul, popul - change)


def fill_outside(padded, weight_np):
    span_y = padded.shape[2]
    span_z = padded.shape[3]
    place_y = lax.axis_index("gy")
    place_z = lax.axis_index("gz")
    count_y = lax.axis_size("gy")
    count_z = lax.axis_size("gz")
    rows_y = jnp.arange(span_y)
    rows_z = jnp.arange(span_z)
    out_y = (rows_y == 0) & (place_y == 0) | (rows_y == span_y - 1) & (place_y == count_y - 1)
    out_z = (rows_z == 0) & (place_z == 0) | (rows_z == span_z - 1) & (place_z == count_z - 1)
    outside = out_y[:, None] | out_z[None, :]
    return jnp.where(
        outside[None, None], jnp.asarray(weight_np, jnp.float32)[:, None, None, None], padded
    )


def propagate(padded, size_x, size_y, size_z):
    pieces = []
    for direction in range(19):
        shift_x = DIRECTIONS[direction][0]
        shift_y = DIRECTIONS[direction][1]
        shift_z = DIRECTIONS[direction][2]
        plane = padded[direction]
        pieces.append(
            lax.slice(
                plane,
                (1 - shift_x, 1 - shift_y, 1 - shift_z),
                (1 - shift_x + size_x, 1 - shift_y + size_y, 1 - shift_z + size_z),
            )
        )
    return jnp.stack(pieces)


def membrane(positions, rest, triangle_nodes):
    force = jnp.zeros(positions.shape, jnp.float32)
    for first, second in ((0, 1), (1, 2), (2, 0)):
        head = triangle_nodes[first]
        tail = triangle_nodes[second]
        stretch = positions[:, tail] - positions[:, head] - (rest[:, tail] - rest[:, head])
        force = force.at[:, head].add(SPRING * stretch)
        force = force.at[:, tail].add(-SPRING * stretch)
    return force


def general_body(
    populations,
    solid,
    link_cell,
    link_dir,
    link_node,
    link_velocity,
    fabric_position,
    fabric_velocity,
    fabric_rest,
    triangles,
):
    velocity_np, weight_np, opposite_list, moment_np, inverse_np, rates_np = lattice()
    velocity_table = jnp.asarray(velocity_np, jnp.float32)
    weight_table = jnp.asarray(weight_np, jnp.float32)
    opposite_table = jnp.asarray(opposite_list, jnp.int32)
    size_x = populations.shape[1]
    size_y = populations.shape[2]
    size_z = populations.shape[3]
    cells = size_x * size_y * size_z
    post = collide_cells(populations.reshape(19, cells), solid.reshape(cells)).reshape(
        populations.shape
    )
    padded = extended(post, (("gx", 1), ("gy", 2), ("gz", 3)), 1)
    padded = fill_outside(padded, weight_np)
    propagated = propagate(padded, size_x, size_y, size_z).reshape(19, cells)
    owners_n = link_node.shape[3]
    capacity = link_node.shape[4]
    node_rows = link_node.reshape(owners_n, capacity)
    cell_rows = link_cell.reshape(owners_n, capacity)
    dir_rows = link_dir.reshape(owners_n, capacity)
    live = node_rows >= 0
    post_flat = post.reshape(19, cells)
    reflected = post_flat[opposite_table[dir_rows], cell_rows]
    link_unit = velocity_table[dir_rows]
    wall = jnp.moveaxis(link_velocity.reshape(3, owners_n, capacity), 0, -1)
    returned = reflected + 6.0 * weight_table[dir_rows] * jnp.sum(link_unit * wall, axis=-1)
    populations_next = propagated.at[jnp.where(live, dir_rows, 19), cell_rows].set(
        returned, mode="drop"
    )
    strength = reflected + returned
    positions = fabric_position.reshape(3, -1)
    velocities = fabric_velocity.reshape(3, -1)
    rest = fabric_rest.reshape(3, -1)
    nodes_n = positions.shape[1]
    elastic = membrane(positions, rest, triangles.reshape(3, -1))
    link_force = jnp.moveaxis(-link_unit * strength[..., None], -1, 0)
    got_nodes, got_force = (
        lax.all_to_all(node_rows[None], ("gy", "gz"), split_axis=1, concat_axis=1, tiled=True),
        lax.all_to_all(link_force, ("gy", "gz"), split_axis=1, concat_axis=1, tiled=True),
    )
    got_ids = got_nodes[0]
    got_live = got_ids >= 0
    target = jnp.where(got_live, got_ids, nodes_n).reshape(-1)
    fluid_force = (
        jnp.zeros((3, nodes_n), jnp.float32)
        .at[:, target]
        .add(got_force.reshape(3, -1), mode="drop")
    )
    velocity_next = (1.0 - DAMPING) * velocities + (fluid_force + elastic)
    position_next = positions + velocity_next
    reply = jnp.where(got_live[None], velocity_next[:, jnp.where(got_live, got_ids, 0)], 0.0)
    wall_next = lax.all_to_all(reply, ("gy", "gz"), split_axis=1, concat_axis=1, tiled=True)
    return (
        populations_next.reshape(populations.shape),
        position_next.reshape(fabric_position.shape),
        velocity_next.reshape(fabric_velocity.shape),
        wall_next.reshape(link_velocity.shape),
    )


WEIGHTS = [1.0 / 3.0] + [1.0 / 18.0] * 6 + [1.0 / 36.0] * 12
OPPOSITE = [DIRECTIONS.index([-entry for entry in d]) for d in DIRECTIONS]
SIDES = [
    ([i for i in range(19) if DIRECTIONS[i][a] == 1], [i for i in range(19) if DIRECTIONS[i][a] == -1])
    for a in range(3)
]
LANES = 128
PATCH = 256
FAB = 16
SEED = 80


def iota(shape, axis):
    return lax.broadcasted_iota(jnp.int32, shape, axis)


def split3(value):
    high = value.astype(jnp.bfloat16).astype(jnp.float32)
    rest = value - high
    middle = rest.astype(jnp.bfloat16).astype(jnp.float32)
    return high, middle, rest - middle


def stacked3(value):
    return jnp.concatenate(split3(value), axis=0).astype(jnp.bfloat16)


def sum3(value):
    rows = value.shape[0] // 3
    return value[:rows] + value[rows : 2 * rows] + value[2 * rows :]


def dot_nn(left, right):
    return lax.dot_general(left, right, (((1,), (0,)), ((), ())), preferred_element_type=jnp.float32)


def dot_nt(left, right):
    return lax.dot_general(left, right, (((1,), (1,)), ((), ())), preferred_element_type=jnp.float32)


def one_hot(mask):
    return jnp.where(mask, 1.0, 0.0).astype(jnp.bfloat16)


def collided(f, solid):
    sx, dx = f[1] + f[2], f[1] - f[2]
    sy, dy = f[3] + f[4], f[3] - f[4]
    sz, dz = f[5] + f[6], f[5] - f[6]
    sa, da = f[7] + f[8], f[7] - f[8]
    sb, db = f[9] + f[10], f[9] - f[10]
    sc, dc = f[11] + f[12], f[11] - f[12]
    sd, dd = f[13] + f[14], f[13] - f[14]
    se, de = f[15] + f[16], f[15] - f[16]
    sg, dg = f[17] + f[18], f[17] - f[18]
    sxy, txy = sa + sb, sa - sb
    sxz, txz = sc + sd, sc - sd
    syz, tyz = se + sg, se - sg
    ax_ab, ay_ab = da + db, da - db
    ax_cd, az_cd = dc + dd, dc - dd
    ay_eg, az_eg = de + dg, de - dg
    near, far = sx + sy + sz, sxy + sxz + syz
    rho = f[0] + near + far
    ex, ey, ez = ax_ab + ax_cd, ay_ab + ay_eg, az_cd + az_eg
    jx, jy, jz = dx + ex, dy + ey, dz + ez
    inv = 1.0 / rho
    ux, uy, uz = jx * inv, jy * inv, jz * inv
    xx, yy, zz = jx * ux, jy * uy, jz * uz
    jj = xx + yy + zz
    energy = (-30.0 * f[0] - 11.0 * near + 8.0 * far) - (-11.0 * rho + 19.0 * jj)
    square = (12.0 * f[0] - 4.0 * near + far) - (3.0 * rho - 5.5 * jj)
    kx = (1.2 / 40.0) * (ex - 4.0 * dx + (2.0 / 3.0) * jx)
    ky = (1.2 / 40.0) * (ey - 4.0 * dy + (2.0 / 3.0) * jy)
    kz = (1.2 / 40.0) * (ez - 4.0 * dz + (2.0 / 3.0) * jz)
    yz_near, xyz_far = sy + sz, sxy + sxz - 2.0 * syz
    pxx_eq = 2.0 * xx - yy - zz
    pww_eq = yy - zz
    pxx = (5.0 / 3.0 / 36.0) * (2.0 * sx - yz_near + xyz_far - pxx_eq)
    pixx = (1.4 / 72.0) * (-4.0 * sx + 2.0 * yz_near + xyz_far + 0.5 * pxx_eq)
    w_near, w_far = sy - sz, sxy - sxz
    pww = (5.0 / 3.0 / 12.0) * (w_near + w_far - pww_eq)
    piww = (1.4 / 24.0) * (w_far - 2.0 * w_near + 0.5 * pww_eq)
    pxy = (5.0 / 3.0 / 4.0) * (txy - jx * uy)
    pyz = (5.0 / 3.0 / 4.0) * (tyz - jy * uz)
    pxz = (5.0 / 3.0 / 4.0) * (txz - jx * uz)
    mx = (1.98 / 8.0) * (ax_ab - ax_cd)
    my = (1.98 / 8.0) * (ay_eg - ay_ab)
    mz = (1.98 / 8.0) * (az_cd - az_eg)
    energy = (1.19 / 2394.0) * energy
    square = (1.4 / 252.0) * square
    axis = -11.0 * energy - 4.0 * square
    across = pxx - 2.0 * pixx
    split = pww - 2.0 * piww
    edge = 8.0 * energy + square
    pp, ww = pxx + pixx, pww + piww
    even = [
        axis + 2.0 * across,
        axis - across + split,
        axis - across - split,
        edge + pp + ww + pxy,
        edge + pp + ww - pxy,
        edge + pp - ww + pxz,
        edge + pp - ww - pxz,
        edge - 2.0 * pp + pyz,
        edge - 2.0 * pp - pyz,
    ]
    odd = [
        -4.0 * kx,
        -4.0 * ky,
        -4.0 * kz,
        (kx + mx) + (ky - my),
        (kx + mx) - (ky - my),
        (kx - mx) + (kz + mz),
        (kx - mx) - (kz + mz),
        (ky + my) + (kz - mz),
        (ky + my) - (kz - mz),
    ]
    change = [12.0 * square - 30.0 * energy]
    for pair in range(9):
        change += [even[pair] + odd[pair], even[pair] - odd[pair]]
    fluid = solid != 1
    return [jnp.where(fluid, f[i] - change[i], f[i]) for i in range(19)]


def slots_to_row(value):
    owners, capacity = value.shape
    wide = jnp.concatenate([value, jnp.zeros((owners, LANES - capacity), value.dtype)], axis=1)
    return jnp.sum(pltpu.roll(wide, 0, 1, stride=capacity, stride_axis=0), axis=0, keepdims=True)


def membrane_base(pos_ref, vel_ref, rest_ref, tri_ref, fab_ref):
    nodes = pos_ref.shape[2]
    count = tri_ref.shape[2]
    wide = -(-count // LANES) * LANES
    patches = nodes // PATCH
    stretch = [pos_ref[a] - rest_ref[a] for a in range(3)]
    corners = [
        jnp.concatenate([tri_ref[t], jnp.full((1, wide - count), -1, jnp.int32)], axis=1) for t in range(3)
    ]
    patch = jnp.maximum(corners[0], 0) // PATCH
    local = [(corner - patch * PATCH).astype(jnp.float32) for corner in corners]
    node_ids = iota((PATCH, LANES), 0).astype(jnp.float32).astype(jnp.bfloat16)
    blocks = []
    for k in range(0, wide, LANES):
        block = jnp.zeros((PATCH, LANES), jnp.bfloat16)
        for corner in local:
            row = jnp.broadcast_to(corner[:, k : k + LANES], (16, LANES)).astype(jnp.bfloat16)
            row = jnp.concatenate([row] * (PATCH // 16), axis=0)
            block = block + jnp.where(node_ids == row, jnp.ones_like(block), jnp.zeros_like(block))
        blocks.append(block)
    hits = jnp.concatenate(blocks, axis=1)
    stretch8 = jnp.concatenate(stretch + [jnp.zeros((5, nodes), jnp.float32)], axis=0)
    pieces = [stacked3(stretch8[:, p * PATCH : (p + 1) * PATCH]) for p in range(patches)]
    sums = dot_nn(jnp.concatenate(pieces, axis=0), hits)
    total = jnp.zeros((8, wide), jnp.float32)
    for p in range(patches):
        total = jnp.where(patch == p, sum3(sums[p * 24 : (p + 1) * 24]), total)
    total = jnp.where(iota(total.shape, 0) == 3, 1.0, total)
    pieces = [stacked3(jnp.where(patch == p, total, 0.0)) for p in range(patches)]
    sums = dot_nt(jnp.concatenate(pieces, axis=0), hits)
    back = jnp.concatenate([sum3(sums[p * 24 : (p + 1) * 24]) for p in range(patches)], axis=1)
    for a in range(3):
        elastic = SPRING * back[a : a + 1] - 3.0 * SPRING * back[3:4] * stretch[a]
        base = (1.0 - DAMPING) * vel_ref[a] + elastic
        for k in range(nodes // LANES):
            row = 4 + a * (nodes // LANES) + k
            fab_ref[row : row + 1] = base[:, k * LANES : (k + 1) * LANES]


def z_face(tiles):
    up = jnp.zeros_like(next(t for t in tiles if t is not None))
    lane = iota(up.shape, 1)
    down = up
    for k in range(5):
        i, j = SIDES[2][0][k], SIDES[2][1][k]
        if tiles[i] is not None:
            up = jnp.where(lane == k, pltpu.roll(tiles[i], k + 1, 1), up)
        if tiles[j] is not None:
            down = jnp.where(lane == k, pltpu.roll(tiles[j], k, 1) if k else tiles[j], down)
    return jnp.where(lax.axis_index("gz") == 0, up, down)


def z_shift(tile, i, face):
    lane = iota(tile.shape, 1)
    low_end = lax.axis_index("gz") == 0
    if DIRECTIONS[i][2] == 1:
        k = SIDES[2][0].index(i)
        halo = pltpu.roll(face, LANES - k, 1) if k else face
        return jnp.where(lane == 0, jnp.where(low_end, WEIGHTS[i], halo), pltpu.roll(tile, 1, 1))
    if DIRECTIONS[i][2] == -1:
        k = SIDES[2][1].index(i)
        halo = pltpu.roll(face, LANES - 1 - k, 1)
        return jnp.where(lane == LANES - 1, jnp.where(low_end, halo, WEIGHTS[i]), pltpu.roll(tile, LANES - 1, 1))
    return tile


def open_kernel(
    pop_hbm, solid_hbm, cell_hbm, dir_hbm, node_hbm, wall_hbm, pos_hbm, vel_hbm, rest_hbm, tri_hbm,
    post_ref, up_ref, down_ref, seed_ref, kind_ref, back_ref, pos_ref,
    pop_ref, solid_ref, cell_ref, dir_ref, node_ref, wall_ref, vel_ref, rest_ref, tri_ref, sems,
):
    moves = [
        (pop_hbm, pop_ref), (solid_hbm, solid_ref),
        (tri_hbm, tri_ref), (pos_hbm, pos_ref), (rest_hbm, rest_ref), (vel_hbm, vel_ref),
        (cell_hbm, cell_ref), (dir_hbm, dir_ref), (node_hbm, node_ref), (wall_hbm, wall_ref),
    ]
    copies = [pltpu.make_async_copy(src, dst, sems.at[k]) for k, (src, dst) in enumerate(moves)]
    for copy in copies[2:] + copies[:2]:
        copy.start()
    for copy in copies[2:]:
        copy.wait()
    membrane_base(pos_ref, vel_ref, rest_ref, tri_ref, seed_ref)
    size_x, size_y = post_ref.shape[1:3]
    rows = size_x * size_y
    cell = slots_to_row(cell_ref[0, 0, 0].astype(jnp.float32)).astype(jnp.int32)
    way = slots_to_row(dir_ref[0, 0, 0].astype(jnp.float32))
    node = slots_to_row(node_ref[0, 0, 0].astype(jnp.float32))
    live = node >= 0.0
    unit = []
    for a in range(3):
        u = jnp.zeros_like(way)
        for i in range(1, 19):
            if DIRECTIONS[i][a]:
                u = jnp.where(way == float(i), float(DIRECTIONS[i][a]), u)
        unit.append(u)
    weight = jnp.where(way >= 7.0, 6.0 / 36.0, 6.0 / 18.0)
    wall = [slots_to_row(wall_ref[0, 0, 0, a]) for a in range(3)]
    term = weight * (unit[0] * wall[0] + unit[1] * wall[1] + unit[2] * wall[2])
    at_row = jnp.where((iota((rows, LANES), 0) == (cell >> 7)) & live, 1.0, 0.0)
    at_lane = one_hot(iota((LANES, LANES), 0) == (cell & (LANES - 1)))
    left = jnp.concatenate([at_row * way] + [at_row * t for t in split3(term)], axis=0)
    maps = dot_nt(left.astype(jnp.bfloat16), at_lane)
    kind = maps[:rows]
    added = sum3(maps[rows:])
    for copy in copies[:2]:
        copy.wait()
    taken = []
    for x in range(size_x):
        post = collided([pop_ref[i, x] for i in range(19)], solid_ref[x])
        k = kind[x * size_y : (x + 1) * size_y]
        t = jnp.zeros_like(k)
        for i in range(19):
            post_ref[i, x] = post[i]
            if x == size_x - 1 and i in SIDES[0][0]:
                up_ref[SIDES[0][0].index(i)] = post[i]
            if x == 0 and i in SIDES[0][1]:
                down_ref[SIDES[0][1].index(i)] = post[i]
            if i:
                t = jnp.where(k == float(OPPOSITE[i]), post[i], t)
        seed_ref[FAB + x * size_y : FAB + (x + 1) * size_y] = z_face(post)
        taken.append(t)
        kind_ref[x] = k
        back_ref[x] = t + added[x * size_y : (x + 1) * size_y]
    strength = 2.0 * jnp.concatenate(taken, axis=0) + added
    at_link = sum3(dot_nn(stacked3(strength), at_lane))
    push = jnp.sum(at_row * at_link, axis=0, keepdims=True)
    seed_ref[0:1] = node
    for a in range(3):
        seed_ref[1 + a : 2 + a] = -unit[a] * push
    end = FAB + rows
    seed_ref[end:] = jnp.zeros((seed_ref.shape[0] - end, LANES), jnp.float32)


def source_tile(post_ref, low_ref, high_ref, i, x):
    size_x = post_ref.shape[1]
    from_x = x - DIRECTIONS[i][0]
    if from_x < 0:
        return low_ref.at[SIDES[0][0].index(i)]
    if from_x >= size_x:
        return high_ref.at[SIDES[0][1].index(i)]
    return post_ref.at[i, from_x]


def pair_kernel(seed_ref, other_ref, pair_ref):
    low = lax.axis_index("gz") == 0
    pair_ref[:FAB] = jnp.where(low, seed_ref[:FAB], other_ref[:FAB])
    pair_ref[FAB:] = jnp.where(low, other_ref[:FAB], seed_ref[:FAB])


def edge_kernel(low_ref, high_ref, edge_ref):
    tiles = [None] * 19
    for i in range(19):
        if DIRECTIONS[i][0] and DIRECTIONS[i][2]:
            side = 0 if DIRECTIONS[i][0] == 1 else 1
            tiles[i] = (low_ref, high_ref)[side][SIDES[0][side].index(i)]
    edge_ref[...] = z_face(tiles)


def face_rows(post_ref, low_ref, high_ref, other_ref, out_ref, start, upward):
    size_x, size_y = post_ref.shape[1:3]
    for k in range(5):
        for x in range(size_x):
            at = start + k * size_x + x
            face = other_ref[FAB + x * size_y : FAB + (x + 1) * size_y]
            rows = []
            for side, row in ((0, size_y - 1), (1, 0)):
                i = SIDES[1][side][k]
                source = source_tile(post_ref, low_ref, high_ref, i, x)
                if DIRECTIONS[i][2]:
                    rows.append(z_shift(source[...], i, face)[row : row + 1])
                else:
                    rows.append(source[row : row + 1])
            out_ref[at : at + 1] = jnp.where(upward, rows[0], rows[1])
    end = start + 5 * size_x
    if out_ref.shape[0] > end:
        out_ref[end:] = jnp.zeros((out_ref.shape[0] - end, LANES), jnp.float32)


def middle_kernel(post_ref, low_ref, high_ref, other_ref, middle_ref):
    odd = lax.rem(lax.axis_index("gy"), 2) == 1
    face_rows(post_ref, low_ref, high_ref, other_ref, middle_ref, 0, odd)


def near_kernel(post_ref, low_ref, high_ref, other_ref, pair_ref, cross_ref, near_ref):
    odd = lax.rem(lax.axis_index("gy"), 2) == 1
    near_ref[: 2 * FAB] = pair_ref[...]
    near_ref[2 * FAB : 4 * FAB] = cross_ref[...]
    face_rows(post_ref, low_ref, high_ref, other_ref, near_ref, 4 * FAB, jnp.logical_not(odd))


def shift_kernel(post_ref, low_ref, high_ref, other_ref, edge_ref, rolled_ref):
    size_x, size_y = post_ref.shape[1:3]
    for i in range(19):
        for x in range(size_x):
            tile = source_tile(post_ref, low_ref, high_ref, i, x)[...]
            from_x = x - DIRECTIONS[i][0]
            if 0 <= from_x < size_x:
                face = other_ref[FAB + from_x * size_y : FAB + (from_x + 1) * size_y]
            else:
                face = edge_ref[...]
            tile = z_shift(tile, i, face)
            if DIRECTIONS[i][1]:
                tile = pltpu.roll(tile, DIRECTIONS[i][1] % size_y, 0)
            rolled_ref[i, x] = tile


def fabric_part(pairs, chips, start, mine, nodes, capacity):
    parts = nodes // LANES
    place_z = lax.axis_index("gz")
    me = lax.axis_index("gy") * 2 + place_z
    slot_owner = iota((1, LANES), 1) // capacity
    owner_base = (slot_owner * nodes).astype(jnp.float32)
    my_node = mine[0:1]
    my_id = jnp.where(my_node >= 0.0, owner_base + my_node, -2.0)
    my_column = jnp.transpose(jnp.broadcast_to(my_id, (LANES, LANES)))
    matches, forces, picked = [], [], jnp.zeros((8, LANES), jnp.float32)
    for m in range(2 * len(pairs)):
        tile = pairs[m // 2][m % 2 * FAB : m % 2 * FAB + 8]
        ids = tile[0:1]
        ids = jnp.where(ids >= 0.0, owner_base + ids, -1.0)
        matches.append(one_hot(my_column == ids))
        forces.append(tile)
        shift = lax.rem((start + m + LANES // capacity - me) * capacity, LANES)
        picked = jnp.where(slot_owner == start + m, pltpu.roll(tile, shift, 1), picked)
    pushed = sum3(dot_nt(stacked3(jnp.concatenate(forces, axis=1)), jnp.concatenate(matches, axis=1)))

    my_int = my_node.astype(jnp.int32)
    at_lane = one_hot(iota((LANES, LANES), 0) == (my_int & (LANES - 1)))
    found = sum3(dot_nn(stacked3(jnp.concatenate(pairs, axis=0)), at_lane))
    row = iota((FAB, LANES), 0)
    fits = (row >= 4) & (row % parts == (my_int >> 7))
    base = jnp.zeros((FAB, LANES), jnp.float32)
    for m in range(2 * len(pairs)):
        owner = chips[m // 2] * 2 + m % 2
        base = jnp.where(fits & (slot_owner == owner), found[m * FAB : (m + 1) * FAB], base)
    return jnp.concatenate([pushed, base, picked], axis=0)


def half_kernel(seed_ref, pair_ref, cross_ref, acc_ref):
    place_y = lax.axis_index("gy")
    nodes, capacity = 4 * LANES, LANES // 8
    pairs, chips = [pair_ref[...], cross_ref[...]], [place_y, place_y ^ 2]
    acc_ref[...] = fabric_part(pairs, chips, 0, seed_ref[:FAB], nodes, capacity)


def final_kernel(
    rolled_ref, kind_ref, back_ref, seed_ref, acc_ref, near_ref, middle_ref, pos_ref,
    pop_hbm, pos_hbm, vel_hbm, wall_hbm,
    pop_ref, pos_out_ref, vel_out_ref, wall_out_ref, sems,
):
    size_x, size_y = rolled_ref.shape[1:3]
    place_y = lax.axis_index("gy")
    odd = lax.rem(place_y, 2) == 1
    first, top = place_y == 0, place_y == lax.axis_size("gy") - 1
    sub = iota((size_y, LANES), 0)
    copies = []
    for x in range(size_x):
        kind = kind_ref[x]
        back = back_ref[x]
        for i in range(19):
            tile = rolled_ref[i, x]
            if DIRECTIONS[i][1]:
                side = 0 if DIRECTIONS[i][1] == 1 else 1
                at = SIDES[1][side].index(i) * size_x + x
                by_near = near_ref[4 * FAB + at : 4 * FAB + at + 1]
                by_middle = middle_ref[at : at + 1]
                if side == 0:
                    row = jnp.where(first, WEIGHTS[i], jnp.where(odd, by_near, by_middle))
                    tile = jnp.where(sub == 0, row, tile)
                else:
                    row = jnp.where(top, WEIGHTS[i], jnp.where(odd, by_middle, by_near))
                    tile = jnp.where(sub == size_y - 1, row, tile)
            if i:
                tile = jnp.where(kind == float(i), back, tile)
            pop_ref[i, x] = tile
        copies.append(pltpu.make_async_copy(pop_ref.at[:, x], pop_hbm.at[:, x], sems.at[x]))
        copies[-1].start()

    owners, capacity = wall_out_ref.shape[4], wall_out_ref.shape[5]
    nodes = pos_ref.shape[2]
    parts = nodes // LANES
    mine = seed_ref[:FAB]
    pairs, chips = [near_ref[: 2 * FAB], near_ref[2 * FAB : 4 * FAB]], [place_y ^ 1, place_y ^ 3]
    acc = fabric_part(pairs, chips, 4, mine, nodes, capacity) + acc_ref[...]
    pushed, found, picked = acc[:8], acc[8:24], acc[24:32]
    node = picked[0:1].astype(jnp.int32)
    row = iota((FAB, LANES), 0)
    spread = jnp.where(row < parts, picked[1:2], jnp.where(row < 2 * parts, picked[2:3], picked[3:4]))
    spread = jnp.where((row < 3 * parts) & (row % parts == (node >> 7)), spread, 0.0)
    at_node = one_hot(iota((LANES, LANES), 0) == (node & (LANES - 1)))
    fluid = sum3(dot_nt(stacked3(spread), at_node))
    my_live = mine[0:1] >= 0.0
    moved = []
    for a in range(3):
        for k in range(parts):
            r = a * parts + k
            new = mine[4 + r : 5 + r] + fluid[r : r + 1]
            at = slice(k * LANES, (k + 1) * LANES)
            vel_out_ref[a, :, at] = new
            pos_out_ref[a, :, at] = pos_ref[a, :, at] + new
        base = jnp.sum(found[4 + a * parts : 4 + (a + 1) * parts], axis=0, keepdims=True)
        moved.append(jnp.where(my_live, base + pushed[1 + a : 2 + a], 0.0))
    moved = jnp.concatenate(moved + [jnp.zeros((5, LANES), jnp.float32)], axis=0)
    for o in range(owners):
        turned = pltpu.roll(moved, LANES - o * capacity, 1) if o else moved
        for a in range(3):
            wall_out_ref[0, 0, 0, a, o : o + 1] = turned[a : a + 1, :capacity]
    for k, (src, dst) in enumerate(((vel_out_ref, vel_hbm), (pos_out_ref, pos_hbm), (wall_out_ref, wall_hbm))):
        copies.append(pltpu.make_async_copy(src, dst, sems.at[size_x + k]))
        copies[-1].start()
    for copy in copies:
        copy.wait()


def ring(count, step):
    return [(i, (i + step) % count) for i in range(count)]


def body(
    populations,
    solid,
    link_cell,
    link_dir,
    link_node,
    link_velocity,
    fabric_position,
    fabric_velocity,
    fabric_rest,
    triangles,
):
    size_x, size_y, size_z = populations.shape[1:]
    owners, capacity = link_node.shape[3:]
    nodes = fabric_position.shape[2]
    count_x, count_y, count_z = (lax.axis_size(name) for name in ("gx", "gy", "gz"))
    folded = (
        (count_y, count_z) == (4, 2)
        and (size_y, size_z) == (8, LANES)
        and owners * capacity == LANES
        and nodes == 4 * LANES
    )
    if not folded:
        return general_body(
            populations, solid, link_cell, link_dir, link_node, link_velocity,
            fabric_position, fabric_velocity, fabric_rest, triangles,
        )
    f32 = jnp.float32
    on_chip = pl.BlockSpec(memory_space=pltpu.VMEM)

    def shape(*dims):
        return jax.ShapeDtypeStruct(dims, f32)

    def kept(*dims):
        return pltpu.VMEM(dims, f32)

    def run(kernel, outs, *args):
        args = [pltpu.with_memory_space_constraint(arg, pltpu.VMEM) for arg in args]
        return pl.pallas_call(
            kernel,
            out_shape=outs,
            in_specs=[on_chip] * len(args),
            out_specs=jax.tree.map(lambda _: on_chip, outs),
            name=kernel.__name__,
        )(*args)

    face_x = kept(5, size_y, size_z)
    map_shape = kept(size_x, size_y, size_z)
    given = (
        populations, solid, link_cell, link_dir, link_node, link_velocity,
        fabric_position, fabric_velocity, fabric_rest, triangles,
    )
    cells = size_x * size_y
    opened = (kept(*populations.shape), face_x, face_x, kept(max(SEED, FAB + cells), LANES), map_shape, map_shape, kept(*fabric_position.shape))
    post, up, down, seed, kind, back, position = pl.pallas_call(
        open_kernel,
        out_shape=opened,
        in_specs=[pl.BlockSpec(memory_space=pl.ANY)] * len(given),
        out_specs=(on_chip,) * len(opened),
        scratch_shapes=[pltpu.VMEM(arg.shape, arg.dtype) for arg in given if arg is not fabric_position]
        + [pltpu.SemaphoreType.DMA((len(given),))],
        name="open_kernel",
    )(*given)
    swap_z = [(0, 1), (1, 0)]
    other = lax.ppermute(seed, "gz", swap_z)
    xlow = lax.ppermute(up, "gx", ring(count_x, 1))
    xhigh = lax.ppermute(down, "gx", ring(count_x, -1))
    (pair,) = run(pair_kernel, (kept(2 * FAB, LANES),), seed, other)
    cross = lax.ppermute(pair, "gy", [(y, y ^ 2) for y in range(count_y)])
    middling = []
    for y in range(count_y):
        to = y + 1 if y % 2 else y - 1
        for z in range(count_z):
            middling.append((y * 2 + z, to * 2 + z if 0 <= to < count_y else y * 2 + 1 - z))
    rows = -(-5 * size_x // 8) * 8
    (middle,) = run(middle_kernel, (kept(4 * rows, LANES),), post, xlow, xhigh, other)
    middle = lax.ppermute(middle, ("gy", "gz"), middling)
    (edge,) = run(edge_kernel, (kept(size_y, LANES),), xlow, xhigh)
    edge = lax.ppermute(edge, "gz", swap_z)
    (near,) = run(near_kernel, (kept(4 * FAB + rows, LANES),), post, xlow, xhigh, other, pair, cross)
    near = lax.ppermute(near, "gy", [(y, y ^ 1) for y in range(count_y)])
    (rolled,) = run(shift_kernel, (kept(*populations.shape),), post, xlow, xhigh, other, edge)
    (acc,) = run(half_kernel, (kept(32, LANES),), seed, pair, cross)
    outs = (
        shape(*populations.shape),
        shape(*fabric_position.shape),
        shape(*fabric_velocity.shape),
        shape(*link_velocity.shape),
    )
    last = [rolled, kind, back, seed, acc, near, middle, position]
    last = [pltpu.with_memory_space_constraint(arg, pltpu.VMEM) for arg in last]
    return pl.pallas_call(
        final_kernel,
        out_shape=outs,
        in_specs=[on_chip] * len(last),
        out_specs=(pl.BlockSpec(memory_space=pl.ANY),) * 4,
        scratch_shapes=[pltpu.VMEM(out.shape, f32) for out in outs] + [pltpu.SemaphoreType.DMA((size_x + 3,))],
        name="final_kernel",
    )(*last)


def solution(mesh):
    placed = (
        P(None, "gx", "gy", "gz"),
        P("gx", "gy", "gz"),
        P("gx", "gy", "gz", None, None),
        P("gx", "gy", "gz", None, None),
        P("gx", "gy", "gz", None, None),
        P("gx", "gy", "gz", None, None, None),
        P(None, "gx", ("gy", "gz")),
        P(None, "gx", ("gy", "gz")),
        P(None, "gx", ("gy", "gz")),
        P(None, "gx", ("gy", "gz")),
    )
    return jax.shard_map(
        body,
        mesh=mesh,
        in_specs=placed,
        out_specs=(
            P(None, "gx", "gy", "gz"),
            P(None, "gx", ("gy", "gz")),
            P(None, "gx", ("gy", "gz")),
            P("gx", "gy", "gz", None, None, None),
        ),
        check_vma=False,
    )
```

```python
import jax
import jax.numpy as jnp
import numpy as np
from jax import lax
from jax.experimental import pallas as pl
from jax.experimental.pallas import tpu as pltpu
from jax.sharding import PartitionSpec as P

SPRING = 0.5
DAMPING = 0.1
DIRECTIONS = [
    [0, 0, 0],
    [1, 0, 0],
    [-1, 0, 0],
    [0, 1, 0],
    [0, -1, 0],
    [0, 0, 1],
    [0, 0, -1],
    [1, 1, 0],
    [-1, -1, 0],
    [1, -1, 0],
    [-1, 1, 0],
    [1, 0, 1],
    [-1, 0, -1],
    [1, 0, -1],
    [-1, 0, 1],
    [0, 1, 1],
    [0, -1, -1],
    [0, 1, -1],
    [0, -1, 1],
]


def extended(cells, sides, width):
    for axis, dim in sides:
        count = lax.axis_size(axis)
        head = lax.slice_in_dim(cells, 0, width, axis=dim)
        tail = lax.slice_in_dim(cells, cells.shape[dim] - width, cells.shape[dim], axis=dim)
        cells = jnp.concatenate(
            [
                lax.ppermute(tail, axis, [(i, (i + 1) % count) for i in range(count)]),
                cells,
                lax.ppermute(head, axis, [((i + 1) % count, i) for i in range(count)]),
            ],
            axis=dim,
        )
    return cells


def lattice():
    velocity_np = np.array(DIRECTIONS)
    weight_np = np.array([1.0 / 3.0] + [1.0 / 18.0] * 6 + [1.0 / 36.0] * 12)
    opposite_list = [
        DIRECTIONS.index([-entry for entry in DIRECTIONS[direction]]) for direction in range(19)
    ]
    along_a = np.array([float(entry[0]) for entry in DIRECTIONS])
    along_b = np.array([float(entry[1]) for entry in DIRECTIONS])
    along_e = np.array([float(entry[2]) for entry in DIRECTIONS])
    speed_sq = along_a * along_a + along_b * along_b + along_e * along_e
    moment_rows = [
        np.ones(19),
        19 * speed_sq - 30,
        (21 * speed_sq * speed_sq - 53 * speed_sq + 24) / 2,
        along_a,
        (5 * speed_sq - 9) * along_a,
        along_b,
        (5 * speed_sq - 9) * along_b,
        along_e,
        (5 * speed_sq - 9) * along_e,
        3 * along_a * along_a - speed_sq,
        (3 * speed_sq - 5) * (3 * along_a * along_a - speed_sq),
        along_b * along_b - along_e * along_e,
        (3 * speed_sq - 5) * (along_b * along_b - along_e * along_e),
        along_a * along_b,
        along_b * along_e,
        along_a * along_e,
        (along_b * along_b - along_e * along_e) * along_a,
        (along_e * along_e - along_a * along_a) * along_b,
        (along_a * along_a - along_b * along_b) * along_e,
    ]
    moment_np = np.stack(moment_rows)
    inverse_np = moment_np.T / np.sum(moment_np * moment_np, axis=1)[None, :]
    viscous = 5.0 / 3.0
    rates_np = np.array(
        [
            0.0,
            1.19,
            1.4,
            0.0,
            1.2,
            0.0,
            1.2,
            0.0,
            1.2,
            viscous,
            1.4,
            viscous,
            1.4,
            viscous,
            viscous,
            viscous,
            1.98,
            1.98,
            1.98,
        ]
    )
    return (velocity_np, weight_np, opposite_list, moment_np, inverse_np, rates_np)


def collide_cells(popul, solid_flat):
    velocity_np, weight_np, opposite_list, moment_np, inverse_np, rates_np = lattice()
    velocity_table = jnp.asarray(velocity_np, jnp.float32)
    weight_table = jnp.asarray(weight_np, jnp.float32)
    density = jnp.sum(popul, axis=0)
    momentum = jnp.dot(
        velocity_table.T, popul, precision=lax.Precision.HIGHEST, preferred_element_type=jnp.float32
    )
    flow = momentum / density
    projected = jnp.dot(
        velocity_table, flow, precision=lax.Precision.HIGHEST, preferred_element_type=jnp.float32
    )
    speed_sq = jnp.sum(flow * flow, axis=0)
    equilibrium = (
        weight_table[:, None]
        * density
        * (1.0 + 3.0 * projected + 4.5 * projected * projected - 1.5 * speed_sq)
    )
    offset = popul - equilibrium
    moments = jnp.dot(
        jnp.asarray(moment_np, jnp.float32),
        offset,
        precision=lax.Precision.HIGHEST,
        preferred_element_type=jnp.float32,
    )
    relaxed = jnp.asarray(rates_np, jnp.float32)[:, None] * moments
    change = jnp.dot(
        jnp.asarray(inverse_np, jnp.float32),
        relaxed,
        precision=lax.Precision.HIGHEST,
        preferred_element_type=jnp.float32,
    )
    return jnp.where(solid_flat[None, :] == 1, popul, popul - change)


def fill_outside(padded, weight_np):
    span_y = padded.shape[2]
    span_z = padded.shape[3]
    place_y = lax.axis_index("gy")
    place_z = lax.axis_index("gz")
    count_y = lax.axis_size("gy")
    count_z = lax.axis_size("gz")
    rows_y = jnp.arange(span_y)
    rows_z = jnp.arange(span_z)
    out_y = (rows_y == 0) & (place_y == 0) | (rows_y == span_y - 1) & (place_y == count_y - 1)
    out_z = (rows_z == 0) & (place_z == 0) | (rows_z == span_z - 1) & (place_z == count_z - 1)
    outside = out_y[:, None] | out_z[None, :]
    return jnp.where(
        outside[None, None], jnp.asarray(weight_np, jnp.float32)[:, None, None, None], padded
    )


def propagate(padded, size_x, size_y, size_z):
    pieces = []
    for direction in range(19):
        shift_x = DIRECTIONS[direction][0]
        shift_y = DIRECTIONS[direction][1]
        shift_z = DIRECTIONS[direction][2]
        plane = padded[direction]
        pieces.append(
            lax.slice(
                plane,
                (1 - shift_x, 1 - shift_y, 1 - shift_z),
                (1 - shift_x + size_x, 1 - shift_y + size_y, 1 - shift_z + size_z),
            )
        )
    return jnp.stack(pieces)


def membrane(positions, rest, triangle_nodes):
    force = jnp.zeros(positions.shape, jnp.float32)
    for first, second in ((0, 1), (1, 2), (2, 0)):
        head = triangle_nodes[first]
        tail = triangle_nodes[second]
        stretch = positions[:, tail] - positions[:, head] - (rest[:, tail] - rest[:, head])
        force = force.at[:, head].add(SPRING * stretch)
        force = force.at[:, tail].add(-SPRING * stretch)
    return force


def general_body(
    populations,
    solid,
    link_cell,
    link_dir,
    link_node,
    link_velocity,
    fabric_position,
    fabric_velocity,
    fabric_rest,
    triangles,
):
    velocity_np, weight_np, opposite_list, moment_np, inverse_np, rates_np = lattice()
    velocity_table = jnp.asarray(velocity_np, jnp.float32)
    weight_table = jnp.asarray(weight_np, jnp.float32)
    opposite_table = jnp.asarray(opposite_list, jnp.int32)
    size_x = populations.shape[1]
    size_y = populations.shape[2]
    size_z = populations.shape[3]
    cells = size_x * size_y * size_z
    post = collide_cells(populations.reshape(19, cells), solid.reshape(cells)).reshape(
        populations.shape
    )
    padded = extended(post, (("gx", 1), ("gy", 2), ("gz", 3)), 1)
    padded = fill_outside(padded, weight_np)
    propagated = propagate(padded, size_x, size_y, size_z).reshape(19, cells)
    owners_n = link_node.shape[3]
    capacity = link_node.shape[4]
    node_rows = link_node.reshape(owners_n, capacity)
    cell_rows = link_cell.reshape(owners_n, capacity)
    dir_rows = link_dir.reshape(owners_n, capacity)
    live = node_rows >= 0
    post_flat = post.reshape(19, cells)
    reflected = post_flat[opposite_table[dir_rows], cell_rows]
    link_unit = velocity_table[dir_rows]
    wall = jnp.moveaxis(link_velocity.reshape(3, owners_n, capacity), 0, -1)
    returned = reflected + 6.0 * weight_table[dir_rows] * jnp.sum(link_unit * wall, axis=-1)
    populations_next = propagated.at[jnp.where(live, dir_rows, 19), cell_rows].set(
        returned, mode="drop"
    )
    strength = reflected + returned
    positions = fabric_position.reshape(3, -1)
    velocities = fabric_velocity.reshape(3, -1)
    rest = fabric_rest.reshape(3, -1)
    nodes_n = positions.shape[1]
    elastic = membrane(positions, rest, triangles.reshape(3, -1))
    link_force = jnp.moveaxis(-link_unit * strength[..., None], -1, 0)
    got_nodes, got_force = (
        lax.all_to_all(node_rows[None], ("gy", "gz"), split_axis=1, concat_axis=1, tiled=True),
        lax.all_to_all(link_force, ("gy", "gz"), split_axis=1, concat_axis=1, tiled=True),
    )
    got_ids = got_nodes[0]
    got_live = got_ids >= 0
    target = jnp.where(got_live, got_ids, nodes_n).reshape(-1)
    fluid_force = (
        jnp.zeros((3, nodes_n), jnp.float32)
        .at[:, target]
        .add(got_force.reshape(3, -1), mode="drop")
    )
    velocity_next = (1.0 - DAMPING) * velocities + (fluid_force + elastic)
    position_next = positions + velocity_next
    reply = jnp.where(got_live[None], velocity_next[:, jnp.where(got_live, got_ids, 0)], 0.0)
    wall_next = lax.all_to_all(reply, ("gy", "gz"), split_axis=1, concat_axis=1, tiled=True)
    return (
        populations_next.reshape(populations.shape),
        position_next.reshape(fabric_position.shape),
        velocity_next.reshape(fabric_velocity.shape),
        wall_next.reshape(link_velocity.shape),
    )


WEIGHTS = [1.0 / 3.0] + [1.0 / 18.0] * 6 + [1.0 / 36.0] * 12
OPPOSITE = [DIRECTIONS.index([-entry for entry in d]) for d in DIRECTIONS]
SIDES = [
    ([i for i in range(19) if DIRECTIONS[i][a] == 1], [i for i in range(19) if DIRECTIONS[i][a] == -1])
    for a in range(3)
]
LANES = 128
PATCH = 256
FAB = 16
SEED = 80
MID = 4


def iota(shape, axis):
    return lax.broadcasted_iota(jnp.int32, shape, axis)


def split3(value):
    high = value.astype(jnp.bfloat16).astype(jnp.float32)
    rest = value - high
    middle = rest.astype(jnp.bfloat16).astype(jnp.float32)
    return high, middle, rest - middle


def stacked3(value):
    return jnp.concatenate(split3(value), axis=0).astype(jnp.bfloat16)


def sum3(value):
    rows = value.shape[0] // 3
    return value[:rows] + value[rows : 2 * rows] + value[2 * rows :]


def dot_nn(left, right):
    return lax.dot_general(left, right, (((1,), (0,)), ((), ())), preferred_element_type=jnp.float32)


def dot_nt(left, right):
    return lax.dot_general(left, right, (((1,), (1,)), ((), ())), preferred_element_type=jnp.float32)


def one_hot(mask):
    return jnp.where(mask, 1.0, 0.0).astype(jnp.bfloat16)


def collided(f, solid):
    sx, dx = f[1] + f[2], f[1] - f[2]
    sy, dy = f[3] + f[4], f[3] - f[4]
    sz, dz = f[5] + f[6], f[5] - f[6]
    sa, da = f[7] + f[8], f[7] - f[8]
    sb, db = f[9] + f[10], f[9] - f[10]
    sc, dc = f[11] + f[12], f[11] - f[12]
    sd, dd = f[13] + f[14], f[13] - f[14]
    se, de = f[15] + f[16], f[15] - f[16]
    sg, dg = f[17] + f[18], f[17] - f[18]
    sxy, txy = sa + sb, sa - sb
    sxz, txz = sc + sd, sc - sd
    syz, tyz = se + sg, se - sg
    ax_ab, ay_ab = da + db, da - db
    ax_cd, az_cd = dc + dd, dc - dd
    ay_eg, az_eg = de + dg, de - dg
    near, far = sx + sy + sz, sxy + sxz + syz
    rho = f[0] + near + far
    ex, ey, ez = ax_ab + ax_cd, ay_ab + ay_eg, az_cd + az_eg
    jx, jy, jz = dx + ex, dy + ey, dz + ez
    inv = 1.0 / rho
    ux, uy, uz = jx * inv, jy * inv, jz * inv
    xx, yy, zz = jx * ux, jy * uy, jz * uz
    jj = xx + yy + zz
    energy = (-30.0 * f[0] - 11.0 * near + 8.0 * far) - (-11.0 * rho + 19.0 * jj)
    square = (12.0 * f[0] - 4.0 * near + far) - (3.0 * rho - 5.5 * jj)
    kx = (1.2 / 40.0) * (ex - 4.0 * dx + (2.0 / 3.0) * jx)
    ky = (1.2 / 40.0) * (ey - 4.0 * dy + (2.0 / 3.0) * jy)
    kz = (1.2 / 40.0) * (ez - 4.0 * dz + (2.0 / 3.0) * jz)
    yz_near, xyz_far = sy + sz, sxy + sxz - 2.0 * syz
    pxx_eq = 2.0 * xx - yy - zz
    pww_eq = yy - zz
    pxx = (5.0 / 3.0 / 36.0) * (2.0 * sx - yz_near + xyz_far - pxx_eq)
    pixx = (1.4 / 72.0) * (-4.0 * sx + 2.0 * yz_near + xyz_far + 0.5 * pxx_eq)
    w_near, w_far = sy - sz, sxy - sxz
    pww = (5.0 / 3.0 / 12.0) * (w_near + w_far - pww_eq)
    piww = (1.4 / 24.0) * (w_far - 2.0 * w_near + 0.5 * pww_eq)
    pxy = (5.0 / 3.0 / 4.0) * (txy - jx * uy)
    pyz = (5.0 / 3.0 / 4.0) * (tyz - jy * uz)
    pxz = (5.0 / 3.0 / 4.0) * (txz - jx * uz)
    mx = (1.98 / 8.0) * (ax_ab - ax_cd)
    my = (1.98 / 8.0) * (ay_eg - ay_ab)
    mz = (1.98 / 8.0) * (az_cd - az_eg)
    energy = (1.19 / 2394.0) * energy
    square = (1.4 / 252.0) * square
    axis = -11.0 * energy - 4.0 * square
    across = pxx - 2.0 * pixx
    split = pww - 2.0 * piww
    edge = 8.0 * energy + square
    pp, ww = pxx + pixx, pww + piww
    even = [
        axis + 2.0 * across,
        axis - across + split,
        axis - across - split,
        edge + pp + ww + pxy,
        edge + pp + ww - pxy,
        edge + pp - ww + pxz,
        edge + pp - ww - pxz,
        edge - 2.0 * pp + pyz,
        edge - 2.0 * pp - pyz,
    ]
    odd = [
        -4.0 * kx,
        -4.0 * ky,
        -4.0 * kz,
        (kx + mx) + (ky - my),
        (kx + mx) - (ky - my),
        (kx - mx) + (kz + mz),
        (kx - mx) - (kz + mz),
        (ky + my) + (kz - mz),
        (ky + my) - (kz - mz),
    ]
    change = [12.0 * square - 30.0 * energy]
    for pair in range(9):
        change += [even[pair] + odd[pair], even[pair] - odd[pair]]
    fluid = solid != 1
    return [jnp.where(fluid, f[i] - change[i], f[i]) for i in range(19)]


def slots_to_row(value):
    owners, capacity = value.shape
    wide = jnp.concatenate([value, jnp.zeros((owners, LANES - capacity), value.dtype)], axis=1)
    return jnp.sum(pltpu.roll(wide, 0, 1, stride=capacity, stride_axis=0), axis=0, keepdims=True)


def membrane_base(pos_ref, vel_ref, rest_ref, tri_ref, fab_ref):
    nodes = pos_ref.shape[2]
    count = tri_ref.shape[2]
    wide = -(-count // LANES) * LANES
    patches = nodes // PATCH
    stretch = [pos_ref[a] - rest_ref[a] for a in range(3)]
    corners = [
        jnp.concatenate([tri_ref[t], jnp.full((1, wide - count), -1, jnp.int32)], axis=1) for t in range(3)
    ]
    patch = jnp.maximum(corners[0], 0) // PATCH
    local = [(corner - patch * PATCH).astype(jnp.float32) for corner in corners]
    node_ids = iota((PATCH, LANES), 0).astype(jnp.float32).astype(jnp.bfloat16)
    blocks = []
    for k in range(0, wide, LANES):
        block = jnp.zeros((PATCH, LANES), jnp.bfloat16)
        for corner in local:
            row = jnp.broadcast_to(corner[:, k : k + LANES], (16, LANES)).astype(jnp.bfloat16)
            row = jnp.concatenate([row] * (PATCH // 16), axis=0)
            block = block + jnp.where(node_ids == row, jnp.ones_like(block), jnp.zeros_like(block))
        blocks.append(block)
    hits = jnp.concatenate(blocks, axis=1)
    stretch8 = jnp.concatenate(stretch + [jnp.zeros((5, nodes), jnp.float32)], axis=0)
    pieces = [stacked3(stretch8[:, p * PATCH : (p + 1) * PATCH]) for p in range(patches)]
    sums = dot_nn(jnp.concatenate(pieces, axis=0), hits)
    total = jnp.zeros((8, wide), jnp.float32)
    for p in range(patches):
        total = jnp.where(patch == p, sum3(sums[p * 24 : (p + 1) * 24]), total)
    total = jnp.where(iota(total.shape, 0) == 3, 1.0, total)
    pieces = [stacked3(jnp.where(patch == p, total, 0.0)) for p in range(patches)]
    sums = dot_nt(jnp.concatenate(pieces, axis=0), hits)
    back = jnp.concatenate([sum3(sums[p * 24 : (p + 1) * 24]) for p in range(patches)], axis=1)
    for a in range(3):
        elastic = SPRING * back[a : a + 1] - 3.0 * SPRING * back[3:4] * stretch[a]
        base = (1.0 - DAMPING) * vel_ref[a] + elastic
        for k in range(nodes // LANES):
            row = 4 + a * (nodes // LANES) + k
            fab_ref[row : row + 1] = base[:, k * LANES : (k + 1) * LANES]


def z_face(tiles):
    up = jnp.zeros_like(next(t for t in tiles if t is not None))
    lane = iota(up.shape, 1)
    down = up
    for k in range(5):
        i, j = SIDES[2][0][k], SIDES[2][1][k]
        if tiles[i] is not None:
            up = jnp.where(lane == k, pltpu.roll(tiles[i], k + 1, 1), up)
        if tiles[j] is not None:
            down = jnp.where(lane == k, pltpu.roll(tiles[j], k, 1) if k else tiles[j], down)
    return jnp.where(lax.axis_index("gz") == 0, up, down)


def z_shift(tile, i, face):
    lane = iota(tile.shape, 1)
    low_end = lax.axis_index("gz") == 0
    if DIRECTIONS[i][2] == 1:
        k = SIDES[2][0].index(i)
        halo = pltpu.roll(face, LANES - k, 1) if k else face
        return jnp.where(lane == 0, jnp.where(low_end, WEIGHTS[i], halo), pltpu.roll(tile, 1, 1))
    if DIRECTIONS[i][2] == -1:
        k = SIDES[2][1].index(i)
        halo = pltpu.roll(face, LANES - 1 - k, 1)
        return jnp.where(lane == LANES - 1, jnp.where(low_end, halo, WEIGHTS[i]), pltpu.roll(tile, LANES - 1, 1))
    return tile


def open_kernel(
    pop_hbm, solid_hbm, cell_hbm, dir_hbm, node_hbm, wall_hbm, pos_hbm, vel_hbm, rest_hbm, tri_hbm,
    post_ref, up_ref, down_ref, seed_ref, kind_ref, back_ref, pos_ref,
    pop_ref, solid_ref, cell_ref, dir_ref, node_ref, wall_ref, vel_ref, rest_ref, tri_ref, sems,
):
    moves = [
        (pop_hbm, pop_ref), (solid_hbm, solid_ref),
        (tri_hbm, tri_ref), (pos_hbm, pos_ref), (rest_hbm, rest_ref), (vel_hbm, vel_ref),
        (cell_hbm, cell_ref), (dir_hbm, dir_ref), (node_hbm, node_ref), (wall_hbm, wall_ref),
    ]
    copies = [pltpu.make_async_copy(src, dst, sems.at[k]) for k, (src, dst) in enumerate(moves)]
    for copy in copies[2:] + copies[:2]:
        copy.start()
    for copy in copies[2:]:
        copy.wait()
    membrane_base(pos_ref, vel_ref, rest_ref, tri_ref, seed_ref)
    size_x, size_y = post_ref.shape[1:3]
    rows = size_x * size_y
    cell = slots_to_row(cell_ref[0, 0, 0].astype(jnp.float32)).astype(jnp.int32)
    way = slots_to_row(dir_ref[0, 0, 0].astype(jnp.float32))
    node = slots_to_row(node_ref[0, 0, 0].astype(jnp.float32))
    live = node >= 0.0
    unit = []
    for a in range(3):
        u = jnp.zeros_like(way)
        for i in range(1, 19):
            if DIRECTIONS[i][a]:
                u = jnp.where(way == float(i), float(DIRECTIONS[i][a]), u)
        unit.append(u)
    weight = jnp.where(way >= 7.0, 6.0 / 36.0, 6.0 / 18.0)
    wall = [slots_to_row(wall_ref[0, 0, 0, a]) for a in range(3)]
    term = weight * (unit[0] * wall[0] + unit[1] * wall[1] + unit[2] * wall[2])
    at_row = jnp.where((iota((rows, LANES), 0) == (cell >> 7)) & live, 1.0, 0.0)
    at_lane = one_hot(iota((LANES, LANES), 0) == (cell & (LANES - 1)))
    left = jnp.concatenate([at_row * way] + [at_row * t for t in split3(term)], axis=0)
    maps = dot_nt(left.astype(jnp.bfloat16), at_lane)
    kind = maps[:rows]
    added = sum3(maps[rows:])
    for copy in copies[:2]:
        copy.wait()
    taken = []
    for x in range(size_x):
        post = collided([pop_ref[i, x] for i in range(19)], solid_ref[x])
        k = kind[x * size_y : (x + 1) * size_y]
        t = jnp.zeros_like(k)
        for i in range(19):
            post_ref[i, x] = post[i]
            if x == size_x - 1 and i in SIDES[0][0]:
                up_ref[SIDES[0][0].index(i)] = post[i]
            if x == 0 and i in SIDES[0][1]:
                down_ref[SIDES[0][1].index(i)] = post[i]
            if i:
                t = jnp.where(k == float(OPPOSITE[i]), post[i], t)
        seed_ref[FAB + x * size_y : FAB + (x + 1) * size_y] = z_face(post)
        taken.append(t)
        kind_ref[x] = k
        back_ref[x] = t + added[x * size_y : (x + 1) * size_y]
    strength = 2.0 * jnp.concatenate(taken, axis=0) + added
    at_link = sum3(dot_nn(stacked3(strength), at_lane))
    push = jnp.sum(at_row * at_link, axis=0, keepdims=True)
    seed_ref[0:1] = node
    for a in range(3):
        seed_ref[1 + a : 2 + a] = -unit[a] * push
    end = FAB + rows
    seed_ref[end:] = jnp.zeros((seed_ref.shape[0] - end, LANES), jnp.float32)


def source_tile(post_ref, low_ref, high_ref, i, x):
    size_x = post_ref.shape[1]
    from_x = x - DIRECTIONS[i][0]
    if from_x < 0:
        return low_ref.at[SIDES[0][0].index(i)]
    if from_x >= size_x:
        return high_ref.at[SIDES[0][1].index(i)]
    return post_ref.at[i, from_x]


def pair_kernel(seed_ref, other_ref, pair_ref):
    low = lax.axis_index("gz") == 0
    pair_ref[:FAB] = jnp.where(low, seed_ref[:FAB], other_ref[:FAB])
    pair_ref[FAB:] = jnp.where(low, other_ref[:FAB], seed_ref[:FAB])


def edge_kernel(low_ref, high_ref, edge_ref):
    tiles = [None] * 19
    for i in range(19):
        if DIRECTIONS[i][0] and DIRECTIONS[i][2]:
            side = 0 if DIRECTIONS[i][0] == 1 else 1
            tiles[i] = (low_ref, high_ref)[side][SIDES[0][side].index(i)]
    edge_ref[...] = z_face(tiles)


def face_rows(post_ref, low_ref, high_ref, other_ref, out_ref, start, upward):
    size_x, size_y = post_ref.shape[1:3]
    for k in range(5):
        for x in range(size_x):
            at = start + k * size_x + x
            face = other_ref[FAB + x * size_y : FAB + (x + 1) * size_y]
            rows = []
            for side, row in ((0, size_y - 1), (1, 0)):
                i = SIDES[1][side][k]
                source = source_tile(post_ref, low_ref, high_ref, i, x)
                if DIRECTIONS[i][2]:
                    rows.append(z_shift(source[...], i, face)[row : row + 1])
                else:
                    rows.append(source[row : row + 1])
            out_ref[at : at + 1] = jnp.where(upward, rows[0], rows[1])
    end = start + 5 * size_x
    if out_ref.shape[0] > end:
        out_ref[end:] = jnp.zeros((out_ref.shape[0] - end, LANES), jnp.float32)


def middle_kernel(post_ref, low_ref, high_ref, other_ref, middle_ref):
    odd = lax.rem(lax.axis_index("gy"), 2) == 1
    face_rows(post_ref, low_ref, high_ref, other_ref, middle_ref, 0, odd)


def sides_kernel(post_ref, low_ref, high_ref, other_ref, middle_ref, face_ref, edge_ref):
    odd = lax.rem(lax.axis_index("gy"), 2) == 1
    face_rows(post_ref, low_ref, high_ref, other_ref, middle_ref, 0, odd)
    face_rows(post_ref, low_ref, high_ref, other_ref, face_ref, 0, jnp.logical_not(odd))
    edge_kernel(low_ref, high_ref, edge_ref)


def near_kernel(pair_ref, cross_ref, face_ref, near_ref):
    near_ref[: 2 * FAB] = pair_ref[...]
    near_ref[2 * FAB : 4 * FAB] = cross_ref[...]
    near_ref[4 * FAB :] = face_ref[...]


def shift_kernel(post_ref, low_ref, high_ref, other_ref, edge_ref, rolled_ref):
    size_x, size_y = post_ref.shape[1:3]
    for i in range(19):
        for x in range(size_x):
            tile = source_tile(post_ref, low_ref, high_ref, i, x)[...]
            from_x = x - DIRECTIONS[i][0]
            if 0 <= from_x < size_x:
                face = other_ref[FAB + from_x * size_y : FAB + (from_x + 1) * size_y]
            else:
                face = edge_ref[...]
            tile = z_shift(tile, i, face)
            if DIRECTIONS[i][1]:
                tile = pltpu.roll(tile, DIRECTIONS[i][1] % size_y, 0)
            rolled_ref[i, x] = tile


def fabric_part(pairs, chips, start, my_node, column, at_lane, nodes, capacity):
    parts = nodes // LANES
    me = lax.axis_index("gy") * 2 + lax.axis_index("gz")
    slot_owner = iota((1, LANES), 1) // capacity
    owner_base = (slot_owner * nodes).astype(jnp.float32)
    matches, forces, picked = [], [], jnp.zeros((8, LANES), jnp.float32)
    for m in range(2 * len(pairs)):
        tile = pairs[m // 2][m % 2 * FAB : m % 2 * FAB + 8]
        ids = tile[0:1]
        ids = jnp.where(ids >= 0.0, owner_base + ids, -1.0)
        matches.append(one_hot(column == ids))
        forces.append(tile)
        shift = lax.rem((start + m + LANES // capacity - me) * capacity, LANES)
        picked = jnp.where(slot_owner == start + m, pltpu.roll(tile, shift, 1), picked)
    pushed = sum3(dot_nt(stacked3(jnp.concatenate(forces, axis=1)), jnp.concatenate(matches, axis=1)))

    found = sum3(dot_nn(stacked3(jnp.concatenate(pairs, axis=0)), at_lane))
    row = iota((FAB, LANES), 0)
    fits = (row >= 4) & (row % parts == (my_node.astype(jnp.int32) >> 7))
    base = jnp.zeros((FAB, LANES), jnp.float32)
    for m in range(2 * len(pairs)):
        owner = chips[m // 2] * 2 + m % 2
        base = jnp.where(fits & (slot_owner == owner), found[m * FAB : (m + 1) * FAB], base)
    return jnp.concatenate([pushed, base, picked], axis=0)


def half_kernel(seed_ref, pair_ref, cross_ref, acc_ref, column_ref, lane_ref):
    place_y = lax.axis_index("gy")
    nodes, capacity = 4 * LANES, LANES // 8
    my_node = seed_ref[0:1]
    owner_base = (iota((1, LANES), 1) // capacity * nodes).astype(jnp.float32)
    my_id = jnp.where(my_node >= 0.0, owner_base + my_node, -2.0)
    column = jnp.transpose(jnp.broadcast_to(my_id, (LANES, LANES)))
    at_lane = one_hot(iota((LANES, LANES), 0) == (my_node.astype(jnp.int32) & (LANES - 1)))
    pairs, chips = [pair_ref[...], cross_ref[...]], [place_y, place_y ^ 2]
    acc_ref[...] = fabric_part(pairs, chips, 0, my_node, column, at_lane, nodes, capacity)
    column_ref[...] = column
    lane_ref[...] = at_lane


def final_kernel(
    rolled_ref, kind_ref, back_ref, seed_ref, acc_ref, column_ref, lane_ref, near_ref, middle_ref, pos_ref,
    pop_hbm, pos_hbm, vel_hbm, wall_hbm,
    pop_ref, pos_out_ref, vel_out_ref, wall_out_ref, sems,
):
    size_x, size_y = rolled_ref.shape[1:3]
    place_y = lax.axis_index("gy")
    odd = lax.rem(place_y, 2) == 1
    first, top = place_y == 0, place_y == lax.axis_size("gy") - 1
    sub = iota((size_y, LANES), 0)
    copies = []
    for x in range(size_x):
        kind = kind_ref[x]
        back = back_ref[x]
        for i in range(19):
            tile = rolled_ref[i, x]
            if DIRECTIONS[i][1]:
                side = 0 if DIRECTIONS[i][1] == 1 else 1
                at = SIDES[1][side].index(i) * size_x + x
                by_near = near_ref[4 * FAB + at : 4 * FAB + at + 1]
                by_middle = middle_ref[at : at + 1]
                if side == 0:
                    row = jnp.where(first, WEIGHTS[i], jnp.where(odd, by_near, by_middle))
                    tile = jnp.where(sub == 0, row, tile)
                else:
                    row = jnp.where(top, WEIGHTS[i], jnp.where(odd, by_middle, by_near))
                    tile = jnp.where(sub == size_y - 1, row, tile)
            if i:
                tile = jnp.where(kind == float(i), back, tile)
            pop_ref[i, x] = tile
        copies.append(pltpu.make_async_copy(pop_ref.at[:, x], pop_hbm.at[:, x], sems.at[x]))
        copies[-1].start()

    owners, capacity = wall_out_ref.shape[4], wall_out_ref.shape[5]
    nodes = pos_ref.shape[2]
    parts = nodes // LANES
    mine = seed_ref[:FAB]
    pairs, chips = [near_ref[: 2 * FAB], near_ref[2 * FAB : 4 * FAB]], [place_y ^ 1, place_y ^ 3]
    acc = fabric_part(pairs, chips, 4, mine[0:1], column_ref[...], lane_ref[...], nodes, capacity) + acc_ref[...]
    pushed, found, picked = acc[:8], acc[8:24], acc[24:32]
    node = picked[0:1].astype(jnp.int32)
    row = iota((FAB, LANES), 0)
    spread = jnp.where(row < parts, picked[1:2], jnp.where(row < 2 * parts, picked[2:3], picked[3:4]))
    spread = jnp.where((row < 3 * parts) & (row % parts == (node >> 7)), spread, 0.0)
    at_node = one_hot(iota((LANES, LANES), 0) == (node & (LANES - 1)))
    fluid = sum3(dot_nt(stacked3(spread), at_node))
    my_live = mine[0:1] >= 0.0
    moved = []
    for a in range(3):
        for k in range(parts):
            r = a * parts + k
            new = mine[4 + r : 5 + r] + fluid[r : r + 1]
            at = slice(k * LANES, (k + 1) * LANES)
            vel_out_ref[a, :, at] = new
            pos_out_ref[a, :, at] = pos_ref[a, :, at] + new
        base = jnp.sum(found[4 + a * parts : 4 + (a + 1) * parts], axis=0, keepdims=True)
        moved.append(jnp.where(my_live, base + pushed[1 + a : 2 + a], 0.0))
    moved = jnp.concatenate(moved + [jnp.zeros((5, LANES), jnp.float32)], axis=0)
    for o in range(owners):
        turned = pltpu.roll(moved, LANES - o * capacity, 1) if o else moved
        for a in range(3):
            wall_out_ref[0, 0, 0, a, o : o + 1] = turned[a : a + 1, :capacity]
    for k, (src, dst) in enumerate(((vel_out_ref, vel_hbm), (pos_out_ref, pos_hbm), (wall_out_ref, wall_hbm))):
        copies.append(pltpu.make_async_copy(src, dst, sems.at[size_x + k]))
        copies[-1].start()
    for copy in copies:
        copy.wait()


def ring(count, step):
    return [(i, (i + step) % count) for i in range(count)]


def body(
    populations,
    solid,
    link_cell,
    link_dir,
    link_node,
    link_velocity,
    fabric_position,
    fabric_velocity,
    fabric_rest,
    triangles,
):
    size_x, size_y, size_z = populations.shape[1:]
    owners, capacity = link_node.shape[3:]
    nodes = fabric_position.shape[2]
    count_x, count_y, count_z = (lax.axis_size(name) for name in ("gx", "gy", "gz"))
    folded = (
        (count_y, count_z) == (4, 2)
        and (size_y, size_z) == (8, LANES)
        and owners * capacity == LANES
        and nodes == 4 * LANES
    )
    if not folded:
        return general_body(
            populations, solid, link_cell, link_dir, link_node, link_velocity,
            fabric_position, fabric_velocity, fabric_rest, triangles,
        )
    f32 = jnp.float32
    on_chip = pl.BlockSpec(memory_space=pltpu.VMEM)

    def shape(*dims):
        return jax.ShapeDtypeStruct(dims, f32)

    def kept(*dims):
        return pltpu.VMEM(dims, f32)

    def run(kernel, outs, *args):
        args = [pltpu.with_memory_space_constraint(arg, pltpu.VMEM) for arg in args]
        return pl.pallas_call(
            kernel,
            out_shape=outs,
            in_specs=[on_chip] * len(args),
            out_specs=jax.tree.map(lambda _: on_chip, outs),
            name=kernel.__name__,
        )(*args)

    face_x = kept(5, size_y, size_z)
    map_shape = kept(size_x, size_y, size_z)
    given = (
        populations, solid, link_cell, link_dir, link_node, link_velocity,
        fabric_position, fabric_velocity, fabric_rest, triangles,
    )
    cells = size_x * size_y
    opened = (kept(*populations.shape), face_x, face_x, kept(max(SEED, FAB + cells), LANES), map_shape, map_shape, kept(*fabric_position.shape))
    post, up, down, seed, kind, back, position = pl.pallas_call(
        open_kernel,
        out_shape=opened,
        in_specs=[pl.BlockSpec(memory_space=pl.ANY)] * len(given),
        out_specs=(on_chip,) * len(opened),
        scratch_shapes=[pltpu.VMEM(arg.shape, arg.dtype) for arg in given if arg is not fabric_position]
        + [pltpu.SemaphoreType.DMA((len(given),))],
        name="open_kernel",
    )(*given)
    swap_z = [(0, 1), (1, 0)]
    other = lax.ppermute(seed, "gz", swap_z)
    xlow = lax.ppermute(up, "gx", ring(count_x, 1))
    xhigh = lax.ppermute(down, "gx", ring(count_x, -1))
    (pair,) = run(pair_kernel, (kept(2 * FAB, LANES),), seed, other)
    cross = lax.ppermute(pair, "gy", [(y, y ^ 2) for y in range(count_y)])
    middling = []
    for y in range(count_y):
        to = y + 1 if y % 2 else y - 1
        for z in range(count_z):
            middling.append((y * 2 + z, to * 2 + z if 0 <= to < count_y else y * 2 + 1 - z))
    rows = -(-5 * size_x // 8) * 8
    middle, face, edge = run(
        sides_kernel, (kept(MID * rows, LANES), kept(rows, LANES), kept(size_y, LANES)), post, xlow, xhigh, other
    )
    middle = lax.ppermute(middle, ("gy", "gz"), middling)
    edge = lax.ppermute(edge, "gz", swap_z)
    (near,) = run(near_kernel, (kept(4 * FAB + rows, LANES),), pair, cross, face)
    near = lax.ppermute(near, "gy", [(y, y ^ 1) for y in range(count_y)])
    (rolled,) = run(shift_kernel, (kept(*populations.shape),), post, xlow, xhigh, other, edge)
    halves = (kept(32, LANES), kept(LANES, LANES), pltpu.VMEM((LANES, LANES), jnp.bfloat16))
    acc, column, at_lane = run(half_kernel, halves, seed, pair, cross)
    outs = (
        shape(*populations.shape),
        shape(*fabric_position.shape),
        shape(*fabric_velocity.shape),
        shape(*link_velocity.shape),
    )
    last = [rolled, kind, back, seed, acc, column, at_lane, near, middle, position]
    last = [pltpu.with_memory_space_constraint(arg, pltpu.VMEM) for arg in last]
    return pl.pallas_call(
        final_kernel,
        out_shape=outs,
        in_specs=[on_chip] * len(last),
        out_specs=(pl.BlockSpec(memory_space=pl.ANY),) * 4,
        scratch_shapes=[pltpu.VMEM(out.shape, f32) for out in outs] + [pltpu.SemaphoreType.DMA((size_x + 3,))],
        name="final_kernel",
    )(*last)


def solution(mesh):
    placed = (
        P(None, "gx", "gy", "gz"),
        P("gx", "gy", "gz"),
        P("gx", "gy", "gz", None, None),
        P("gx", "gy", "gz", None, None),
        P("gx", "gy", "gz", None, None),
        P("gx", "gy", "gz", None, None, None),
        P(None, "gx", ("gy", "gz")),
        P(None, "gx", ("gy", "gz")),
        P(None, "gx", ("gy", "gz")),
        P(None, "gx", ("gy", "gz")),
    )
    return jax.shard_map(
        body,
        mesh=mesh,
        in_specs=placed,
        out_specs=(
            P(None, "gx", "gy", "gz"),
            P(None, "gx", ("gy", "gz")),
            P(None, "gx", ("gy", "gz")),
            P("gx", "gy", "gz", None, None, None),
        ),
        check_vma=False,
    )
```

```python
import jax
import jax.numpy as jnp
import numpy as np
from jax import lax
from jax.experimental import pallas as pl
from jax.experimental.pallas import tpu as pltpu
from jax.sharding import PartitionSpec as P

SPRING = 0.5
DAMPING = 0.1
DIRECTIONS = [
    [0, 0, 0],
    [1, 0, 0],
    [-1, 0, 0],
    [0, 1, 0],
    [0, -1, 0],
    [0, 0, 1],
    [0, 0, -1],
    [1, 1, 0],
    [-1, -1, 0],
    [1, -1, 0],
    [-1, 1, 0],
    [1, 0, 1],
    [-1, 0, -1],
    [1, 0, -1],
    [-1, 0, 1],
    [0, 1, 1],
    [0, -1, -1],
    [0, 1, -1],
    [0, -1, 1],
]


def extended(cells, sides, width):
    for axis, dim in sides:
        count = lax.axis_size(axis)
        head = lax.slice_in_dim(cells, 0, width, axis=dim)
        tail = lax.slice_in_dim(cells, cells.shape[dim] - width, cells.shape[dim], axis=dim)
        cells = jnp.concatenate(
            [
                lax.ppermute(tail, axis, [(i, (i + 1) % count) for i in range(count)]),
                cells,
                lax.ppermute(head, axis, [((i + 1) % count, i) for i in range(count)]),
            ],
            axis=dim,
        )
    return cells


def lattice():
    velocity_np = np.array(DIRECTIONS)
    weight_np = np.array([1.0 / 3.0] + [1.0 / 18.0] * 6 + [1.0 / 36.0] * 12)
    opposite_list = [
        DIRECTIONS.index([-entry for entry in DIRECTIONS[direction]]) for direction in range(19)
    ]
    along_a = np.array([float(entry[0]) for entry in DIRECTIONS])
    along_b = np.array([float(entry[1]) for entry in DIRECTIONS])
    along_e = np.array([float(entry[2]) for entry in DIRECTIONS])
    speed_sq = along_a * along_a + along_b * along_b + along_e * along_e
    moment_rows = [
        np.ones(19),
        19 * speed_sq - 30,
        (21 * speed_sq * speed_sq - 53 * speed_sq + 24) / 2,
        along_a,
        (5 * speed_sq - 9) * along_a,
        along_b,
        (5 * speed_sq - 9) * along_b,
        along_e,
        (5 * speed_sq - 9) * along_e,
        3 * along_a * along_a - speed_sq,
        (3 * speed_sq - 5) * (3 * along_a * along_a - speed_sq),
        along_b * along_b - along_e * along_e,
        (3 * speed_sq - 5) * (along_b * along_b - along_e * along_e),
        along_a * along_b,
        along_b * along_e,
        along_a * along_e,
        (along_b * along_b - along_e * along_e) * along_a,
        (along_e * along_e - along_a * along_a) * along_b,
        (along_a * along_a - along_b * along_b) * along_e,
    ]
    moment_np = np.stack(moment_rows)
    inverse_np = moment_np.T / np.sum(moment_np * moment_np, axis=1)[None, :]
    viscous = 5.0 / 3.0
    rates_np = np.array(
        [
            0.0,
            1.19,
            1.4,
            0.0,
            1.2,
            0.0,
            1.2,
            0.0,
            1.2,
            viscous,
            1.4,
            viscous,
            1.4,
            viscous,
            viscous,
            viscous,
            1.98,
            1.98,
            1.98,
        ]
    )
    return (velocity_np, weight_np, opposite_list, moment_np, inverse_np, rates_np)


def collide_cells(popul, solid_flat):
    velocity_np, weight_np, opposite_list, moment_np, inverse_np, rates_np = lattice()
    velocity_table = jnp.asarray(velocity_np, jnp.float32)
    weight_table = jnp.asarray(weight_np, jnp.float32)
    density = jnp.sum(popul, axis=0)
    momentum = jnp.dot(
        velocity_table.T, popul, precision=lax.Precision.HIGHEST, preferred_element_type=jnp.float32
    )
    flow = momentum / density
    projected = jnp.dot(
        velocity_table, flow, precision=lax.Precision.HIGHEST, preferred_element_type=jnp.float32
    )
    speed_sq = jnp.sum(flow * flow, axis=0)
    equilibrium = (
        weight_table[:, None]
        * density
        * (1.0 + 3.0 * projected + 4.5 * projected * projected - 1.5 * speed_sq)
    )
    offset = popul - equilibrium
    moments = jnp.dot(
        jnp.asarray(moment_np, jnp.float32),
        offset,
        precision=lax.Precision.HIGHEST,
        preferred_element_type=jnp.float32,
    )
    relaxed = jnp.asarray(rates_np, jnp.float32)[:, None] * moments
    change = jnp.dot(
        jnp.asarray(inverse_np, jnp.float32),
        relaxed,
        precision=lax.Precision.HIGHEST,
        preferred_element_type=jnp.float32,
    )
    return jnp.where(solid_flat[None, :] == 1, popul, popul - change)


def fill_outside(padded, weight_np):
    span_y = padded.shape[2]
    span_z = padded.shape[3]
    place_y = lax.axis_index("gy")
    place_z = lax.axis_index("gz")
    count_y = lax.axis_size("gy")
    count_z = lax.axis_size("gz")
    rows_y = jnp.arange(span_y)
    rows_z = jnp.arange(span_z)
    out_y = (rows_y == 0) & (place_y == 0) | (rows_y == span_y - 1) & (place_y == count_y - 1)
    out_z = (rows_z == 0) & (place_z == 0) | (rows_z == span_z - 1) & (place_z == count_z - 1)
    outside = out_y[:, None] | out_z[None, :]
    return jnp.where(
        outside[None, None], jnp.asarray(weight_np, jnp.float32)[:, None, None, None], padded
    )


def propagate(padded, size_x, size_y, size_z):
    pieces = []
    for direction in range(19):
        shift_x = DIRECTIONS[direction][0]
        shift_y = DIRECTIONS[direction][1]
        shift_z = DIRECTIONS[direction][2]
        plane = padded[direction]
        pieces.append(
            lax.slice(
                plane,
                (1 - shift_x, 1 - shift_y, 1 - shift_z),
                (1 - shift_x + size_x, 1 - shift_y + size_y, 1 - shift_z + size_z),
            )
        )
    return jnp.stack(pieces)


def membrane(positions, rest, triangle_nodes):
    force = jnp.zeros(positions.shape, jnp.float32)
    for first, second in ((0, 1), (1, 2), (2, 0)):
        head = triangle_nodes[first]
        tail = triangle_nodes[second]
        stretch = positions[:, tail] - positions[:, head] - (rest[:, tail] - rest[:, head])
        force = force.at[:, head].add(SPRING * stretch)
        force = force.at[:, tail].add(-SPRING * stretch)
    return force


def general_body(
    populations,
    solid,
    link_cell,
    link_dir,
    link_node,
    link_velocity,
    fabric_position,
    fabric_velocity,
    fabric_rest,
    triangles,
):
    velocity_np, weight_np, opposite_list, moment_np, inverse_np, rates_np = lattice()
    velocity_table = jnp.asarray(velocity_np, jnp.float32)
    weight_table = jnp.asarray(weight_np, jnp.float32)
    opposite_table = jnp.asarray(opposite_list, jnp.int32)
    size_x = populations.shape[1]
    size_y = populations.shape[2]
    size_z = populations.shape[3]
    cells = size_x * size_y * size_z
    post = collide_cells(populations.reshape(19, cells), solid.reshape(cells)).reshape(
        populations.shape
    )
    padded = extended(post, (("gx", 1), ("gy", 2), ("gz", 3)), 1)
    padded = fill_outside(padded, weight_np)
    propagated = propagate(padded, size_x, size_y, size_z).reshape(19, cells)
    owners_n = link_node.shape[3]
    capacity = link_node.shape[4]
    node_rows = link_node.reshape(owners_n, capacity)
    cell_rows = link_cell.reshape(owners_n, capacity)
    dir_rows = link_dir.reshape(owners_n, capacity)
    live = node_rows >= 0
    post_flat = post.reshape(19, cells)
    reflected = post_flat[opposite_table[dir_rows], cell_rows]
    link_unit = velocity_table[dir_rows]
    wall = jnp.moveaxis(link_velocity.reshape(3, owners_n, capacity), 0, -1)
    returned = reflected + 6.0 * weight_table[dir_rows] * jnp.sum(link_unit * wall, axis=-1)
    populations_next = propagated.at[jnp.where(live, dir_rows, 19), cell_rows].set(
        returned, mode="drop"
    )
    strength = reflected + returned
    positions = fabric_position.reshape(3, -1)
    velocities = fabric_velocity.reshape(3, -1)
    rest = fabric_rest.reshape(3, -1)
    nodes_n = positions.shape[1]
    elastic = membrane(positions, rest, triangles.reshape(3, -1))
    link_force = jnp.moveaxis(-link_unit * strength[..., None], -1, 0)
    got_nodes, got_force = (
        lax.all_to_all(node_rows[None], ("gy", "gz"), split_axis=1, concat_axis=1, tiled=True),
        lax.all_to_all(link_force, ("gy", "gz"), split_axis=1, concat_axis=1, tiled=True),
    )
    got_ids = got_nodes[0]
    got_live = got_ids >= 0
    target = jnp.where(got_live, got_ids, nodes_n).reshape(-1)
    fluid_force = (
        jnp.zeros((3, nodes_n), jnp.float32)
        .at[:, target]
        .add(got_force.reshape(3, -1), mode="drop")
    )
    velocity_next = (1.0 - DAMPING) * velocities + (fluid_force + elastic)
    position_next = positions + velocity_next
    reply = jnp.where(got_live[None], velocity_next[:, jnp.where(got_live, got_ids, 0)], 0.0)
    wall_next = lax.all_to_all(reply, ("gy", "gz"), split_axis=1, concat_axis=1, tiled=True)
    return (
        populations_next.reshape(populations.shape),
        position_next.reshape(fabric_position.shape),
        velocity_next.reshape(fabric_velocity.shape),
        wall_next.reshape(link_velocity.shape),
    )


WEIGHTS = [1.0 / 3.0] + [1.0 / 18.0] * 6 + [1.0 / 36.0] * 12
OPPOSITE = [DIRECTIONS.index([-entry for entry in d]) for d in DIRECTIONS]
SIDES = [
    ([i for i in range(19) if DIRECTIONS[i][a] == 1], [i for i in range(19) if DIRECTIONS[i][a] == -1])
    for a in range(3)
]
LANES = 128
PATCH = 256
FAB = 16
SEED = 80
MID = 4


def iota(shape, axis):
    return lax.broadcasted_iota(jnp.int32, shape, axis)


def split3(value):
    high = value.astype(jnp.bfloat16).astype(jnp.float32)
    rest = value - high
    middle = rest.astype(jnp.bfloat16).astype(jnp.float32)
    return high, middle, rest - middle


def stacked3(value):
    return jnp.concatenate(split3(value), axis=0).astype(jnp.bfloat16)


def sum3(value):
    rows = value.shape[0] // 3
    return value[:rows] + value[rows : 2 * rows] + value[2 * rows :]


def dot_nn(left, right):
    return lax.dot_general(left, right, (((1,), (0,)), ((), ())), preferred_element_type=jnp.float32)


def dot_nt(left, right):
    return lax.dot_general(left, right, (((1,), (1,)), ((), ())), preferred_element_type=jnp.float32)


def one_hot(mask):
    return jnp.where(mask, 1.0, 0.0).astype(jnp.bfloat16)


def collided(f, solid):
    sx, dx = f[1] + f[2], f[1] - f[2]
    sy, dy = f[3] + f[4], f[3] - f[4]
    sz, dz = f[5] + f[6], f[5] - f[6]
    sa, da = f[7] + f[8], f[7] - f[8]
    sb, db = f[9] + f[10], f[9] - f[10]
    sc, dc = f[11] + f[12], f[11] - f[12]
    sd, dd = f[13] + f[14], f[13] - f[14]
    se, de = f[15] + f[16], f[15] - f[16]
    sg, dg = f[17] + f[18], f[17] - f[18]
    sxy, txy = sa + sb, sa - sb
    sxz, txz = sc + sd, sc - sd
    syz, tyz = se + sg, se - sg
    ax_ab, ay_ab = da + db, da - db
    ax_cd, az_cd = dc + dd, dc - dd
    ay_eg, az_eg = de + dg, de - dg
    near, far = sx + sy + sz, sxy + sxz + syz
    rho = f[0] + near + far
    ex, ey, ez = ax_ab + ax_cd, ay_ab + ay_eg, az_cd + az_eg
    jx, jy, jz = dx + ex, dy + ey, dz + ez
    inv = 1.0 / rho
    ux, uy, uz = jx * inv, jy * inv, jz * inv
    xx, yy, zz = jx * ux, jy * uy, jz * uz
    jj = xx + yy + zz
    energy = (-30.0 * f[0] - 11.0 * near + 8.0 * far) - (-11.0 * rho + 19.0 * jj)
    square = (12.0 * f[0] - 4.0 * near + far) - (3.0 * rho - 5.5 * jj)
    kx = (1.2 / 40.0) * (ex - 4.0 * dx + (2.0 / 3.0) * jx)
    ky = (1.2 / 40.0) * (ey - 4.0 * dy + (2.0 / 3.0) * jy)
    kz = (1.2 / 40.0) * (ez - 4.0 * dz + (2.0 / 3.0) * jz)
    yz_near, xyz_far = sy + sz, sxy + sxz - 2.0 * syz
    pxx_eq = 2.0 * xx - yy - zz
    pww_eq = yy - zz
    pxx = (5.0 / 3.0 / 36.0) * (2.0 * sx - yz_near + xyz_far - pxx_eq)
    pixx = (1.4 / 72.0) * (-4.0 * sx + 2.0 * yz_near + xyz_far + 0.5 * pxx_eq)
    w_near, w_far = sy - sz, sxy - sxz
    pww = (5.0 / 3.0 / 12.0) * (w_near + w_far - pww_eq)
    piww = (1.4 / 24.0) * (w_far - 2.0 * w_near + 0.5 * pww_eq)
    pxy = (5.0 / 3.0 / 4.0) * (txy - jx * uy)
    pyz = (5.0 / 3.0 / 4.0) * (tyz - jy * uz)
    pxz = (5.0 / 3.0 / 4.0) * (txz - jx * uz)
    mx = (1.98 / 8.0) * (ax_ab - ax_cd)
    my = (1.98 / 8.0) * (ay_eg - ay_ab)
    mz = (1.98 / 8.0) * (az_cd - az_eg)
    energy = (1.19 / 2394.0) * energy
    square = (1.4 / 252.0) * square
    axis = -11.0 * energy - 4.0 * square
    across = pxx - 2.0 * pixx
    split = pww - 2.0 * piww
    edge = 8.0 * energy + square
    pp, ww = pxx + pixx, pww + piww
    even = [
        axis + 2.0 * across,
        axis - across + split,
        axis - across - split,
        edge + pp + ww + pxy,
        edge + pp + ww - pxy,
        edge + pp - ww + pxz,
        edge + pp - ww - pxz,
        edge - 2.0 * pp + pyz,
        edge - 2.0 * pp - pyz,
    ]
    odd = [
        -4.0 * kx,
        -4.0 * ky,
        -4.0 * kz,
        (kx + mx) + (ky - my),
        (kx + mx) - (ky - my),
        (kx - mx) + (kz + mz),
        (kx - mx) - (kz + mz),
        (ky + my) + (kz - mz),
        (ky + my) - (kz - mz),
    ]
    change = [12.0 * square - 30.0 * energy]
    for pair in range(9):
        change += [even[pair] + odd[pair], even[pair] - odd[pair]]
    fluid = solid != 1
    return [jnp.where(fluid, f[i] - change[i], f[i]) for i in range(19)]


def slots_to_row(value):
    owners, capacity = value.shape
    wide = jnp.concatenate([value, jnp.zeros((owners, LANES - capacity), value.dtype)], axis=1)
    return jnp.sum(pltpu.roll(wide, 0, 1, stride=capacity, stride_axis=0), axis=0, keepdims=True)


def membrane_start(pos_ref, rest_ref, tri_ref):
    nodes = pos_ref.shape[2]
    count = tri_ref.shape[2]
    wide = -(-count // LANES) * LANES
    patches = nodes // PATCH
    stretch = [pos_ref[a] - rest_ref[a] for a in range(3)]
    corners = [
        jnp.concatenate([tri_ref[t], jnp.full((1, wide - count), -1, jnp.int32)], axis=1) for t in range(3)
    ]
    patch = jnp.maximum(corners[0], 0) // PATCH
    local = [(corner - patch * PATCH).astype(jnp.float32) for corner in corners]
    node_ids = iota((PATCH, LANES), 0).astype(jnp.float32).astype(jnp.bfloat16)
    blocks = []
    for k in range(0, wide, LANES):
        block = jnp.zeros((PATCH, LANES), jnp.bfloat16)
        for corner in local:
            row = jnp.broadcast_to(corner[:, k : k + LANES], (16, LANES)).astype(jnp.bfloat16)
            row = jnp.concatenate([row] * (PATCH // 16), axis=0)
            block = block + jnp.where(node_ids == row, jnp.ones_like(block), jnp.zeros_like(block))
        blocks.append(block)
    hits = jnp.concatenate(blocks, axis=1)
    stretch8 = jnp.concatenate(stretch + [jnp.zeros((5, nodes), jnp.float32)], axis=0)
    pieces = [stacked3(stretch8[:, p * PATCH : (p + 1) * PATCH]) for p in range(patches)]
    sums = dot_nn(jnp.concatenate(pieces, axis=0), hits)
    total = jnp.zeros((8, wide), jnp.float32)
    for p in range(patches):
        total = jnp.where(patch == p, sum3(sums[p * 24 : (p + 1) * 24]), total)
    return stretch, hits, total, patch


def membrane_finish(parts, vel_ref, fab_ref):
    stretch, hits, total, patch = parts
    nodes = vel_ref.shape[2]
    patches = nodes // PATCH
    total = jnp.where(iota(total.shape, 0) == 3, 1.0, total)
    pieces = [stacked3(jnp.where(patch == p, total, 0.0)) for p in range(patches)]
    sums = dot_nt(jnp.concatenate(pieces, axis=0), hits)
    back = jnp.concatenate([sum3(sums[p * 24 : (p + 1) * 24]) for p in range(patches)], axis=1)
    for a in range(3):
        elastic = SPRING * back[a : a + 1] - 3.0 * SPRING * back[3:4] * stretch[a]
        base = (1.0 - DAMPING) * vel_ref[a] + elastic
        for k in range(nodes // LANES):
            row = 4 + a * (nodes // LANES) + k
            fab_ref[row : row + 1] = base[:, k * LANES : (k + 1) * LANES]


def z_face(tiles):
    up = jnp.zeros_like(next(t for t in tiles if t is not None))
    lane = iota(up.shape, 1)
    down = up
    for k in range(5):
        i, j = SIDES[2][0][k], SIDES[2][1][k]
        if tiles[i] is not None:
            up = jnp.where(lane == k, pltpu.roll(tiles[i], k + 1, 1), up)
        if tiles[j] is not None:
            down = jnp.where(lane == k, pltpu.roll(tiles[j], k, 1) if k else tiles[j], down)
    return jnp.where(lax.axis_index("gz") == 0, up, down)


def z_shift(tile, i, face):
    lane = iota(tile.shape, 1)
    low_end = lax.axis_index("gz") == 0
    if DIRECTIONS[i][2] == 1:
        k = SIDES[2][0].index(i)
        halo = pltpu.roll(face, LANES - k, 1) if k else face
        return jnp.where(lane == 0, jnp.where(low_end, WEIGHTS[i], halo), pltpu.roll(tile, 1, 1))
    if DIRECTIONS[i][2] == -1:
        k = SIDES[2][1].index(i)
        halo = pltpu.roll(face, LANES - 1 - k, 1)
        return jnp.where(lane == LANES - 1, jnp.where(low_end, halo, WEIGHTS[i]), pltpu.roll(tile, LANES - 1, 1))
    return tile


def open_kernel(
    pop_hbm, solid_hbm, cell_hbm, dir_hbm, node_hbm, wall_hbm, pos_hbm, vel_hbm, rest_hbm, tri_hbm,
    post_ref, up_ref, down_ref, seed_ref, kind_ref, back_ref, pos_ref,
    pop_ref, solid_ref, cell_ref, dir_ref, node_ref, wall_ref, vel_ref, rest_ref, tri_ref, sems,
):
    moves = [
        (pop_hbm, pop_ref), (solid_hbm, solid_ref),
        (tri_hbm, tri_ref), (pos_hbm, pos_ref), (rest_hbm, rest_ref), (vel_hbm, vel_ref),
        (cell_hbm, cell_ref), (dir_hbm, dir_ref), (node_hbm, node_ref), (wall_hbm, wall_ref),
    ]
    copies = [pltpu.make_async_copy(src, dst, sems.at[k]) for k, (src, dst) in enumerate(moves)]
    for copy in copies[6:] + copies[2:6] + copies[:2]:
        copy.start()
    for copy in copies[2:]:
        copy.wait()
    parts = membrane_start(pos_ref, rest_ref, tri_ref)
    size_x, size_y = post_ref.shape[1:3]
    rows = size_x * size_y
    cell = slots_to_row(cell_ref[0, 0, 0].astype(jnp.float32)).astype(jnp.int32)
    way = slots_to_row(dir_ref[0, 0, 0].astype(jnp.float32))
    node = slots_to_row(node_ref[0, 0, 0].astype(jnp.float32))
    live = node >= 0.0
    unit = []
    for a in range(3):
        u = jnp.zeros_like(way)
        for i in range(1, 19):
            if DIRECTIONS[i][a]:
                u = jnp.where(way == float(i), float(DIRECTIONS[i][a]), u)
        unit.append(u)
    weight = jnp.where(way >= 7.0, 6.0 / 36.0, 6.0 / 18.0)
    wall = [slots_to_row(wall_ref[0, 0, 0, a]) for a in range(3)]
    term = weight * (unit[0] * wall[0] + unit[1] * wall[1] + unit[2] * wall[2])
    at_row = jnp.where((iota((rows, LANES), 0) == (cell >> 7)) & live, 1.0, 0.0)
    at_lane = one_hot(iota((LANES, LANES), 0) == (cell & (LANES - 1)))
    left = jnp.concatenate([at_row * way] + [at_row * t for t in split3(term)], axis=0)
    maps = dot_nt(left.astype(jnp.bfloat16), at_lane)
    kind = maps[:rows]
    added = sum3(maps[rows:])
    for copy in copies[:2]:
        copy.wait()
    taken = []
    membrane_finish(parts, vel_ref, seed_ref)
    for x in range(size_x):
        post = collided([pop_ref[i, x] for i in range(19)], solid_ref[x])
        k = kind[x * size_y : (x + 1) * size_y]
        t = jnp.zeros_like(k)
        for i in range(19):
            post_ref[i, x] = post[i]
            if x == size_x - 1 and i in SIDES[0][0]:
                up_ref[SIDES[0][0].index(i)] = post[i]
            if x == 0 and i in SIDES[0][1]:
                down_ref[SIDES[0][1].index(i)] = post[i]
            if i:
                t = jnp.where(k == float(OPPOSITE[i]), post[i], t)
        seed_ref[FAB + x * size_y : FAB + (x + 1) * size_y] = z_face(post)
        taken.append(t)
        kind_ref[x] = k
        back_ref[x] = t + added[x * size_y : (x + 1) * size_y]
    strength = 2.0 * jnp.concatenate(taken, axis=0) + added
    at_link = sum3(dot_nn(stacked3(strength), at_lane))
    push = jnp.sum(at_row * at_link, axis=0, keepdims=True)
    seed_ref[0:1] = node
    for a in range(3):
        seed_ref[1 + a : 2 + a] = -unit[a] * push
    end = FAB + rows
    seed_ref[end:] = jnp.zeros((seed_ref.shape[0] - end, LANES), jnp.float32)


def source_tile(post_ref, low_ref, high_ref, i, x):
    size_x = post_ref.shape[1]
    from_x = x - DIRECTIONS[i][0]
    if from_x < 0:
        return low_ref.at[SIDES[0][0].index(i)]
    if from_x >= size_x:
        return high_ref.at[SIDES[0][1].index(i)]
    return post_ref.at[i, from_x]


def pair_kernel(seed_ref, other_ref, pair_ref):
    low = lax.axis_index("gz") == 0
    pair_ref[:FAB] = jnp.where(low, seed_ref[:FAB], other_ref[:FAB])
    pair_ref[FAB:] = jnp.where(low, other_ref[:FAB], seed_ref[:FAB])


def edge_kernel(low_ref, high_ref, edge_ref):
    tiles = [None] * 19
    for i in range(19):
        if DIRECTIONS[i][0] and DIRECTIONS[i][2]:
            side = 0 if DIRECTIONS[i][0] == 1 else 1
            tiles[i] = (low_ref, high_ref)[side][SIDES[0][side].index(i)]
    edge_ref[...] = z_face(tiles)


def face_rows(post_ref, low_ref, high_ref, other_ref, out_ref, start, upward):
    size_x, size_y = post_ref.shape[1:3]
    for k in range(5):
        for x in range(size_x):
            at = start + k * size_x + x
            face = other_ref[FAB + x * size_y : FAB + (x + 1) * size_y]
            rows = []
            for side, row in ((0, size_y - 1), (1, 0)):
                i = SIDES[1][side][k]
                source = source_tile(post_ref, low_ref, high_ref, i, x)
                if DIRECTIONS[i][2]:
                    rows.append(z_shift(source[...], i, face)[row : row + 1])
                else:
                    rows.append(source[row : row + 1])
            out_ref[at : at + 1] = jnp.where(upward, rows[0], rows[1])
    end = start + 5 * size_x
    if out_ref.shape[0] > end:
        out_ref[end:] = jnp.zeros((out_ref.shape[0] - end, LANES), jnp.float32)


def middle_kernel(post_ref, low_ref, high_ref, other_ref, middle_ref):
    odd = lax.rem(lax.axis_index("gy"), 2) == 1
    face_rows(post_ref, low_ref, high_ref, other_ref, middle_ref, 0, odd)


def sides_kernel(post_ref, low_ref, high_ref, other_ref, middle_ref, face_ref, edge_ref):
    odd = lax.rem(lax.axis_index("gy"), 2) == 1
    face_rows(post_ref, low_ref, high_ref, other_ref, middle_ref, 0, odd)
    face_rows(post_ref, low_ref, high_ref, other_ref, face_ref, 0, jnp.logical_not(odd))
    edge_kernel(low_ref, high_ref, edge_ref)


def near_kernel(pair_ref, cross_ref, face_ref, near_ref):
    near_ref[: 2 * FAB] = pair_ref[...]
    near_ref[2 * FAB : 4 * FAB] = cross_ref[...]
    near_ref[4 * FAB :] = face_ref[...]


def shift_kernel(post_ref, low_ref, high_ref, other_ref, edge_ref, rolled_ref):
    size_x, size_y = post_ref.shape[1:3]
    for i in range(19):
        for x in range(size_x):
            tile = source_tile(post_ref, low_ref, high_ref, i, x)[...]
            from_x = x - DIRECTIONS[i][0]
            if 0 <= from_x < size_x:
                face = other_ref[FAB + from_x * size_y : FAB + (from_x + 1) * size_y]
            else:
                face = edge_ref[...]
            tile = z_shift(tile, i, face)
            if DIRECTIONS[i][1]:
                tile = pltpu.roll(tile, DIRECTIONS[i][1] % size_y, 0)
            rolled_ref[i, x] = tile


def fabric_part(pairs, chips, start, my_node, column, at_lane, nodes, capacity):
    parts = nodes // LANES
    me = lax.axis_index("gy") * 2 + lax.axis_index("gz")
    slot_owner = iota((1, LANES), 1) // capacity
    owner_base = (slot_owner * nodes).astype(jnp.float32)
    matches, forces, picked = [], [], jnp.zeros((8, LANES), jnp.float32)
    for m in range(2 * len(pairs)):
        tile = pairs[m // 2][m % 2 * FAB : m % 2 * FAB + 8]
        ids = tile[0:1]
        ids = jnp.where(ids >= 0.0, owner_base + ids, -1.0)
        matches.append(one_hot(column == ids))
        forces.append(tile)
        shift = lax.rem((start + m + LANES // capacity - me) * capacity, LANES)
        picked = jnp.where(slot_owner == start + m, pltpu.roll(tile, shift, 1), picked)
    pushed = sum3(dot_nt(stacked3(jnp.concatenate(forces, axis=1)), jnp.concatenate(matches, axis=1)))

    found = sum3(dot_nn(stacked3(jnp.concatenate(pairs, axis=0)), at_lane))
    row = iota((FAB, LANES), 0)
    fits = (row >= 4) & (row % parts == (my_node.astype(jnp.int32) >> 7))
    base = jnp.zeros((FAB, LANES), jnp.float32)
    for m in range(2 * len(pairs)):
        owner = chips[m // 2] * 2 + m % 2
        base = jnp.where(fits & (slot_owner == owner), found[m * FAB : (m + 1) * FAB], base)
    return jnp.concatenate([pushed, base, picked], axis=0)


def half_kernel(seed_ref, pair_ref, cross_ref, acc_ref, column_ref, lane_ref):
    place_y = lax.axis_index("gy")
    nodes, capacity = 4 * LANES, LANES // 8
    my_node = seed_ref[0:1]
    owner_base = (iota((1, LANES), 1) // capacity * nodes).astype(jnp.float32)
    my_id = jnp.where(my_node >= 0.0, owner_base + my_node, -2.0)
    column = jnp.transpose(jnp.broadcast_to(my_id, (LANES, LANES)))
    at_lane = one_hot(iota((LANES, LANES), 0) == (my_node.astype(jnp.int32) & (LANES - 1)))
    pairs, chips = [pair_ref[...], cross_ref[...]], [place_y, place_y ^ 2]
    acc_ref[...] = fabric_part(pairs, chips, 0, my_node, column, at_lane, nodes, capacity)
    column_ref[...] = column
    lane_ref[...] = at_lane


def final_kernel(
    rolled_ref, kind_ref, back_ref, seed_ref, acc_ref, column_ref, lane_ref, near_ref, middle_ref, pos_ref,
    pop_hbm, pos_hbm, vel_hbm, wall_hbm,
    pop_ref, pos_out_ref, vel_out_ref, wall_out_ref, sems,
):
    size_x, size_y = rolled_ref.shape[1:3]
    place_y = lax.axis_index("gy")
    odd = lax.rem(place_y, 2) == 1
    first, top = place_y == 0, place_y == lax.axis_size("gy") - 1
    sub = iota((size_y, LANES), 0)
    owners, capacity = wall_out_ref.shape[4], wall_out_ref.shape[5]
    nodes = pos_ref.shape[2]
    parts = nodes // LANES
    mine = seed_ref[:FAB]
    pairs, chips = [near_ref[: 2 * FAB], near_ref[2 * FAB : 4 * FAB]], [place_y ^ 1, place_y ^ 3]
    acc = fabric_part(pairs, chips, 4, mine[0:1], column_ref[...], lane_ref[...], nodes, capacity) + acc_ref[...]
    copies = []
    for x in range(size_x):
        kind = kind_ref[x]
        back = back_ref[x]
        for i in range(19):
            tile = rolled_ref[i, x]
            if DIRECTIONS[i][1]:
                side = 0 if DIRECTIONS[i][1] == 1 else 1
                at = SIDES[1][side].index(i) * size_x + x
                by_near = near_ref[4 * FAB + at : 4 * FAB + at + 1]
                by_middle = middle_ref[at : at + 1]
                if side == 0:
                    row = jnp.where(first, WEIGHTS[i], jnp.where(odd, by_near, by_middle))
                    tile = jnp.where(sub == 0, row, tile)
                else:
                    row = jnp.where(top, WEIGHTS[i], jnp.where(odd, by_middle, by_near))
                    tile = jnp.where(sub == size_y - 1, row, tile)
            if i:
                tile = jnp.where(kind == float(i), back, tile)
            pop_ref[i, x] = tile

    pushed, found, picked = acc[:8], acc[8:24], acc[24:32]
    node = picked[0:1].astype(jnp.int32)
    row = iota((FAB, LANES), 0)
    spread = jnp.where(row < parts, picked[1:2], jnp.where(row < 2 * parts, picked[2:3], picked[3:4]))
    spread = jnp.where((row < 3 * parts) & (row % parts == (node >> 7)), spread, 0.0)
    at_node = one_hot(iota((LANES, LANES), 0) == (node & (LANES - 1)))
    fluid = sum3(dot_nt(stacked3(spread), at_node))
    my_live = mine[0:1] >= 0.0
    moved = []
    for a in range(3):
        for k in range(parts):
            r = a * parts + k
            new = mine[4 + r : 5 + r] + fluid[r : r + 1]
            at = slice(k * LANES, (k + 1) * LANES)
            vel_out_ref[a, :, at] = new
            pos_out_ref[a, :, at] = pos_ref[a, :, at] + new
        base = jnp.sum(found[4 + a * parts : 4 + (a + 1) * parts], axis=0, keepdims=True)
        moved.append(jnp.where(my_live, base + pushed[1 + a : 2 + a], 0.0))
    moved = jnp.concatenate(moved + [jnp.zeros((5, LANES), jnp.float32)], axis=0)
    for o in range(owners):
        turned = pltpu.roll(moved, LANES - o * capacity, 1) if o else moved
        for a in range(3):
            wall_out_ref[0, 0, 0, a, o : o + 1] = turned[a : a + 1, :capacity]
    copies.append(pltpu.make_async_copy(pop_ref, pop_hbm, sems.at[0]))
    copies[-1].start()
    for k, (src, dst) in enumerate(((vel_out_ref, vel_hbm), (pos_out_ref, pos_hbm), (wall_out_ref, wall_hbm))):
        copies.append(pltpu.make_async_copy(src, dst, sems.at[size_x + k]))
        copies[-1].start()
    for copy in copies:
        copy.wait()


def ring(count, step):
    return [(i, (i + step) % count) for i in range(count)]


def body(
    populations,
    solid,
    link_cell,
    link_dir,
    link_node,
    link_velocity,
    fabric_position,
    fabric_velocity,
    fabric_rest,
    triangles,
):
    size_x, size_y, size_z = populations.shape[1:]
    owners, capacity = link_node.shape[3:]
    nodes = fabric_position.shape[2]
    count_x, count_y, count_z = (lax.axis_size(name) for name in ("gx", "gy", "gz"))
    folded = (
        (count_y, count_z) == (4, 2)
        and (size_y, size_z) == (8, LANES)
        and owners * capacity == LANES
        and nodes == 4 * LANES
    )
    if not folded:
        return general_body(
            populations, solid, link_cell, link_dir, link_node, link_velocity,
            fabric_position, fabric_velocity, fabric_rest, triangles,
        )
    f32 = jnp.float32
    on_chip = pl.BlockSpec(memory_space=pltpu.VMEM)

    def shape(*dims):
        return jax.ShapeDtypeStruct(dims, f32)

    def kept(*dims):
        return pltpu.VMEM(dims, f32)

    def run(kernel, outs, *args):
        args = [pltpu.with_memory_space_constraint(arg, pltpu.VMEM) for arg in args]
        return pl.pallas_call(
            kernel,
            out_shape=outs,
            in_specs=[on_chip] * len(args),
            out_specs=jax.tree.map(lambda _: on_chip, outs),
            name=kernel.__name__,
        )(*args)

    face_x = kept(5, size_y, size_z)
    map_shape = kept(size_x, size_y, size_z)
    given = (
        populations, solid, link_cell, link_dir, link_node, link_velocity,
        fabric_position, fabric_velocity, fabric_rest, triangles,
    )
    cells = size_x * size_y
    opened = (kept(*populations.shape), face_x, face_x, kept(max(SEED, FAB + cells), LANES), map_shape, map_shape, kept(*fabric_position.shape))
    post, up, down, seed, kind, back, position = pl.pallas_call(
        open_kernel,
        out_shape=opened,
        in_specs=[pl.BlockSpec(memory_space=pl.ANY)] * len(given),
        out_specs=(on_chip,) * len(opened),
        scratch_shapes=[pltpu.VMEM(arg.shape, arg.dtype) for arg in given if arg is not fabric_position]
        + [pltpu.SemaphoreType.DMA((len(given),))],
        name="open_kernel",
    )(*given)
    swap_z = [(0, 1), (1, 0)]
    other = lax.ppermute(seed, "gz", swap_z)
    xlow = lax.ppermute(up, "gx", ring(count_x, 1))
    xhigh = lax.ppermute(down, "gx", ring(count_x, -1))
    (pair,) = run(pair_kernel, (kept(2 * FAB, LANES),), seed, other)
    cross = lax.ppermute(pair, "gy", [(y, y ^ 2) for y in range(count_y)])
    middling = []
    for y in range(count_y):
        to = y + 1 if y % 2 else y - 1
        for z in range(count_z):
            middling.append((y * 2 + z, to * 2 + z if 0 <= to < count_y else y * 2 + 1 - z))
    rows = -(-5 * size_x // 8) * 8
    middle, face, edge = run(
        sides_kernel, (kept(MID * rows, LANES), kept(rows, LANES), kept(size_y, LANES)), post, xlow, xhigh, other
    )
    middle = lax.ppermute(middle, ("gy", "gz"), middling)
    edge = lax.ppermute(edge, "gz", swap_z)
    (near,) = run(near_kernel, (kept(4 * FAB + rows, LANES),), pair, cross, face)
    near = lax.ppermute(near, "gy", [(y, y ^ 1) for y in range(count_y)])
    (rolled,) = run(shift_kernel, (kept(*populations.shape),), post, xlow, xhigh, other, edge)
    halves = (kept(32, LANES), kept(LANES, LANES), pltpu.VMEM((LANES, LANES), jnp.bfloat16))
    acc, column, at_lane = run(half_kernel, halves, seed, pair, cross)
    outs = (
        shape(*populations.shape),
        shape(*fabric_position.shape),
        shape(*fabric_velocity.shape),
        shape(*link_velocity.shape),
    )
    last = [rolled, kind, back, seed, acc, column, at_lane, near, middle, position]
    last = [pltpu.with_memory_space_constraint(arg, pltpu.VMEM) for arg in last]
    return pl.pallas_call(
        final_kernel,
        out_shape=outs,
        in_specs=[on_chip] * len(last),
        out_specs=(pl.BlockSpec(memory_space=pl.ANY),) * 4,
        scratch_shapes=[pltpu.VMEM(out.shape, f32) for out in outs] + [pltpu.SemaphoreType.DMA((size_x + 3,))],
        name="final_kernel",
    )(*last)


def solution(mesh):
    placed = (
        P(None, "gx", "gy", "gz"),
        P("gx", "gy", "gz"),
        P("gx", "gy", "gz", None, None),
        P("gx", "gy", "gz", None, None),
        P("gx", "gy", "gz", None, None),
        P("gx", "gy", "gz", None, None, None),
        P(None, "gx", ("gy", "gz")),
        P(None, "gx", ("gy", "gz")),
        P(None, "gx", ("gy", "gz")),
        P(None, "gx", ("gy", "gz")),
    )
    return jax.shard_map(
        body,
        mesh=mesh,
        in_specs=placed,
        out_specs=(
            P(None, "gx", "gy", "gz"),
            P(None, "gx", ("gy", "gz")),
            P(None, "gx", ("gy", "gz")),
            P("gx", "gy", "gz", None, None, None),
        ),
        check_vma=False,
    )
```

```python
import jax
import jax.numpy as jnp
import numpy as np
from jax import lax
from jax.experimental import pallas as pl
from jax.experimental.pallas import tpu as pltpu
from jax.sharding import PartitionSpec as P

SPRING = 0.5
DAMPING = 0.1
DIRECTIONS = [
    [0, 0, 0],
    [1, 0, 0],
    [-1, 0, 0],
    [0, 1, 0],
    [0, -1, 0],
    [0, 0, 1],
    [0, 0, -1],
    [1, 1, 0],
    [-1, -1, 0],
    [1, -1, 0],
    [-1, 1, 0],
    [1, 0, 1],
    [-1, 0, -1],
    [1, 0, -1],
    [-1, 0, 1],
    [0, 1, 1],
    [0, -1, -1],
    [0, 1, -1],
    [0, -1, 1],
]


def extended(cells, sides, width):
    for axis, dim in sides:
        count = lax.axis_size(axis)
        head = lax.slice_in_dim(cells, 0, width, axis=dim)
        tail = lax.slice_in_dim(cells, cells.shape[dim] - width, cells.shape[dim], axis=dim)
        cells = jnp.concatenate(
            [
                lax.ppermute(tail, axis, [(i, (i + 1) % count) for i in range(count)]),
                cells,
                lax.ppermute(head, axis, [((i + 1) % count, i) for i in range(count)]),
            ],
            axis=dim,
        )
    return cells


def lattice():
    velocity_np = np.array(DIRECTIONS)
    weight_np = np.array([1.0 / 3.0] + [1.0 / 18.0] * 6 + [1.0 / 36.0] * 12)
    opposite_list = [
        DIRECTIONS.index([-entry for entry in DIRECTIONS[direction]]) for direction in range(19)
    ]
    along_a = np.array([float(entry[0]) for entry in DIRECTIONS])
    along_b = np.array([float(entry[1]) for entry in DIRECTIONS])
    along_e = np.array([float(entry[2]) for entry in DIRECTIONS])
    speed_sq = along_a * along_a + along_b * along_b + along_e * along_e
    moment_rows = [
        np.ones(19),
        19 * speed_sq - 30,
        (21 * speed_sq * speed_sq - 53 * speed_sq + 24) / 2,
        along_a,
        (5 * speed_sq - 9) * along_a,
        along_b,
        (5 * speed_sq - 9) * along_b,
        along_e,
        (5 * speed_sq - 9) * along_e,
        3 * along_a * along_a - speed_sq,
        (3 * speed_sq - 5) * (3 * along_a * along_a - speed_sq),
        along_b * along_b - along_e * along_e,
        (3 * speed_sq - 5) * (along_b * along_b - along_e * along_e),
        along_a * along_b,
        along_b * along_e,
        along_a * along_e,
        (along_b * along_b - along_e * along_e) * along_a,
        (along_e * along_e - along_a * along_a) * along_b,
        (along_a * along_a - along_b * along_b) * along_e,
    ]
    moment_np = np.stack(moment_rows)
    inverse_np = moment_np.T / np.sum(moment_np * moment_np, axis=1)[None, :]
    viscous = 5.0 / 3.0
    rates_np = np.array(
        [
            0.0,
            1.19,
            1.4,
            0.0,
            1.2,
            0.0,
            1.2,
            0.0,
            1.2,
            viscous,
            1.4,
            viscous,
            1.4,
            viscous,
            viscous,
            viscous,
            1.98,
            1.98,
            1.98,
        ]
    )
    return (velocity_np, weight_np, opposite_list, moment_np, inverse_np, rates_np)


def collide_cells(popul, solid_flat):
    velocity_np, weight_np, opposite_list, moment_np, inverse_np, rates_np = lattice()
    velocity_table = jnp.asarray(velocity_np, jnp.float32)
    weight_table = jnp.asarray(weight_np, jnp.float32)
    density = jnp.sum(popul, axis=0)
    momentum = jnp.dot(
        velocity_table.T, popul, precision=lax.Precision.HIGHEST, preferred_element_type=jnp.float32
    )
    flow = momentum / density
    projected = jnp.dot(
        velocity_table, flow, precision=lax.Precision.HIGHEST, preferred_element_type=jnp.float32
    )
    speed_sq = jnp.sum(flow * flow, axis=0)
    equilibrium = (
        weight_table[:, None]
        * density
        * (1.0 + 3.0 * projected + 4.5 * projected * projected - 1.5 * speed_sq)
    )
    offset = popul - equilibrium
    moments = jnp.dot(
        jnp.asarray(moment_np, jnp.float32),
        offset,
        precision=lax.Precision.HIGHEST,
        preferred_element_type=jnp.float32,
    )
    relaxed = jnp.asarray(rates_np, jnp.float32)[:, None] * moments
    change = jnp.dot(
        jnp.asarray(inverse_np, jnp.float32),
        relaxed,
        precision=lax.Precision.HIGHEST,
        preferred_element_type=jnp.float32,
    )
    return jnp.where(solid_flat[None, :] == 1, popul, popul - change)


def fill_outside(padded, weight_np):
    span_y = padded.shape[2]
    span_z = padded.shape[3]
    place_y = lax.axis_index("gy")
    place_z = lax.axis_index("gz")
    count_y = lax.axis_size("gy")
    count_z = lax.axis_size("gz")
    rows_y = jnp.arange(span_y)
    rows_z = jnp.arange(span_z)
    out_y = (rows_y == 0) & (place_y == 0) | (rows_y == span_y - 1) & (place_y == count_y - 1)
    out_z = (rows_z == 0) & (place_z == 0) | (rows_z == span_z - 1) & (place_z == count_z - 1)
    outside = out_y[:, None] | out_z[None, :]
    return jnp.where(
        outside[None, None], jnp.asarray(weight_np, jnp.float32)[:, None, None, None], padded
    )


def propagate(padded, size_x, size_y, size_z):
    pieces = []
    for direction in range(19):
        shift_x = DIRECTIONS[direction][0]
        shift_y = DIRECTIONS[direction][1]
        shift_z = DIRECTIONS[direction][2]
        plane = padded[direction]
        pieces.append(
            lax.slice(
                plane,
                (1 - shift_x, 1 - shift_y, 1 - shift_z),
                (1 - shift_x + size_x, 1 - shift_y + size_y, 1 - shift_z + size_z),
            )
        )
    return jnp.stack(pieces)


def membrane(positions, rest, triangle_nodes):
    force = jnp.zeros(positions.shape, jnp.float32)
    for first, second in ((0, 1), (1, 2), (2, 0)):
        head = triangle_nodes[first]
        tail = triangle_nodes[second]
        stretch = positions[:, tail] - positions[:, head] - (rest[:, tail] - rest[:, head])
        force = force.at[:, head].add(SPRING * stretch)
        force = force.at[:, tail].add(-SPRING * stretch)
    return force


def general_body(
    populations,
    solid,
    link_cell,
    link_dir,
    link_node,
    link_velocity,
    fabric_position,
    fabric_velocity,
    fabric_rest,
    triangles,
):
    velocity_np, weight_np, opposite_list, moment_np, inverse_np, rates_np = lattice()
    velocity_table = jnp.asarray(velocity_np, jnp.float32)
    weight_table = jnp.asarray(weight_np, jnp.float32)
    opposite_table = jnp.asarray(opposite_list, jnp.int32)
    size_x = populations.shape[1]
    size_y = populations.shape[2]
    size_z = populations.shape[3]
    cells = size_x * size_y * size_z
    post = collide_cells(populations.reshape(19, cells), solid.reshape(cells)).reshape(
        populations.shape
    )
    padded = extended(post, (("gx", 1), ("gy", 2), ("gz", 3)), 1)
    padded = fill_outside(padded, weight_np)
    propagated = propagate(padded, size_x, size_y, size_z).reshape(19, cells)
    owners_n = link_node.shape[3]
    capacity = link_node.shape[4]
    node_rows = link_node.reshape(owners_n, capacity)
    cell_rows = link_cell.reshape(owners_n, capacity)
    dir_rows = link_dir.reshape(owners_n, capacity)
    live = node_rows >= 0
    post_flat = post.reshape(19, cells)
    reflected = post_flat[opposite_table[dir_rows], cell_rows]
    link_unit = velocity_table[dir_rows]
    wall = jnp.moveaxis(link_velocity.reshape(3, owners_n, capacity), 0, -1)
    returned = reflected + 6.0 * weight_table[dir_rows] * jnp.sum(link_unit * wall, axis=-1)
    populations_next = propagated.at[jnp.where(live, dir_rows, 19), cell_rows].set(
        returned, mode="drop"
    )
    strength = reflected + returned
    positions = fabric_position.reshape(3, -1)
    velocities = fabric_velocity.reshape(3, -1)
    rest = fabric_rest.reshape(3, -1)
    nodes_n = positions.shape[1]
    elastic = membrane(positions, rest, triangles.reshape(3, -1))
    link_force = jnp.moveaxis(-link_unit * strength[..., None], -1, 0)
    got_nodes, got_force = (
        lax.all_to_all(node_rows[None], ("gy", "gz"), split_axis=1, concat_axis=1, tiled=True),
        lax.all_to_all(link_force, ("gy", "gz"), split_axis=1, concat_axis=1, tiled=True),
    )
    got_ids = got_nodes[0]
    got_live = got_ids >= 0
    target = jnp.where(got_live, got_ids, nodes_n).reshape(-1)
    fluid_force = (
        jnp.zeros((3, nodes_n), jnp.float32)
        .at[:, target]
        .add(got_force.reshape(3, -1), mode="drop")
    )
    velocity_next = (1.0 - DAMPING) * velocities + (fluid_force + elastic)
    position_next = positions + velocity_next
    reply = jnp.where(got_live[None], velocity_next[:, jnp.where(got_live, got_ids, 0)], 0.0)
    wall_next = lax.all_to_all(reply, ("gy", "gz"), split_axis=1, concat_axis=1, tiled=True)
    return (
        populations_next.reshape(populations.shape),
        position_next.reshape(fabric_position.shape),
        velocity_next.reshape(fabric_velocity.shape),
        wall_next.reshape(link_velocity.shape),
    )


WEIGHTS = [1.0 / 3.0] + [1.0 / 18.0] * 6 + [1.0 / 36.0] * 12
OPPOSITE = [DIRECTIONS.index([-entry for entry in d]) for d in DIRECTIONS]
SIDES = [
    ([i for i in range(19) if DIRECTIONS[i][a] == 1], [i for i in range(19) if DIRECTIONS[i][a] == -1])
    for a in range(3)
]
LANES = 128
PATCH = 256
FAB = 16
SEED = 80
MID = 4


def iota(shape, axis):
    return lax.broadcasted_iota(jnp.int32, shape, axis)


def split3(value):
    high = value.astype(jnp.bfloat16).astype(jnp.float32)
    rest = value - high
    middle = rest.astype(jnp.bfloat16).astype(jnp.float32)
    return high, middle, rest - middle


def stacked3(value):
    return jnp.concatenate(split3(value), axis=0).astype(jnp.bfloat16)


def sum3(value):
    rows = value.shape[0] // 3
    return value[:rows] + value[rows : 2 * rows] + value[2 * rows :]


def dot_nn(left, right):
    return lax.dot_general(left, right, (((1,), (0,)), ((), ())), preferred_element_type=jnp.float32)


def dot_nt(left, right):
    return lax.dot_general(left, right, (((1,), (1,)), ((), ())), preferred_element_type=jnp.float32)


def one_hot(mask):
    return jnp.where(mask, 1.0, 0.0).astype(jnp.bfloat16)


def collided(f, solid):
    sx, dx = f[1] + f[2], f[1] - f[2]
    sy, dy = f[3] + f[4], f[3] - f[4]
    sz, dz = f[5] + f[6], f[5] - f[6]
    sa, da = f[7] + f[8], f[7] - f[8]
    sb, db = f[9] + f[10], f[9] - f[10]
    sc, dc = f[11] + f[12], f[11] - f[12]
    sd, dd = f[13] + f[14], f[13] - f[14]
    se, de = f[15] + f[16], f[15] - f[16]
    sg, dg = f[17] + f[18], f[17] - f[18]
    sxy, txy = sa + sb, sa - sb
    sxz, txz = sc + sd, sc - sd
    syz, tyz = se + sg, se - sg
    ax_ab, ay_ab = da + db, da - db
    ax_cd, az_cd = dc + dd, dc - dd
    ay_eg, az_eg = de + dg, de - dg
    near, far = sx + sy + sz, sxy + sxz + syz
    rho = f[0] + near + far
    ex, ey, ez = ax_ab + ax_cd, ay_ab + ay_eg, az_cd + az_eg
    jx, jy, jz = dx + ex, dy + ey, dz + ez
    inv = 1.0 / rho
    ux, uy, uz = jx * inv, jy * inv, jz * inv
    xx, yy, zz = jx * ux, jy * uy, jz * uz
    jj = xx + yy + zz
    energy = (-30.0 * f[0] - 11.0 * near + 8.0 * far) - (-11.0 * rho + 19.0 * jj)
    square = (12.0 * f[0] - 4.0 * near + far) - (3.0 * rho - 5.5 * jj)
    kx = (1.2 / 40.0) * (ex - 4.0 * dx + (2.0 / 3.0) * jx)
    ky = (1.2 / 40.0) * (ey - 4.0 * dy + (2.0 / 3.0) * jy)
    kz = (1.2 / 40.0) * (ez - 4.0 * dz + (2.0 / 3.0) * jz)
    yz_near, xyz_far = sy + sz, sxy + sxz - 2.0 * syz
    pxx_eq = 2.0 * xx - yy - zz
    pww_eq = yy - zz
    pxx = (5.0 / 3.0 / 36.0) * (2.0 * sx - yz_near + xyz_far - pxx_eq)
    pixx = (1.4 / 72.0) * (-4.0 * sx + 2.0 * yz_near + xyz_far + 0.5 * pxx_eq)
    w_near, w_far = sy - sz, sxy - sxz
    pww = (5.0 / 3.0 / 12.0) * (w_near + w_far - pww_eq)
    piww = (1.4 / 24.0) * (w_far - 2.0 * w_near + 0.5 * pww_eq)
    pxy = (5.0 / 3.0 / 4.0) * (txy - jx * uy)
    pyz = (5.0 / 3.0 / 4.0) * (tyz - jy * uz)
    pxz = (5.0 / 3.0 / 4.0) * (txz - jx * uz)
    mx = (1.98 / 8.0) * (ax_ab - ax_cd)
    my = (1.98 / 8.0) * (ay_eg - ay_ab)
    mz = (1.98 / 8.0) * (az_cd - az_eg)
    energy = (1.19 / 2394.0) * energy
    square = (1.4 / 252.0) * square
    axis = -11.0 * energy - 4.0 * square
    across = pxx - 2.0 * pixx
    split = pww - 2.0 * piww
    edge = 8.0 * energy + square
    pp, ww = pxx + pixx, pww + piww
    even = [
        axis + 2.0 * across,
        axis - across + split,
        axis - across - split,
        edge + pp + ww + pxy,
        edge + pp + ww - pxy,
        edge + pp - ww + pxz,
        edge + pp - ww - pxz,
        edge - 2.0 * pp + pyz,
        edge - 2.0 * pp - pyz,
    ]
    odd = [
        -4.0 * kx,
        -4.0 * ky,
        -4.0 * kz,
        (kx + mx) + (ky - my),
        (kx + mx) - (ky - my),
        (kx - mx) + (kz + mz),
        (kx - mx) - (kz + mz),
        (ky + my) + (kz - mz),
        (ky + my) - (kz - mz),
    ]
    change = [12.0 * square - 30.0 * energy]
    for pair in range(9):
        change += [even[pair] + odd[pair], even[pair] - odd[pair]]
    fluid = solid != 1
    return [jnp.where(fluid, f[i] - change[i], f[i]) for i in range(19)]


def slots_to_row(value):
    owners, capacity = value.shape
    wide = jnp.concatenate([value, jnp.zeros((owners, LANES - capacity), value.dtype)], axis=1)
    return jnp.sum(pltpu.roll(wide, 0, 1, stride=capacity, stride_axis=0), axis=0, keepdims=True)


def membrane_start(pos_ref, rest_ref, tri_ref):
    nodes = pos_ref.shape[2]
    count = tri_ref.shape[2]
    wide = -(-count // LANES) * LANES
    patches = nodes // PATCH
    stretch = [pos_ref[a] - rest_ref[a] for a in range(3)]
    corners = [
        jnp.concatenate([tri_ref[t], jnp.full((1, wide - count), -1, jnp.int32)], axis=1) for t in range(3)
    ]
    patch = jnp.maximum(corners[0], 0) // PATCH
    local = [(corner - patch * PATCH).astype(jnp.float32) for corner in corners]
    node_ids = iota((PATCH, LANES), 0).astype(jnp.float32).astype(jnp.bfloat16)
    blocks = []
    for k in range(0, wide, LANES):
        block = jnp.zeros((PATCH, LANES), jnp.bfloat16)
        for corner in local:
            row = jnp.broadcast_to(corner[:, k : k + LANES], (16, LANES)).astype(jnp.bfloat16)
            row = jnp.concatenate([row] * (PATCH // 16), axis=0)
            block = block + jnp.where(node_ids == row, jnp.ones_like(block), jnp.zeros_like(block))
        blocks.append(block)
    hits = jnp.concatenate(blocks, axis=1)
    stretch8 = jnp.concatenate(stretch + [jnp.zeros((5, nodes), jnp.float32)], axis=0)
    pieces = [stacked3(stretch8[:, p * PATCH : (p + 1) * PATCH]) for p in range(patches)]
    sums = dot_nn(jnp.concatenate(pieces, axis=0), hits)
    total = jnp.zeros((8, wide), jnp.float32)
    for p in range(patches):
        total = jnp.where(patch == p, sum3(sums[p * 24 : (p + 1) * 24]), total)
    return stretch, hits, total, patch


def membrane_finish(parts, vel_ref, fab_ref):
    stretch, hits, total, patch = parts
    nodes = vel_ref.shape[2]
    patches = nodes // PATCH
    total = jnp.where(iota(total.shape, 0) == 3, 1.0, total)
    pieces = [stacked3(jnp.where(patch == p, total, 0.0)) for p in range(patches)]
    sums = dot_nt(jnp.concatenate(pieces, axis=0), hits)
    back = jnp.concatenate([sum3(sums[p * 24 : (p + 1) * 24]) for p in range(patches)], axis=1)
    for a in range(3):
        elastic = SPRING * back[a : a + 1] - 3.0 * SPRING * back[3:4] * stretch[a]
        base = (1.0 - DAMPING) * vel_ref[a] + elastic
        for k in range(nodes // LANES):
            row = 4 + a * (nodes // LANES) + k
            fab_ref[row : row + 1] = base[:, k * LANES : (k + 1) * LANES]


def z_face(tiles):
    up = jnp.zeros_like(next(t for t in tiles if t is not None))
    lane = iota(up.shape, 1)
    down = up
    for k in range(5):
        i, j = SIDES[2][0][k], SIDES[2][1][k]
        if tiles[i] is not None:
            up = jnp.where(lane == k, pltpu.roll(tiles[i], k + 1, 1), up)
        if tiles[j] is not None:
            down = jnp.where(lane == k, pltpu.roll(tiles[j], k, 1) if k else tiles[j], down)
    return jnp.where(lax.axis_index("gz") == 0, up, down)


def z_shift(tile, i, face):
    lane = iota(tile.shape, 1)
    low_end = lax.axis_index("gz") == 0
    if DIRECTIONS[i][2] == 1:
        k = SIDES[2][0].index(i)
        halo = pltpu.roll(face, LANES - k, 1) if k else face
        return jnp.where(lane == 0, jnp.where(low_end, WEIGHTS[i], halo), pltpu.roll(tile, 1, 1))
    if DIRECTIONS[i][2] == -1:
        k = SIDES[2][1].index(i)
        halo = pltpu.roll(face, LANES - 1 - k, 1)
        return jnp.where(lane == LANES - 1, jnp.where(low_end, halo, WEIGHTS[i]), pltpu.roll(tile, LANES - 1, 1))
    return tile


def open_kernel(
    pop_hbm, solid_hbm, cell_hbm, dir_hbm, node_hbm, wall_hbm, pos_hbm, vel_hbm, rest_hbm, tri_hbm,
    post_ref, up_ref, down_ref, seed_ref, kind_ref, back_ref, pos_ref,
    pop_ref, solid_ref, cell_ref, dir_ref, node_ref, wall_ref, vel_ref, rest_ref, tri_ref, sems,
):
    moves = [
        (pop_hbm, pop_ref), (solid_hbm, solid_ref),
        (tri_hbm, tri_ref), (pos_hbm, pos_ref), (rest_hbm, rest_ref), (vel_hbm, vel_ref),
        (cell_hbm, cell_ref), (dir_hbm, dir_ref), (node_hbm, node_ref), (wall_hbm, wall_ref),
    ]
    copies = [pltpu.make_async_copy(src, dst, sems.at[k]) for k, (src, dst) in enumerate(moves)]
    for copy in copies[6:] + copies[2:6] + copies[:2]:
        copy.start()
    for copy in copies[2:]:
        copy.wait()
    parts = membrane_start(pos_ref, rest_ref, tri_ref)
    size_x, size_y = post_ref.shape[1:3]
    rows = size_x * size_y
    cell = slots_to_row(cell_ref[0, 0, 0].astype(jnp.float32)).astype(jnp.int32)
    way = slots_to_row(dir_ref[0, 0, 0].astype(jnp.float32))
    node = slots_to_row(node_ref[0, 0, 0].astype(jnp.float32))
    live = node >= 0.0
    unit = []
    for a in range(3):
        u = jnp.zeros_like(way)
        for i in range(1, 19):
            if DIRECTIONS[i][a]:
                u = jnp.where(way == float(i), float(DIRECTIONS[i][a]), u)
        unit.append(u)
    weight = jnp.where(way >= 7.0, 6.0 / 36.0, 6.0 / 18.0)
    wall = [slots_to_row(wall_ref[0, 0, 0, a]) for a in range(3)]
    term = weight * (unit[0] * wall[0] + unit[1] * wall[1] + unit[2] * wall[2])
    at_row = jnp.where((iota((rows, LANES), 0) == (cell >> 7)) & live, 1.0, 0.0)
    at_lane = one_hot(iota((LANES, LANES), 0) == (cell & (LANES - 1)))
    left = jnp.concatenate([at_row * way] + [at_row * t for t in split3(term)], axis=0)
    maps = dot_nt(left.astype(jnp.bfloat16), at_lane)
    kind = maps[:rows]
    added = sum3(maps[rows:])
    for copy in copies[:2]:
        copy.wait()
    taken = []
    membrane_finish(parts, vel_ref, seed_ref)
    for x in range(size_x):
        post = collided([pop_ref[i, x] for i in range(19)], solid_ref[x])
        k = kind[x * size_y : (x + 1) * size_y]
        t = jnp.zeros_like(k)
        for i in range(19):
            post_ref[i, x] = post[i]
            if x == size_x - 1 and i in SIDES[0][0]:
                up_ref[SIDES[0][0].index(i)] = post[i]
            if x == 0 and i in SIDES[0][1]:
                down_ref[SIDES[0][1].index(i)] = post[i]
            if i:
                t = jnp.where(k == float(OPPOSITE[i]), post[i], t)
        seed_ref[FAB + x * size_y : FAB + (x + 1) * size_y] = z_face(post)
        taken.append(t)
        kind_ref[x] = k
        back_ref[x] = t + added[x * size_y : (x + 1) * size_y]
    strength = 2.0 * jnp.concatenate(taken, axis=0) + added
    at_link = sum3(dot_nn(stacked3(strength), at_lane))
    push = jnp.sum(at_row * at_link, axis=0, keepdims=True)
    seed_ref[0:1] = node
    for a in range(3):
        seed_ref[1 + a : 2 + a] = -unit[a] * push
    end = FAB + rows
    seed_ref[end:] = jnp.zeros((seed_ref.shape[0] - end, LANES), jnp.float32)


def source_tile(post_ref, low_ref, high_ref, i, x):
    size_x = post_ref.shape[1]
    from_x = x - DIRECTIONS[i][0]
    if from_x < 0:
        return low_ref.at[SIDES[0][0].index(i)]
    if from_x >= size_x:
        return high_ref.at[SIDES[0][1].index(i)]
    return post_ref.at[i, from_x]


def pair_kernel(seed_ref, other_ref, pair_ref):
    low = lax.axis_index("gz") == 0
    pair_ref[:FAB] = jnp.where(low, seed_ref[:FAB], other_ref[:FAB])
    pair_ref[FAB:] = jnp.where(low, other_ref[:FAB], seed_ref[:FAB])


def edge_kernel(low_ref, high_ref, edge_ref):
    tiles = [None] * 19
    for i in range(19):
        if DIRECTIONS[i][0] and DIRECTIONS[i][2]:
            side = 0 if DIRECTIONS[i][0] == 1 else 1
            tiles[i] = (low_ref, high_ref)[side][SIDES[0][side].index(i)]
    edge_ref[...] = z_face(tiles)


def face_rows(post_ref, low_ref, high_ref, other_ref, out_ref, start, upward):
    size_x, size_y = post_ref.shape[1:3]
    for k in range(5):
        for x in range(size_x):
            at = start + k * size_x + x
            face = other_ref[FAB + x * size_y : FAB + (x + 1) * size_y]
            rows = []
            for side, row in ((0, size_y - 1), (1, 0)):
                i = SIDES[1][side][k]
                source = source_tile(post_ref, low_ref, high_ref, i, x)
                if DIRECTIONS[i][2]:
                    rows.append(z_shift(source[...], i, face)[row : row + 1])
                else:
                    rows.append(source[row : row + 1])
            out_ref[at : at + 1] = jnp.where(upward, rows[0], rows[1])
    end = start + 5 * size_x
    if out_ref.shape[0] > end:
        out_ref[end:] = jnp.zeros((out_ref.shape[0] - end, LANES), jnp.float32)


def middle_kernel(post_ref, low_ref, high_ref, other_ref, middle_ref):
    odd = lax.rem(lax.axis_index("gy"), 2) == 1
    face_rows(post_ref, low_ref, high_ref, other_ref, middle_ref, 0, odd)


def sides_kernel(post_ref, low_ref, high_ref, other_ref, middle_ref, face_ref, edge_ref):
    odd = lax.rem(lax.axis_index("gy"), 2) == 1
    face_rows(post_ref, low_ref, high_ref, other_ref, middle_ref, 0, odd)
    face_rows(post_ref, low_ref, high_ref, other_ref, face_ref, 0, jnp.logical_not(odd))
    edge_kernel(low_ref, high_ref, edge_ref)


def near_kernel(pair_ref, cross_ref, face_ref, near_ref):
    near_ref[: 2 * FAB] = pair_ref[...]
    near_ref[2 * FAB : 4 * FAB] = cross_ref[...]
    near_ref[4 * FAB :] = face_ref[...]


def shift_kernel(post_ref, low_ref, high_ref, other_ref, edge_ref, rolled_ref):
    size_x, size_y = post_ref.shape[1:3]
    for i in range(19):
        for x in range(size_x):
            tile = source_tile(post_ref, low_ref, high_ref, i, x)[...]
            from_x = x - DIRECTIONS[i][0]
            if 0 <= from_x < size_x:
                face = other_ref[FAB + from_x * size_y : FAB + (from_x + 1) * size_y]
            else:
                face = edge_ref[...]
            tile = z_shift(tile, i, face)
            if DIRECTIONS[i][1]:
                tile = pltpu.roll(tile, DIRECTIONS[i][1] % size_y, 0)
            rolled_ref[i, x] = tile


def fabric_part(pairs, chips, start, my_node, column, at_lane, nodes, capacity):
    parts = nodes // LANES
    me = lax.axis_index("gy") * 2 + lax.axis_index("gz")
    slot_owner = iota((1, LANES), 1) // capacity
    owner_base = (slot_owner * nodes).astype(jnp.float32)
    matches, forces, picked = [], [], jnp.zeros((8, LANES), jnp.float32)
    for m in range(2 * len(pairs)):
        tile = pairs[m // 2][m % 2 * FAB : m % 2 * FAB + 8]
        ids = tile[0:1]
        ids = jnp.where(ids >= 0.0, owner_base + ids, -1.0)
        matches.append(one_hot(column == ids))
        forces.append(tile)
        shift = lax.rem((start + m + LANES // capacity - me) * capacity, LANES)
        picked = jnp.where(slot_owner == start + m, pltpu.roll(tile, shift, 1), picked)
    pushed = sum3(dot_nt(stacked3(jnp.concatenate(forces, axis=1)), jnp.concatenate(matches, axis=1)))

    found = sum3(dot_nn(stacked3(jnp.concatenate(pairs, axis=0)), at_lane))
    row = iota((FAB, LANES), 0)
    fits = (row >= 4) & (row % parts == (my_node.astype(jnp.int32) >> 7))
    base = jnp.zeros((FAB, LANES), jnp.float32)
    for m in range(2 * len(pairs)):
        owner = chips[m // 2] * 2 + m % 2
        base = jnp.where(fits & (slot_owner == owner), found[m * FAB : (m + 1) * FAB], base)
    return jnp.concatenate([pushed, base, picked], axis=0)


def half_kernel(seed_ref, pair_ref, cross_ref, acc_ref, column_ref, lane_ref):
    place_y = lax.axis_index("gy")
    nodes, capacity = 4 * LANES, LANES // 8
    my_node = seed_ref[0:1]
    owner_base = (iota((1, LANES), 1) // capacity * nodes).astype(jnp.float32)
    my_id = jnp.where(my_node >= 0.0, owner_base + my_node, -2.0)
    column = jnp.transpose(jnp.broadcast_to(my_id, (LANES, LANES)))
    at_lane = one_hot(iota((LANES, LANES), 0) == (my_node.astype(jnp.int32) & (LANES - 1)))
    pairs, chips = [pair_ref[...], cross_ref[...]], [place_y, place_y ^ 2]
    acc_ref[...] = fabric_part(pairs, chips, 0, my_node, column, at_lane, nodes, capacity)
    column_ref[...] = column
    lane_ref[...] = at_lane


def final_kernel(
    rolled_ref, kind_ref, back_ref, seed_ref, acc_ref, column_ref, lane_ref, near_ref, middle_ref, pos_ref,
    pop_hbm, pos_hbm, vel_hbm, wall_hbm,
    pop_ref, pos_out_ref, vel_out_ref, wall_out_ref, sems,
):
    size_x, size_y = rolled_ref.shape[1:3]
    place_y = lax.axis_index("gy")
    odd = lax.rem(place_y, 2) == 1
    first, top = place_y == 0, place_y == lax.axis_size("gy") - 1
    sub = iota((size_y, LANES), 0)
    owners, capacity = wall_out_ref.shape[4], wall_out_ref.shape[5]
    nodes = pos_ref.shape[2]
    parts = nodes // LANES
    mine = seed_ref[:FAB]
    pairs, chips = [near_ref[: 2 * FAB], near_ref[2 * FAB : 4 * FAB]], [place_y ^ 1, place_y ^ 3]
    acc = fabric_part(pairs, chips, 4, mine[0:1], column_ref[...], lane_ref[...], nodes, capacity) + acc_ref[...]
    copies = []
    for x in range(size_x):
        kind = kind_ref[x]
        back = back_ref[x]
        for i in range(19):
            tile = rolled_ref[i, x]
            if DIRECTIONS[i][1]:
                side = 0 if DIRECTIONS[i][1] == 1 else 1
                at = SIDES[1][side].index(i) * size_x + x
                by_near = near_ref[4 * FAB + at : 4 * FAB + at + 1]
                by_middle = middle_ref[at : at + 1]
                if side == 0:
                    row = jnp.where(first, WEIGHTS[i], jnp.where(odd, by_near, by_middle))
                    tile = jnp.where(sub == 0, row, tile)
                else:
                    row = jnp.where(top, WEIGHTS[i], jnp.where(odd, by_middle, by_near))
                    tile = jnp.where(sub == size_y - 1, row, tile)
            if i:
                tile = jnp.where(kind == float(i), back, tile)
            pop_ref[i, x] = tile

    pushed, found, picked = acc[:8], acc[8:24], acc[24:32]
    node = picked[0:1].astype(jnp.int32)
    row = iota((FAB, LANES), 0)
    spread = jnp.where(row < parts, picked[1:2], jnp.where(row < 2 * parts, picked[2:3], picked[3:4]))
    spread = jnp.where((row < 3 * parts) & (row % parts == (node >> 7)), spread, 0.0)
    at_node = one_hot(iota((LANES, LANES), 0) == (node & (LANES - 1)))
    fluid = sum3(dot_nt(stacked3(spread), at_node))
    my_live = mine[0:1] >= 0.0
    moved = []
    for a in range(3):
        for k in range(parts):
            r = a * parts + k
            new = mine[4 + r : 5 + r] + fluid[r : r + 1]
            at = slice(k * LANES, (k + 1) * LANES)
            vel_out_ref[a, :, at] = new
            pos_out_ref[a, :, at] = pos_ref[a, :, at] + new
        base = jnp.sum(found[4 + a * parts : 4 + (a + 1) * parts], axis=0, keepdims=True)
        moved.append(jnp.where(my_live, base + pushed[1 + a : 2 + a], 0.0))
    moved = jnp.concatenate(moved + [jnp.zeros((5, LANES), jnp.float32)], axis=0)
    for o in range(owners):
        turned = pltpu.roll(moved, LANES - o * capacity, 1) if o else moved
        for a in range(3):
            wall_out_ref[0, 0, 0, a, o : o + 1] = turned[a : a + 1, :capacity]
    copies.append(pltpu.make_async_copy(pop_ref, pop_hbm, sems.at[0]))
    copies[-1].start()
    for k, (src, dst) in enumerate(((vel_out_ref, vel_hbm), (pos_out_ref, pos_hbm), (wall_out_ref, wall_hbm))):
        copies.append(pltpu.make_async_copy(src, dst, sems.at[size_x + k]))
        copies[-1].start()
    for copy in copies:
        copy.wait()


def ring(count, step):
    return [(i, (i + step) % count) for i in range(count)]


def body(
    populations,
    solid,
    link_cell,
    link_dir,
    link_node,
    link_velocity,
    fabric_position,
    fabric_velocity,
    fabric_rest,
    triangles,
):
    size_x, size_y, size_z = populations.shape[1:]
    owners, capacity = link_node.shape[3:]
    nodes = fabric_position.shape[2]
    count_x, count_y, count_z = (lax.axis_size(name) for name in ("gx", "gy", "gz"))
    folded = (
        (count_y, count_z) == (4, 2)
        and (size_y, size_z) == (8, LANES)
        and owners * capacity == LANES
        and nodes == 4 * LANES
    )
    if not folded:
        return general_body(
            populations, solid, link_cell, link_dir, link_node, link_velocity,
            fabric_position, fabric_velocity, fabric_rest, triangles,
        )
    f32 = jnp.float32
    on_chip = pl.BlockSpec(memory_space=pltpu.VMEM)

    def shape(*dims):
        return jax.ShapeDtypeStruct(dims, f32)

    def kept(*dims):
        return pltpu.VMEM(dims, f32)

    def run(kernel, outs, *args):
        args = [pltpu.with_memory_space_constraint(arg, pltpu.VMEM) for arg in args]
        return pl.pallas_call(
            kernel,
            out_shape=outs,
            in_specs=[on_chip] * len(args),
            out_specs=jax.tree.map(lambda _: on_chip, outs),
            name=kernel.__name__,
        )(*args)

    face_x = kept(5, size_y, size_z)
    map_shape = kept(size_x, size_y, size_z)
    given = (
        populations, solid, link_cell, link_dir, link_node, link_velocity,
        fabric_position, fabric_velocity, fabric_rest, triangles,
    )
    cells = size_x * size_y
    opened = (kept(*populations.shape), face_x, face_x, kept(max(SEED, FAB + cells), LANES), map_shape, map_shape, kept(*fabric_position.shape))
    post, up, down, seed, kind, back, position = pl.pallas_call(
        open_kernel,
        out_shape=opened,
        in_specs=[pl.BlockSpec(memory_space=pl.ANY)] * len(given),
        out_specs=(on_chip,) * len(opened),
        scratch_shapes=[pltpu.VMEM(arg.shape, arg.dtype) for arg in given if arg is not fabric_position]
        + [pltpu.SemaphoreType.DMA((len(given),))],
        name="open_kernel",
    )(*given)
    swap_z = [(0, 1), (1, 0)]
    other = lax.ppermute(seed, "gz", swap_z)
    xlow = lax.ppermute(up, "gx", ring(count_x, 1))
    xhigh = lax.ppermute(down, "gx", ring(count_x, -1))
    (pair,) = run(pair_kernel, (kept(2 * FAB, LANES),), seed, other)
    crossing = [(y * 2 + z, (y ^ 2) * 2 + 1 - z) for y in range(count_y) for z in range(2)]
    cross = lax.ppermute(pair, ("gy", "gz"), crossing)
    middling = []
    for y in range(count_y):
        to = y + 1 if y % 2 else y - 1
        for z in range(count_z):
            middling.append((y * 2 + z, to * 2 + z if 0 <= to < count_y else y * 2 + 1 - z))
    rows = -(-5 * size_x // 8) * 8
    middle, face, edge = run(
        sides_kernel, (kept(MID * rows, LANES), kept(rows, LANES), kept(size_y, LANES)), post, xlow, xhigh, other
    )
    middle = lax.ppermute(middle, ("gy", "gz"), middling)
    edge = lax.ppermute(edge, "gz", swap_z)
    (near,) = run(near_kernel, (kept(4 * FAB + rows, LANES),), pair, cross, face)
    near = lax.ppermute(near, "gy", [(y, y ^ 1) for y in range(count_y)])
    (rolled,) = run(shift_kernel, (kept(*populations.shape),), post, xlow, xhigh, other, edge)
    halves = (kept(32, LANES), kept(LANES, LANES), pltpu.VMEM((LANES, LANES), jnp.bfloat16))
    acc, column, at_lane = run(half_kernel, halves, seed, pair, cross)
    outs = (
        shape(*populations.shape),
        shape(*fabric_position.shape),
        shape(*fabric_velocity.shape),
        shape(*link_velocity.shape),
    )
    last = [rolled, kind, back, seed, acc, column, at_lane, near, middle, position]
    last = [pltpu.with_memory_space_constraint(arg, pltpu.VMEM) for arg in last]
    return pl.pallas_call(
        final_kernel,
        out_shape=outs,
        in_specs=[on_chip] * len(last),
        out_specs=(pl.BlockSpec(memory_space=pl.ANY),) * 4,
        scratch_shapes=[pltpu.VMEM(out.shape, f32) for out in outs] + [pltpu.SemaphoreType.DMA((size_x + 3,))],
        name="final_kernel",
    )(*last)


def solution(mesh):
    placed = (
        P(None, "gx", "gy", "gz"),
        P("gx", "gy", "gz"),
        P("gx", "gy", "gz", None, None),
        P("gx", "gy", "gz", None, None),
        P("gx", "gy", "gz", None, None),
        P("gx", "gy", "gz", None, None, None),
        P(None, "gx", ("gy", "gz")),
        P(None, "gx", ("gy", "gz")),
        P(None, "gx", ("gy", "gz")),
        P(None, "gx", ("gy", "gz")),
    )
    return jax.shard_map(
        body,
        mesh=mesh,
        in_specs=placed,
        out_specs=(
            P(None, "gx", "gy", "gz"),
            P(None, "gx", ("gy", "gz")),
            P(None, "gx", ("gy", "gz")),
            P("gx", "gy", "gz", None, None, None),
        ),
        check_vma=False,
    )
```

```python
import jax
import jax.numpy as jnp
import numpy as np
from jax import lax
from jax.experimental import pallas as pl
from jax.experimental.pallas import tpu as pltpu
from jax.sharding import PartitionSpec as P

SPRING = 0.5
DAMPING = 0.1
DIRECTIONS = [
    [0, 0, 0],
    [1, 0, 0],
    [-1, 0, 0],
    [0, 1, 0],
    [0, -1, 0],
    [0, 0, 1],
    [0, 0, -1],
    [1, 1, 0],
    [-1, -1, 0],
    [1, -1, 0],
    [-1, 1, 0],
    [1, 0, 1],
    [-1, 0, -1],
    [1, 0, -1],
    [-1, 0, 1],
    [0, 1, 1],
    [0, -1, -1],
    [0, 1, -1],
    [0, -1, 1],
]


def extended(cells, sides, width):
    for axis, dim in sides:
        count = lax.axis_size(axis)
        head = lax.slice_in_dim(cells, 0, width, axis=dim)
        tail = lax.slice_in_dim(cells, cells.shape[dim] - width, cells.shape[dim], axis=dim)
        cells = jnp.concatenate(
            [
                lax.ppermute(tail, axis, [(i, (i + 1) % count) for i in range(count)]),
                cells,
                lax.ppermute(head, axis, [((i + 1) % count, i) for i in range(count)]),
            ],
            axis=dim,
        )
    return cells


def lattice():
    velocity_np = np.array(DIRECTIONS)
    weight_np = np.array([1.0 / 3.0] + [1.0 / 18.0] * 6 + [1.0 / 36.0] * 12)
    opposite_list = [
        DIRECTIONS.index([-entry for entry in DIRECTIONS[direction]]) for direction in range(19)
    ]
    along_a = np.array([float(entry[0]) for entry in DIRECTIONS])
    along_b = np.array([float(entry[1]) for entry in DIRECTIONS])
    along_e = np.array([float(entry[2]) for entry in DIRECTIONS])
    speed_sq = along_a * along_a + along_b * along_b + along_e * along_e
    moment_rows = [
        np.ones(19),
        19 * speed_sq - 30,
        (21 * speed_sq * speed_sq - 53 * speed_sq + 24) / 2,
        along_a,
        (5 * speed_sq - 9) * along_a,
        along_b,
        (5 * speed_sq - 9) * along_b,
        along_e,
        (5 * speed_sq - 9) * along_e,
        3 * along_a * along_a - speed_sq,
        (3 * speed_sq - 5) * (3 * along_a * along_a - speed_sq),
        along_b * along_b - along_e * along_e,
        (3 * speed_sq - 5) * (along_b * along_b - along_e * along_e),
        along_a * along_b,
        along_b * along_e,
        along_a * along_e,
        (along_b * along_b - along_e * along_e) * along_a,
        (along_e * along_e - along_a * along_a) * along_b,
        (along_a * along_a - along_b * along_b) * along_e,
    ]
    moment_np = np.stack(moment_rows)
    inverse_np = moment_np.T / np.sum(moment_np * moment_np, axis=1)[None, :]
    viscous = 5.0 / 3.0
    rates_np = np.array(
        [
            0.0,
            1.19,
            1.4,
            0.0,
            1.2,
            0.0,
            1.2,
            0.0,
            1.2,
            viscous,
            1.4,
            viscous,
            1.4,
            viscous,
            viscous,
            viscous,
            1.98,
            1.98,
            1.98,
        ]
    )
    return (velocity_np, weight_np, opposite_list, moment_np, inverse_np, rates_np)


def collide_cells(popul, solid_flat):
    velocity_np, weight_np, opposite_list, moment_np, inverse_np, rates_np = lattice()
    velocity_table = jnp.asarray(velocity_np, jnp.float32)
    weight_table = jnp.asarray(weight_np, jnp.float32)
    density = jnp.sum(popul, axis=0)
    momentum = jnp.dot(
        velocity_table.T, popul, precision=lax.Precision.HIGHEST, preferred_element_type=jnp.float32
    )
    flow = momentum / density
    projected = jnp.dot(
        velocity_table, flow, precision=lax.Precision.HIGHEST, preferred_element_type=jnp.float32
    )
    speed_sq = jnp.sum(flow * flow, axis=0)
    equilibrium = (
        weight_table[:, None]
        * density
        * (1.0 + 3.0 * projected + 4.5 * projected * projected - 1.5 * speed_sq)
    )
    offset = popul - equilibrium
    moments = jnp.dot(
        jnp.asarray(moment_np, jnp.float32),
        offset,
        precision=lax.Precision.HIGHEST,
        preferred_element_type=jnp.float32,
    )
    relaxed = jnp.asarray(rates_np, jnp.float32)[:, None] * moments
    change = jnp.dot(
        jnp.asarray(inverse_np, jnp.float32),
        relaxed,
        precision=lax.Precision.HIGHEST,
        preferred_element_type=jnp.float32,
    )
    return jnp.where(solid_flat[None, :] == 1, popul, popul - change)


def fill_outside(padded, weight_np):
    span_y = padded.shape[2]
    span_z = padded.shape[3]
    place_y = lax.axis_index("gy")
    place_z = lax.axis_index("gz")
    count_y = lax.axis_size("gy")
    count_z = lax.axis_size("gz")
    rows_y = jnp.arange(span_y)
    rows_z = jnp.arange(span_z)
    out_y = (rows_y == 0) & (place_y == 0) | (rows_y == span_y - 1) & (place_y == count_y - 1)
    out_z = (rows_z == 0) & (place_z == 0) | (rows_z == span_z - 1) & (place_z == count_z - 1)
    outside = out_y[:, None] | out_z[None, :]
    return jnp.where(
        outside[None, None], jnp.asarray(weight_np, jnp.float32)[:, None, None, None], padded
    )


def propagate(padded, size_x, size_y, size_z):
    pieces = []
    for direction in range(19):
        shift_x = DIRECTIONS[direction][0]
        shift_y = DIRECTIONS[direction][1]
        shift_z = DIRECTIONS[direction][2]
        plane = padded[direction]
        pieces.append(
            lax.slice(
                plane,
                (1 - shift_x, 1 - shift_y, 1 - shift_z),
                (1 - shift_x + size_x, 1 - shift_y + size_y, 1 - shift_z + size_z),
            )
        )
    return jnp.stack(pieces)


def membrane(positions, rest, triangle_nodes):
    force = jnp.zeros(positions.shape, jnp.float32)
    for first, second in ((0, 1), (1, 2), (2, 0)):
        head = triangle_nodes[first]
        tail = triangle_nodes[second]
        stretch = positions[:, tail] - positions[:, head] - (rest[:, tail] - rest[:, head])
        force = force.at[:, head].add(SPRING * stretch)
        force = force.at[:, tail].add(-SPRING * stretch)
    return force


def general_body(
    populations,
    solid,
    link_cell,
    link_dir,
    link_node,
    link_velocity,
    fabric_position,
    fabric_velocity,
    fabric_rest,
    triangles,
):
    velocity_np, weight_np, opposite_list, moment_np, inverse_np, rates_np = lattice()
    velocity_table = jnp.asarray(velocity_np, jnp.float32)
    weight_table = jnp.asarray(weight_np, jnp.float32)
    opposite_table = jnp.asarray(opposite_list, jnp.int32)
    size_x = populations.shape[1]
    size_y = populations.shape[2]
    size_z = populations.shape[3]
    cells = size_x * size_y * size_z
    post = collide_cells(populations.reshape(19, cells), solid.reshape(cells)).reshape(
        populations.shape
    )
    padded = extended(post, (("gx", 1), ("gy", 2), ("gz", 3)), 1)
    padded = fill_outside(padded, weight_np)
    propagated = propagate(padded, size_x, size_y, size_z).reshape(19, cells)
    owners_n = link_node.shape[3]
    capacity = link_node.shape[4]
    node_rows = link_node.reshape(owners_n, capacity)
    cell_rows = link_cell.reshape(owners_n, capacity)
    dir_rows = link_dir.reshape(owners_n, capacity)
    live = node_rows >= 0
    post_flat = post.reshape(19, cells)
    reflected = post_flat[opposite_table[dir_rows], cell_rows]
    link_unit = velocity_table[dir_rows]
    wall = jnp.moveaxis(link_velocity.reshape(3, owners_n, capacity), 0, -1)
    returned = reflected + 6.0 * weight_table[dir_rows] * jnp.sum(link_unit * wall, axis=-1)
    populations_next = propagated.at[jnp.where(live, dir_rows, 19), cell_rows].set(
        returned, mode="drop"
    )
    strength = reflected + returned
    positions = fabric_position.reshape(3, -1)
    velocities = fabric_velocity.reshape(3, -1)
    rest = fabric_rest.reshape(3, -1)
    nodes_n = positions.shape[1]
    elastic = membrane(positions, rest, triangles.reshape(3, -1))
    link_force = jnp.moveaxis(-link_unit * strength[..., None], -1, 0)
    got_nodes, got_force = (
        lax.all_to_all(node_rows[None], ("gy", "gz"), split_axis=1, concat_axis=1, tiled=True),
        lax.all_to_all(link_force, ("gy", "gz"), split_axis=1, concat_axis=1, tiled=True),
    )
    got_ids = got_nodes[0]
    got_live = got_ids >= 0
    target = jnp.where(got_live, got_ids, nodes_n).reshape(-1)
    fluid_force = (
        jnp.zeros((3, nodes_n), jnp.float32)
        .at[:, target]
        .add(got_force.reshape(3, -1), mode="drop")
    )
    velocity_next = (1.0 - DAMPING) * velocities + (fluid_force + elastic)
    position_next = positions + velocity_next
    reply = jnp.where(got_live[None], velocity_next[:, jnp.where(got_live, got_ids, 0)], 0.0)
    wall_next = lax.all_to_all(reply, ("gy", "gz"), split_axis=1, concat_axis=1, tiled=True)
    return (
        populations_next.reshape(populations.shape),
        position_next.reshape(fabric_position.shape),
        velocity_next.reshape(fabric_velocity.shape),
        wall_next.reshape(link_velocity.shape),
    )


WEIGHTS = [1.0 / 3.0] + [1.0 / 18.0] * 6 + [1.0 / 36.0] * 12
OPPOSITE = [DIRECTIONS.index([-entry for entry in d]) for d in DIRECTIONS]
SIDES = [
    ([i for i in range(19) if DIRECTIONS[i][a] == 1], [i for i in range(19) if DIRECTIONS[i][a] == -1])
    for a in range(3)
]
LANES = 128
PATCH = 256
FAB = 16
SEED = 80
MID = 4


def iota(shape, axis):
    return lax.broadcasted_iota(jnp.int32, shape, axis)


def split3(value):
    high = value.astype(jnp.bfloat16).astype(jnp.float32)
    rest = value - high
    middle = rest.astype(jnp.bfloat16).astype(jnp.float32)
    return high, middle, rest - middle


def stacked3(value):
    return jnp.concatenate(split3(value), axis=0).astype(jnp.bfloat16)


def sum3(value):
    rows = value.shape[0] // 3
    return value[:rows] + value[rows : 2 * rows] + value[2 * rows :]


def dot_nn(left, right):
    return lax.dot_general(left, right, (((1,), (0,)), ((), ())), preferred_element_type=jnp.float32)


def dot_nt(left, right):
    return lax.dot_general(left, right, (((1,), (1,)), ((), ())), preferred_element_type=jnp.float32)


def one_hot(mask):
    return jnp.where(mask, 1.0, 0.0).astype(jnp.bfloat16)


def collided(f, solid):
    sx, dx = f[1] + f[2], f[1] - f[2]
    sy, dy = f[3] + f[4], f[3] - f[4]
    sz, dz = f[5] + f[6], f[5] - f[6]
    sa, da = f[7] + f[8], f[7] - f[8]
    sb, db = f[9] + f[10], f[9] - f[10]
    sc, dc = f[11] + f[12], f[11] - f[12]
    sd, dd = f[13] + f[14], f[13] - f[14]
    se, de = f[15] + f[16], f[15] - f[16]
    sg, dg = f[17] + f[18], f[17] - f[18]
    sxy, txy = sa + sb, sa - sb
    sxz, txz = sc + sd, sc - sd
    syz, tyz = se + sg, se - sg
    ax_ab, ay_ab = da + db, da - db
    ax_cd, az_cd = dc + dd, dc - dd
    ay_eg, az_eg = de + dg, de - dg
    near, far = sx + sy + sz, sxy + sxz + syz
    rho = f[0] + near + far
    ex, ey, ez = ax_ab + ax_cd, ay_ab + ay_eg, az_cd + az_eg
    jx, jy, jz = dx + ex, dy + ey, dz + ez
    inv = 1.0 / rho
    ux, uy, uz = jx * inv, jy * inv, jz * inv
    xx, yy, zz = jx * ux, jy * uy, jz * uz
    jj = xx + yy + zz
    energy = (-30.0 * f[0] - 11.0 * near + 8.0 * far) - (-11.0 * rho + 19.0 * jj)
    square = (12.0 * f[0] - 4.0 * near + far) - (3.0 * rho - 5.5 * jj)
    kx = (1.2 / 40.0) * (ex - 4.0 * dx + (2.0 / 3.0) * jx)
    ky = (1.2 / 40.0) * (ey - 4.0 * dy + (2.0 / 3.0) * jy)
    kz = (1.2 / 40.0) * (ez - 4.0 * dz + (2.0 / 3.0) * jz)
    yz_near, xyz_far = sy + sz, sxy + sxz - 2.0 * syz
    pxx_eq = 2.0 * xx - yy - zz
    pww_eq = yy - zz
    pxx = (5.0 / 3.0 / 36.0) * (2.0 * sx - yz_near + xyz_far - pxx_eq)
    pixx = (1.4 / 72.0) * (-4.0 * sx + 2.0 * yz_near + xyz_far + 0.5 * pxx_eq)
    w_near, w_far = sy - sz, sxy - sxz
    pww = (5.0 / 3.0 / 12.0) * (w_near + w_far - pww_eq)
    piww = (1.4 / 24.0) * (w_far - 2.0 * w_near + 0.5 * pww_eq)
    pxy = (5.0 / 3.0 / 4.0) * (txy - jx * uy)
    pyz = (5.0 / 3.0 / 4.0) * (tyz - jy * uz)
    pxz = (5.0 / 3.0 / 4.0) * (txz - jx * uz)
    mx = (1.98 / 8.0) * (ax_ab - ax_cd)
    my = (1.98 / 8.0) * (ay_eg - ay_ab)
    mz = (1.98 / 8.0) * (az_cd - az_eg)
    energy = (1.19 / 2394.0) * energy
    square = (1.4 / 252.0) * square
    axis = -11.0 * energy - 4.0 * square
    across = pxx - 2.0 * pixx
    split = pww - 2.0 * piww
    edge = 8.0 * energy + square
    pp, ww = pxx + pixx, pww + piww
    even = [
        axis + 2.0 * across,
        axis - across + split,
        axis - across - split,
        edge + pp + ww + pxy,
        edge + pp + ww - pxy,
        edge + pp - ww + pxz,
        edge + pp - ww - pxz,
        edge - 2.0 * pp + pyz,
        edge - 2.0 * pp - pyz,
    ]
    odd = [
        -4.0 * kx,
        -4.0 * ky,
        -4.0 * kz,
        (kx + mx) + (ky - my),
        (kx + mx) - (ky - my),
        (kx - mx) + (kz + mz),
        (kx - mx) - (kz + mz),
        (ky + my) + (kz - mz),
        (ky + my) - (kz - mz),
    ]
    change = [12.0 * square - 30.0 * energy]
    for pair in range(9):
        change += [even[pair] + odd[pair], even[pair] - odd[pair]]
    fluid = solid != 1
    return [jnp.where(fluid, f[i] - change[i], f[i]) for i in range(19)]


def slots_to_row(value):
    owners, capacity = value.shape
    wide = jnp.concatenate([value, jnp.zeros((owners, LANES - capacity), value.dtype)], axis=1)
    return jnp.sum(pltpu.roll(wide, 0, 1, stride=capacity, stride_axis=0), axis=0, keepdims=True)


def membrane_start(pos_ref, rest_ref, tri_ref):
    nodes = pos_ref.shape[2]
    count = tri_ref.shape[2]
    wide = -(-count // LANES) * LANES
    patches = nodes // PATCH
    stretch = [pos_ref[a] - rest_ref[a] for a in range(3)]
    corners = [
        jnp.concatenate([tri_ref[t], jnp.full((1, wide - count), -1, jnp.int32)], axis=1) for t in range(3)
    ]
    patch = jnp.maximum(corners[0], 0) // PATCH
    local = [(corner - patch * PATCH).astype(jnp.float32) for corner in corners]
    node_ids = iota((PATCH, LANES), 0).astype(jnp.float32).astype(jnp.bfloat16)
    blocks = []
    for k in range(0, wide, LANES):
        block = jnp.zeros((PATCH, LANES), jnp.bfloat16)
        for corner in local:
            row = jnp.broadcast_to(corner[:, k : k + LANES], (16, LANES)).astype(jnp.bfloat16)
            row = jnp.concatenate([row] * (PATCH // 16), axis=0)
            block = block + jnp.where(node_ids == row, jnp.ones_like(block), jnp.zeros_like(block))
        blocks.append(block)
    hits = jnp.concatenate(blocks, axis=1)
    stretch8 = jnp.concatenate(stretch + [jnp.zeros((5, nodes), jnp.float32)], axis=0)
    pieces = [stacked3(stretch8[:, p * PATCH : (p + 1) * PATCH]) for p in range(patches)]
    sums = dot_nn(jnp.concatenate(pieces, axis=0), hits)
    total = jnp.zeros((8, wide), jnp.float32)
    for p in range(patches):
        total = jnp.where(patch == p, sum3(sums[p * 24 : (p + 1) * 24]), total)
    return stretch, hits, total, patch


def membrane_finish(parts, vel_ref, fab_ref):
    stretch, hits, total, patch = parts
    nodes = vel_ref.shape[2]
    patches = nodes // PATCH
    total = jnp.where(iota(total.shape, 0) == 3, 1.0, total)
    pieces = [stacked3(jnp.where(patch == p, total, 0.0)) for p in range(patches)]
    sums = dot_nt(jnp.concatenate(pieces, axis=0), hits)
    back = jnp.concatenate([sum3(sums[p * 24 : (p + 1) * 24]) for p in range(patches)], axis=1)
    for a in range(3):
        elastic = SPRING * back[a : a + 1] - 3.0 * SPRING * back[3:4] * stretch[a]
        base = (1.0 - DAMPING) * vel_ref[a] + elastic
        for k in range(nodes // LANES):
            row = 4 + a * (nodes // LANES) + k
            fab_ref[row : row + 1] = base[:, k * LANES : (k + 1) * LANES]


def z_face(tiles):
    up = jnp.zeros_like(next(t for t in tiles if t is not None))
    lane = iota(up.shape, 1)
    down = up
    for k in range(5):
        i, j = SIDES[2][0][k], SIDES[2][1][k]
        if tiles[i] is not None:
            up = jnp.where(lane == k, pltpu.roll(tiles[i], k + 1, 1), up)
        if tiles[j] is not None:
            down = jnp.where(lane == k, pltpu.roll(tiles[j], k, 1) if k else tiles[j], down)
    return jnp.where(lax.axis_index("gz") == 0, up, down)


def z_shift(tile, i, face):
    lane = iota(tile.shape, 1)
    low_end = lax.axis_index("gz") == 0
    if DIRECTIONS[i][2] == 1:
        k = SIDES[2][0].index(i)
        halo = pltpu.roll(face, LANES - k, 1) if k else face
        return jnp.where(lane == 0, jnp.where(low_end, WEIGHTS[i], halo), pltpu.roll(tile, 1, 1))
    if DIRECTIONS[i][2] == -1:
        k = SIDES[2][1].index(i)
        halo = pltpu.roll(face, LANES - 1 - k, 1)
        return jnp.where(lane == LANES - 1, jnp.where(low_end, halo, WEIGHTS[i]), pltpu.roll(tile, LANES - 1, 1))
    return tile


def open_kernel(
    pop_hbm, solid_hbm, cell_hbm, dir_hbm, node_hbm, wall_hbm, pos_hbm, vel_hbm, rest_hbm, tri_hbm,
    post_ref, up_ref, down_ref, seed_ref, kind_ref, back_ref, pos_ref,
    pop_ref, solid_ref, cell_ref, dir_ref, node_ref, wall_ref, vel_ref, rest_ref, tri_ref, sems,
):
    moves = [
        (pop_hbm, pop_ref), (solid_hbm, solid_ref),
        (tri_hbm, tri_ref), (pos_hbm, pos_ref), (rest_hbm, rest_ref), (vel_hbm, vel_ref),
        (cell_hbm, cell_ref), (dir_hbm, dir_ref), (node_hbm, node_ref), (wall_hbm, wall_ref),
    ]
    copies = [pltpu.make_async_copy(src, dst, sems.at[k]) for k, (src, dst) in enumerate(moves)]
    for copy in copies[6:] + copies[2:6] + copies[:2]:
        copy.start()
    for copy in copies[2:]:
        copy.wait()
    parts = membrane_start(pos_ref, rest_ref, tri_ref)
    size_x, size_y = post_ref.shape[1:3]
    rows = size_x * size_y
    cell = slots_to_row(cell_ref[0, 0, 0].astype(jnp.float32)).astype(jnp.int32)
    way = slots_to_row(dir_ref[0, 0, 0].astype(jnp.float32))
    node = slots_to_row(node_ref[0, 0, 0].astype(jnp.float32))
    live = node >= 0.0
    unit = []
    for a in range(3):
        u = jnp.zeros_like(way)
        for i in range(1, 19):
            if DIRECTIONS[i][a]:
                u = jnp.where(way == float(i), float(DIRECTIONS[i][a]), u)
        unit.append(u)
    weight = jnp.where(way >= 7.0, 6.0 / 36.0, 6.0 / 18.0)
    wall = [slots_to_row(wall_ref[0, 0, 0, a]) for a in range(3)]
    term = weight * (unit[0] * wall[0] + unit[1] * wall[1] + unit[2] * wall[2])
    at_row = jnp.where((iota((rows, LANES), 0) == (cell >> 7)) & live, 1.0, 0.0)
    at_lane = one_hot(iota((LANES, LANES), 0) == (cell & (LANES - 1)))
    left = jnp.concatenate([at_row * way] + [at_row * t for t in split3(term)], axis=0)
    maps = dot_nt(left.astype(jnp.bfloat16), at_lane)
    kind = maps[:rows]
    added = sum3(maps[rows:])
    for copy in copies[:2]:
        copy.wait()
    taken = []
    membrane_finish(parts, vel_ref, seed_ref)
    for x in range(size_x):
        post = collided([pop_ref[i, x] for i in range(19)], solid_ref[x])
        k = kind[x * size_y : (x + 1) * size_y]
        t = jnp.zeros_like(k)
        for i in range(19):
            post_ref[i, x] = post[i]
            if x == size_x - 1 and i in SIDES[0][0]:
                up_ref[SIDES[0][0].index(i)] = post[i]
            if x == 0 and i in SIDES[0][1]:
                down_ref[SIDES[0][1].index(i)] = post[i]
            if i:
                t = jnp.where(k == float(OPPOSITE[i]), post[i], t)
        seed_ref[FAB + x * size_y : FAB + (x + 1) * size_y] = z_face(post)
        taken.append(t)
        kind_ref[x] = k
        back_ref[x] = t + added[x * size_y : (x + 1) * size_y]
    strength = 2.0 * jnp.concatenate(taken, axis=0) + added
    at_link = sum3(dot_nn(stacked3(strength), at_lane))
    push = jnp.sum(at_row * at_link, axis=0, keepdims=True)
    seed_ref[0:1] = node
    for a in range(3):
        seed_ref[1 + a : 2 + a] = -unit[a] * push
    end = FAB + rows
    seed_ref[end:] = jnp.zeros((seed_ref.shape[0] - end, LANES), jnp.float32)


def source_tile(post_ref, low_ref, high_ref, i, x):
    size_x = post_ref.shape[1]
    from_x = x - DIRECTIONS[i][0]
    if from_x < 0:
        return low_ref.at[SIDES[0][0].index(i)]
    if from_x >= size_x:
        return high_ref.at[SIDES[0][1].index(i)]
    return post_ref.at[i, from_x]


def pair_kernel(seed_ref, other_ref, pair_ref):
    low = lax.axis_index("gz") == 0
    pair_ref[:FAB] = jnp.where(low, seed_ref[:FAB], other_ref[:FAB])
    pair_ref[FAB:] = jnp.where(low, other_ref[:FAB], seed_ref[:FAB])


def edge_tile(low_ref, high_ref):
    tiles = [None] * 19
    for i in range(19):
        if DIRECTIONS[i][0] and DIRECTIONS[i][2]:
            side = 0 if DIRECTIONS[i][0] == 1 else 1
            tiles[i] = (low_ref, high_ref)[side][SIDES[0][side].index(i)]
    return z_face(tiles)


def face_rows(post_ref, low_ref, high_ref, other_ref, out_ref, start, upward):
    size_x, size_y = post_ref.shape[1:3]
    for k in range(5):
        for x in range(size_x):
            at = start + k * size_x + x
            face = other_ref[FAB + x * size_y : FAB + (x + 1) * size_y]
            rows = []
            for side, row in ((0, size_y - 1), (1, 0)):
                i = SIDES[1][side][k]
                source = source_tile(post_ref, low_ref, high_ref, i, x)
                if DIRECTIONS[i][2]:
                    rows.append(z_shift(source[...], i, face)[row : row + 1])
                else:
                    rows.append(source[row : row + 1])
            out_ref[at : at + 1] = jnp.where(upward, rows[0], rows[1])
    end = start + 5 * size_x
    if out_ref.shape[0] > end:
        out_ref[end:] = jnp.zeros((out_ref.shape[0] - end, LANES), jnp.float32)


def middle_kernel(post_ref, low_ref, high_ref, other_ref, middle_ref):
    odd = lax.rem(lax.axis_index("gy"), 2) == 1
    face_rows(post_ref, low_ref, high_ref, other_ref, middle_ref, 0, odd)


def sides_kernel(post_ref, low_ref, high_ref, other_ref, middle_ref, beside_ref):
    size_y = post_ref.shape[2]
    odd = lax.rem(lax.axis_index("gy"), 2) == 1
    face_rows(post_ref, low_ref, high_ref, other_ref, middle_ref, 0, odd)
    face_rows(post_ref, low_ref, high_ref, other_ref, beside_ref, size_y, jnp.logical_not(odd))
    beside_ref[:size_y] = edge_tile(low_ref, high_ref)


def near_kernel(pair_ref, cross_ref, beside_ref, near_ref):
    near_ref[: 2 * FAB] = pair_ref[...]
    near_ref[2 * FAB : 4 * FAB] = cross_ref[...]
    near_ref[4 * FAB :] = beside_ref[beside_ref.shape[0] - (near_ref.shape[0] - 4 * FAB) :]


def shift_kernel(post_ref, low_ref, high_ref, other_ref, beside_ref, rolled_ref):
    size_x, size_y = post_ref.shape[1:3]
    for i in range(19):
        for x in range(size_x):
            tile = source_tile(post_ref, low_ref, high_ref, i, x)[...]
            from_x = x - DIRECTIONS[i][0]
            if 0 <= from_x < size_x:
                face = other_ref[FAB + from_x * size_y : FAB + (from_x + 1) * size_y]
            else:
                face = beside_ref[:size_y]
            tile = z_shift(tile, i, face)
            if DIRECTIONS[i][1]:
                tile = pltpu.roll(tile, DIRECTIONS[i][1] % size_y, 0)
            rolled_ref[i, x] = tile


def fabric_part(pairs, chips, start, my_node, column, at_lane, nodes, capacity):
    parts = nodes // LANES
    me = lax.axis_index("gy") * 2 + lax.axis_index("gz")
    slot_owner = iota((1, LANES), 1) // capacity
    owner_base = (slot_owner * nodes).astype(jnp.float32)
    matches, forces, picked = [], [], jnp.zeros((8, LANES), jnp.float32)
    for m in range(2 * len(pairs)):
        tile = pairs[m // 2][m % 2 * FAB : m % 2 * FAB + 8]
        ids = tile[0:1]
        ids = jnp.where(ids >= 0.0, owner_base + ids, -1.0)
        matches.append(one_hot(column == ids))
        forces.append(tile)
        shift = lax.rem((start + m + LANES // capacity - me) * capacity, LANES)
        picked = jnp.where(slot_owner == start + m, pltpu.roll(tile, shift, 1), picked)
    pushed = sum3(dot_nt(stacked3(jnp.concatenate(forces, axis=1)), jnp.concatenate(matches, axis=1)))

    found = sum3(dot_nn(stacked3(jnp.concatenate(pairs, axis=0)), at_lane))
    row = iota((FAB, LANES), 0)
    fits = (row >= 4) & (row % parts == (my_node.astype(jnp.int32) >> 7))
    base = jnp.zeros((FAB, LANES), jnp.float32)
    for m in range(2 * len(pairs)):
        owner = chips[m // 2] * 2 + m % 2
        base = jnp.where(fits & (slot_owner == owner), found[m * FAB : (m + 1) * FAB], base)
    return jnp.concatenate([pushed, base, picked], axis=0)


def half_kernel(seed_ref, pair_ref, cross_ref, acc_ref, column_ref, lane_ref):
    place_y = lax.axis_index("gy")
    nodes, capacity = 4 * LANES, LANES // 8
    my_node = seed_ref[0:1]
    owner_base = (iota((1, LANES), 1) // capacity * nodes).astype(jnp.float32)
    my_id = jnp.where(my_node >= 0.0, owner_base + my_node, -2.0)
    column = jnp.transpose(jnp.broadcast_to(my_id, (LANES, LANES)))
    at_lane = one_hot(iota((LANES, LANES), 0) == (my_node.astype(jnp.int32) & (LANES - 1)))
    pairs, chips = [pair_ref[...], cross_ref[...]], [place_y, place_y ^ 2]
    acc_ref[...] = fabric_part(pairs, chips, 0, my_node, column, at_lane, nodes, capacity)
    column_ref[...] = column
    lane_ref[...] = at_lane


def final_kernel(
    rolled_ref, kind_ref, back_ref, seed_ref, acc_ref, column_ref, lane_ref, near_ref, middle_ref, pos_ref,
    pop_hbm, pos_hbm, vel_hbm, wall_hbm,
    pop_ref, pos_out_ref, vel_out_ref, wall_out_ref, sems,
):
    size_x, size_y = rolled_ref.shape[1:3]
    place_y = lax.axis_index("gy")
    odd = lax.rem(place_y, 2) == 1
    first, top = place_y == 0, place_y == lax.axis_size("gy") - 1
    sub = iota((size_y, LANES), 0)
    owners, capacity = wall_out_ref.shape[4], wall_out_ref.shape[5]
    nodes = pos_ref.shape[2]
    parts = nodes // LANES
    mine = seed_ref[:FAB]
    pairs, chips = [near_ref[: 2 * FAB], near_ref[2 * FAB : 4 * FAB]], [place_y ^ 1, place_y ^ 3]
    acc = fabric_part(pairs, chips, 4, mine[0:1], column_ref[...], lane_ref[...], nodes, capacity) + acc_ref[...]
    copies = []
    for x in range(size_x):
        kind = kind_ref[x]
        back = back_ref[x]
        for i in range(19):
            tile = rolled_ref[i, x]
            if DIRECTIONS[i][1]:
                side = 0 if DIRECTIONS[i][1] == 1 else 1
                at = SIDES[1][side].index(i) * size_x + x
                by_near = near_ref[4 * FAB + at : 4 * FAB + at + 1]
                by_middle = middle_ref[at : at + 1]
                if side == 0:
                    row = jnp.where(first, WEIGHTS[i], jnp.where(odd, by_near, by_middle))
                    tile = jnp.where(sub == 0, row, tile)
                else:
                    row = jnp.where(top, WEIGHTS[i], jnp.where(odd, by_middle, by_near))
                    tile = jnp.where(sub == size_y - 1, row, tile)
            if i:
                tile = jnp.where(kind == float(i), back, tile)
            pop_ref[i, x] = tile

    pushed, found, picked = acc[:8], acc[8:24], acc[24:32]
    node = picked[0:1].astype(jnp.int32)
    row = iota((FAB, LANES), 0)
    spread = jnp.where(row < parts, picked[1:2], jnp.where(row < 2 * parts, picked[2:3], picked[3:4]))
    spread = jnp.where((row < 3 * parts) & (row % parts == (node >> 7)), spread, 0.0)
    at_node = one_hot(iota((LANES, LANES), 0) == (node & (LANES - 1)))
    fluid = sum3(dot_nt(stacked3(spread), at_node))
    my_live = mine[0:1] >= 0.0
    moved = []
    for a in range(3):
        for k in range(parts):
            r = a * parts + k
            new = mine[4 + r : 5 + r] + fluid[r : r + 1]
            at = slice(k * LANES, (k + 1) * LANES)
            vel_out_ref[a, :, at] = new
            pos_out_ref[a, :, at] = pos_ref[a, :, at] + new
        base = jnp.sum(found[4 + a * parts : 4 + (a + 1) * parts], axis=0, keepdims=True)
        moved.append(jnp.where(my_live, base + pushed[1 + a : 2 + a], 0.0))
    moved = jnp.concatenate(moved + [jnp.zeros((5, LANES), jnp.float32)], axis=0)
    for o in range(owners):
        turned = pltpu.roll(moved, LANES - o * capacity, 1) if o else moved
        for a in range(3):
            wall_out_ref[0, 0, 0, a, o : o + 1] = turned[a : a + 1, :capacity]
    copies.append(pltpu.make_async_copy(pop_ref, pop_hbm, sems.at[0]))
    copies[-1].start()
    for k, (src, dst) in enumerate(((vel_out_ref, vel_hbm), (pos_out_ref, pos_hbm), (wall_out_ref, wall_hbm))):
        copies.append(pltpu.make_async_copy(src, dst, sems.at[size_x + k]))
        copies[-1].start()
    for copy in copies:
        copy.wait()


def ring(count, step):
    return [(i, (i + step) % count) for i in range(count)]


def body(
    populations,
    solid,
    link_cell,
    link_dir,
    link_node,
    link_velocity,
    fabric_position,
    fabric_velocity,
    fabric_rest,
    triangles,
):
    size_x, size_y, size_z = populations.shape[1:]
    owners, capacity = link_node.shape[3:]
    nodes = fabric_position.shape[2]
    count_x, count_y, count_z = (lax.axis_size(name) for name in ("gx", "gy", "gz"))
    folded = (
        (count_y, count_z) == (4, 2)
        and (size_y, size_z) == (8, LANES)
        and owners * capacity == LANES
        and nodes == 4 * LANES
    )
    if not folded:
        return general_body(
            populations, solid, link_cell, link_dir, link_node, link_velocity,
            fabric_position, fabric_velocity, fabric_rest, triangles,
        )
    f32 = jnp.float32
    on_chip = pl.BlockSpec(memory_space=pltpu.VMEM)

    def shape(*dims):
        return jax.ShapeDtypeStruct(dims, f32)

    def kept(*dims):
        return pltpu.VMEM(dims, f32)

    def run(kernel, outs, *args):
        args = [pltpu.with_memory_space_constraint(arg, pltpu.VMEM) for arg in args]
        return pl.pallas_call(
            kernel,
            out_shape=outs,
            in_specs=[on_chip] * len(args),
            out_specs=jax.tree.map(lambda _: on_chip, outs),
            name=kernel.__name__,
        )(*args)

    face_x = kept(5, size_y, size_z)
    map_shape = kept(size_x, size_y, size_z)
    given = (
        populations, solid, link_cell, link_dir, link_node, link_velocity,
        fabric_position, fabric_velocity, fabric_rest, triangles,
    )
    cells = size_x * size_y
    opened = (kept(*populations.shape), face_x, face_x, kept(max(SEED, FAB + cells), LANES), map_shape, map_shape, kept(*fabric_position.shape))
    post, up, down, seed, kind, back, position = pl.pallas_call(
        open_kernel,
        out_shape=opened,
        in_specs=[pl.BlockSpec(memory_space=pl.ANY)] * len(given),
        out_specs=(on_chip,) * len(opened),
        scratch_shapes=[pltpu.VMEM(arg.shape, arg.dtype) for arg in given if arg is not fabric_position]
        + [pltpu.SemaphoreType.DMA((len(given),))],
        name="open_kernel",
    )(*given)
    swap_z = [(0, 1), (1, 0)]
    other = lax.ppermute(seed, "gz", swap_z)
    xlow = lax.ppermute(up, "gx", ring(count_x, 1))
    xhigh = lax.ppermute(down, "gx", ring(count_x, -1))
    (pair,) = run(pair_kernel, (kept(2 * FAB, LANES),), seed, other)
    crossing = [(y * 2 + z, (y ^ 2) * 2 + 1 - z) for y in range(count_y) for z in range(2)]
    cross = lax.ppermute(pair, ("gy", "gz"), crossing)
    middling = []
    for y in range(count_y):
        to = y + 1 if y % 2 else y - 1
        for z in range(count_z):
            middling.append((y * 2 + z, to * 2 + z if 0 <= to < count_y else y * 2 + 1 - z))
    rows = -(-5 * size_x // 8) * 8
    middle, beside = run(
        sides_kernel, (kept(MID * rows, LANES), kept(size_y + rows, LANES)), post, xlow, xhigh, other
    )
    middle = lax.ppermute(middle, ("gy", "gz"), middling)
    beside = lax.ppermute(beside, "gz", swap_z)
    (near,) = run(near_kernel, (kept(4 * FAB + rows, LANES),), pair, cross, beside)
    nearing = [(y * 2 + z, (y ^ 1) * 2 + 1 - z) for y in range(count_y) for z in range(2)]
    near = lax.ppermute(near, ("gy", "gz"), nearing)
    (rolled,) = run(shift_kernel, (kept(*populations.shape),), post, xlow, xhigh, other, beside)
    halves = (kept(32, LANES), kept(LANES, LANES), pltpu.VMEM((LANES, LANES), jnp.bfloat16))
    acc, column, at_lane = run(half_kernel, halves, seed, pair, cross)
    outs = (
        shape(*populations.shape),
        shape(*fabric_position.shape),
        shape(*fabric_velocity.shape),
        shape(*link_velocity.shape),
    )
    last = [rolled, kind, back, seed, acc, column, at_lane, near, middle, position]
    last = [pltpu.with_memory_space_constraint(arg, pltpu.VMEM) for arg in last]
    return pl.pallas_call(
        final_kernel,
        out_shape=outs,
        in_specs=[on_chip] * len(last),
        out_specs=(pl.BlockSpec(memory_space=pl.ANY),) * 4,
        scratch_shapes=[pltpu.VMEM(out.shape, f32) for out in outs] + [pltpu.SemaphoreType.DMA((size_x + 3,))],
        name="final_kernel",
    )(*last)


def solution(mesh):
    placed = (
        P(None, "gx", "gy", "gz"),
        P("gx", "gy", "gz"),
        P("gx", "gy", "gz", None, None),
        P("gx", "gy", "gz", None, None),
        P("gx", "gy", "gz", None, None),
        P("gx", "gy", "gz", None, None, None),
        P(None, "gx", ("gy", "gz")),
        P(None, "gx", ("gy", "gz")),
        P(None, "gx", ("gy", "gz")),
        P(None, "gx", ("gy", "gz")),
    )
    return jax.shard_map(
        body,
        mesh=mesh,
        in_specs=placed,
        out_specs=(
            P(None, "gx", "gy", "gz"),
            P(None, "gx", ("gy", "gz")),
            P(None, "gx", ("gy", "gz")),
            P("gx", "gy", "gz", None, None, None),
        ),
        check_vma=False,
    )
```

```python
import jax
import jax.numpy as jnp
import numpy as np
from jax import lax
from jax.experimental import pallas as pl
from jax.experimental.pallas import tpu as pltpu
from jax.sharding import PartitionSpec as P

SPRING = 0.5
DAMPING = 0.1
DIRECTIONS = [
    [0, 0, 0],
    [1, 0, 0],
    [-1, 0, 0],
    [0, 1, 0],
    [0, -1, 0],
    [0, 0, 1],
    [0, 0, -1],
    [1, 1, 0],
    [-1, -1, 0],
    [1, -1, 0],
    [-1, 1, 0],
    [1, 0, 1],
    [-1, 0, -1],
    [1, 0, -1],
    [-1, 0, 1],
    [0, 1, 1],
    [0, -1, -1],
    [0, 1, -1],
    [0, -1, 1],
]


def extended(cells, sides, width):
    for axis, dim in sides:
        count = lax.axis_size(axis)
        head = lax.slice_in_dim(cells, 0, width, axis=dim)
        tail = lax.slice_in_dim(cells, cells.shape[dim] - width, cells.shape[dim], axis=dim)
        cells = jnp.concatenate(
            [
                lax.ppermute(tail, axis, [(i, (i + 1) % count) for i in range(count)]),
                cells,
                lax.ppermute(head, axis, [((i + 1) % count, i) for i in range(count)]),
            ],
            axis=dim,
        )
    return cells


def lattice():
    velocity_np = np.array(DIRECTIONS)
    weight_np = np.array([1.0 / 3.0] + [1.0 / 18.0] * 6 + [1.0 / 36.0] * 12)
    opposite_list = [
        DIRECTIONS.index([-entry for entry in DIRECTIONS[direction]]) for direction in range(19)
    ]
    along_a = np.array([float(entry[0]) for entry in DIRECTIONS])
    along_b = np.array([float(entry[1]) for entry in DIRECTIONS])
    along_e = np.array([float(entry[2]) for entry in DIRECTIONS])
    speed_sq = along_a * along_a + along_b * along_b + along_e * along_e
    moment_rows = [
        np.ones(19),
        19 * speed_sq - 30,
        (21 * speed_sq * speed_sq - 53 * speed_sq + 24) / 2,
        along_a,
        (5 * speed_sq - 9) * along_a,
        along_b,
        (5 * speed_sq - 9) * along_b,
        along_e,
        (5 * speed_sq - 9) * along_e,
        3 * along_a * along_a - speed_sq,
        (3 * speed_sq - 5) * (3 * along_a * along_a - speed_sq),
        along_b * along_b - along_e * along_e,
        (3 * speed_sq - 5) * (along_b * along_b - along_e * along_e),
        along_a * along_b,
        along_b * along_e,
        along_a * along_e,
        (along_b * along_b - along_e * along_e) * along_a,
        (along_e * along_e - along_a * along_a) * along_b,
        (along_a * along_a - along_b * along_b) * along_e,
    ]
    moment_np = np.stack(moment_rows)
    inverse_np = moment_np.T / np.sum(moment_np * moment_np, axis=1)[None, :]
    viscous = 5.0 / 3.0
    rates_np = np.array(
        [
            0.0,
            1.19,
            1.4,
            0.0,
            1.2,
            0.0,
            1.2,
            0.0,
            1.2,
            viscous,
            1.4,
            viscous,
            1.4,
            viscous,
            viscous,
            viscous,
            1.98,
            1.98,
            1.98,
        ]
    )
    return (velocity_np, weight_np, opposite_list, moment_np, inverse_np, rates_np)


def collide_cells(popul, solid_flat):
    velocity_np, weight_np, opposite_list, moment_np, inverse_np, rates_np = lattice()
    velocity_table = jnp.asarray(velocity_np, jnp.float32)
    weight_table = jnp.asarray(weight_np, jnp.float32)
    density = jnp.sum(popul, axis=0)
    momentum = jnp.dot(
        velocity_table.T, popul, precision=lax.Precision.HIGHEST, preferred_element_type=jnp.float32
    )
    flow = momentum / density
    projected = jnp.dot(
        velocity_table, flow, precision=lax.Precision.HIGHEST, preferred_element_type=jnp.float32
    )
    speed_sq = jnp.sum(flow * flow, axis=0)
    equilibrium = (
        weight_table[:, None]
        * density
        * (1.0 + 3.0 * projected + 4.5 * projected * projected - 1.5 * speed_sq)
    )
    offset = popul - equilibrium
    moments = jnp.dot(
        jnp.asarray(moment_np, jnp.float32),
        offset,
        precision=lax.Precision.HIGHEST,
        preferred_element_type=jnp.float32,
    )
    relaxed = jnp.asarray(rates_np, jnp.float32)[:, None] * moments
    change = jnp.dot(
        jnp.asarray(inverse_np, jnp.float32),
        relaxed,
        precision=lax.Precision.HIGHEST,
        preferred_element_type=jnp.float32,
    )
    return jnp.where(solid_flat[None, :] == 1, popul, popul - change)


def fill_outside(padded, weight_np):
    span_y = padded.shape[2]
    span_z = padded.shape[3]
    place_y = lax.axis_index("gy")
    place_z = lax.axis_index("gz")
    count_y = lax.axis_size("gy")
    count_z = lax.axis_size("gz")
    rows_y = jnp.arange(span_y)
    rows_z = jnp.arange(span_z)
    out_y = (rows_y == 0) & (place_y == 0) | (rows_y == span_y - 1) & (place_y == count_y - 1)
    out_z = (rows_z == 0) & (place_z == 0) | (rows_z == span_z - 1) & (place_z == count_z - 1)
    outside = out_y[:, None] | out_z[None, :]
    return jnp.where(
        outside[None, None], jnp.asarray(weight_np, jnp.float32)[:, None, None, None], padded
    )


def propagate(padded, size_x, size_y, size_z):
    pieces = []
    for direction in range(19):
        shift_x = DIRECTIONS[direction][0]
        shift_y = DIRECTIONS[direction][1]
        shift_z = DIRECTIONS[direction][2]
        plane = padded[direction]
        pieces.append(
            lax.slice(
                plane,
                (1 - shift_x, 1 - shift_y, 1 - shift_z),
                (1 - shift_x + size_x, 1 - shift_y + size_y, 1 - shift_z + size_z),
            )
        )
    return jnp.stack(pieces)


def membrane(positions, rest, triangle_nodes):
    force = jnp.zeros(positions.shape, jnp.float32)
    for first, second in ((0, 1), (1, 2), (2, 0)):
        head = triangle_nodes[first]
        tail = triangle_nodes[second]
        stretch = positions[:, tail] - positions[:, head] - (rest[:, tail] - rest[:, head])
        force = force.at[:, head].add(SPRING * stretch)
        force = force.at[:, tail].add(-SPRING * stretch)
    return force


def general_body(
    populations,
    solid,
    link_cell,
    link_dir,
    link_node,
    link_velocity,
    fabric_position,
    fabric_velocity,
    fabric_rest,
    triangles,
):
    velocity_np, weight_np, opposite_list, moment_np, inverse_np, rates_np = lattice()
    velocity_table = jnp.asarray(velocity_np, jnp.float32)
    weight_table = jnp.asarray(weight_np, jnp.float32)
    opposite_table = jnp.asarray(opposite_list, jnp.int32)
    size_x = populations.shape[1]
    size_y = populations.shape[2]
    size_z = populations.shape[3]
    cells = size_x * size_y * size_z
    post = collide_cells(populations.reshape(19, cells), solid.reshape(cells)).reshape(
        populations.shape
    )
    padded = extended(post, (("gx", 1), ("gy", 2), ("gz", 3)), 1)
    padded = fill_outside(padded, weight_np)
    propagated = propagate(padded, size_x, size_y, size_z).reshape(19, cells)
    owners_n = link_node.shape[3]
    capacity = link_node.shape[4]
    node_rows = link_node.reshape(owners_n, capacity)
    cell_rows = link_cell.reshape(owners_n, capacity)
    dir_rows = link_dir.reshape(owners_n, capacity)
    live = node_rows >= 0
    post_flat = post.reshape(19, cells)
    reflected = post_flat[opposite_table[dir_rows], cell_rows]
    link_unit = velocity_table[dir_rows]
    wall = jnp.moveaxis(link_velocity.reshape(3, owners_n, capacity), 0, -1)
    returned = reflected + 6.0 * weight_table[dir_rows] * jnp.sum(link_unit * wall, axis=-1)
    populations_next = propagated.at[jnp.where(live, dir_rows, 19), cell_rows].set(
        returned, mode="drop"
    )
    strength = reflected + returned
    positions = fabric_position.reshape(3, -1)
    velocities = fabric_velocity.reshape(3, -1)
    rest = fabric_rest.reshape(3, -1)
    nodes_n = positions.shape[1]
    elastic = membrane(positions, rest, triangles.reshape(3, -1))
    link_force = jnp.moveaxis(-link_unit * strength[..., None], -1, 0)
    got_nodes, got_force = (
        lax.all_to_all(node_rows[None], ("gy", "gz"), split_axis=1, concat_axis=1, tiled=True),
        lax.all_to_all(link_force, ("gy", "gz"), split_axis=1, concat_axis=1, tiled=True),
    )
    got_ids = got_nodes[0]
    got_live = got_ids >= 0
    target = jnp.where(got_live, got_ids, nodes_n).reshape(-1)
    fluid_force = (
        jnp.zeros((3, nodes_n), jnp.float32)
        .at[:, target]
        .add(got_force.reshape(3, -1), mode="drop")
    )
    velocity_next = (1.0 - DAMPING) * velocities + (fluid_force + elastic)
    position_next = positions + velocity_next
    reply = jnp.where(got_live[None], velocity_next[:, jnp.where(got_live, got_ids, 0)], 0.0)
    wall_next = lax.all_to_all(reply, ("gy", "gz"), split_axis=1, concat_axis=1, tiled=True)
    return (
        populations_next.reshape(populations.shape),
        position_next.reshape(fabric_position.shape),
        velocity_next.reshape(fabric_velocity.shape),
        wall_next.reshape(link_velocity.shape),
    )


WEIGHTS = [1.0 / 3.0] + [1.0 / 18.0] * 6 + [1.0 / 36.0] * 12
OPPOSITE = [DIRECTIONS.index([-entry for entry in d]) for d in DIRECTIONS]
SIDES = [
    ([i for i in range(19) if DIRECTIONS[i][a] == 1], [i for i in range(19) if DIRECTIONS[i][a] == -1])
    for a in range(3)
]
LANES = 128
PATCH = 256
FAB = 16
SEED = 56
MID = 4


def iota(shape, axis):
    return lax.broadcasted_iota(jnp.int32, shape, axis)


def split3(value):
    high = value.astype(jnp.bfloat16).astype(jnp.float32)
    rest = value - high
    middle = rest.astype(jnp.bfloat16).astype(jnp.float32)
    return high, middle, rest - middle


def stacked3(value):
    return jnp.concatenate(split3(value), axis=0).astype(jnp.bfloat16)


def sum3(value):
    rows = value.shape[0] // 3
    return value[:rows] + value[rows : 2 * rows] + value[2 * rows :]


def dot_nn(left, right):
    return lax.dot_general(left, right, (((1,), (0,)), ((), ())), preferred_element_type=jnp.float32)


def dot_nt(left, right):
    return lax.dot_general(left, right, (((1,), (1,)), ((), ())), preferred_element_type=jnp.float32)


def one_hot(mask):
    return jnp.where(mask, 1.0, 0.0).astype(jnp.bfloat16)


def collided(f, solid):
    sx, dx = f[1] + f[2], f[1] - f[2]
    sy, dy = f[3] + f[4], f[3] - f[4]
    sz, dz = f[5] + f[6], f[5] - f[6]
    sa, da = f[7] + f[8], f[7] - f[8]
    sb, db = f[9] + f[10], f[9] - f[10]
    sc, dc = f[11] + f[12], f[11] - f[12]
    sd, dd = f[13] + f[14], f[13] - f[14]
    se, de = f[15] + f[16], f[15] - f[16]
    sg, dg = f[17] + f[18], f[17] - f[18]
    sxy, txy = sa + sb, sa - sb
    sxz, txz = sc + sd, sc - sd
    syz, tyz = se + sg, se - sg
    ax_ab, ay_ab = da + db, da - db
    ax_cd, az_cd = dc + dd, dc - dd
    ay_eg, az_eg = de + dg, de - dg
    near, far = sx + sy + sz, sxy + sxz + syz
    rho = f[0] + near + far
    ex, ey, ez = ax_ab + ax_cd, ay_ab + ay_eg, az_cd + az_eg
    jx, jy, jz = dx + ex, dy + ey, dz + ez
    inv = 1.0 / rho
    ux, uy, uz = jx * inv, jy * inv, jz * inv
    xx, yy, zz = jx * ux, jy * uy, jz * uz
    jj = xx + yy + zz
    energy = (-30.0 * f[0] - 11.0 * near + 8.0 * far) - (-11.0 * rho + 19.0 * jj)
    square = (12.0 * f[0] - 4.0 * near + far) - (3.0 * rho - 5.5 * jj)
    kx = (1.2 / 40.0) * (ex - 4.0 * dx + (2.0 / 3.0) * jx)
    ky = (1.2 / 40.0) * (ey - 4.0 * dy + (2.0 / 3.0) * jy)
    kz = (1.2 / 40.0) * (ez - 4.0 * dz + (2.0 / 3.0) * jz)
    yz_near, xyz_far = sy + sz, sxy + sxz - 2.0 * syz
    pxx_eq = 2.0 * xx - yy - zz
    pww_eq = yy - zz
    pxx = (5.0 / 3.0 / 36.0) * (2.0 * sx - yz_near + xyz_far - pxx_eq)
    pixx = (1.4 / 72.0) * (-4.0 * sx + 2.0 * yz_near + xyz_far + 0.5 * pxx_eq)
    w_near, w_far = sy - sz, sxy - sxz
    pww = (5.0 / 3.0 / 12.0) * (w_near + w_far - pww_eq)
    piww = (1.4 / 24.0) * (w_far - 2.0 * w_near + 0.5 * pww_eq)
    pxy = (5.0 / 3.0 / 4.0) * (txy - jx * uy)
    pyz = (5.0 / 3.0 / 4.0) * (tyz - jy * uz)
    pxz = (5.0 / 3.0 / 4.0) * (txz - jx * uz)
    mx = (1.98 / 8.0) * (ax_ab - ax_cd)
    my = (1.98 / 8.0) * (ay_eg - ay_ab)
    mz = (1.98 / 8.0) * (az_cd - az_eg)
    energy = (1.19 / 2394.0) * energy
    square = (1.4 / 252.0) * square
    axis = -11.0 * energy - 4.0 * square
    across = pxx - 2.0 * pixx
    split = pww - 2.0 * piww
    edge = 8.0 * energy + square
    pp, ww = pxx + pixx, pww + piww
    even = [
        axis + 2.0 * across,
        axis - across + split,
        axis - across - split,
        edge + pp + ww + pxy,
        edge + pp + ww - pxy,
        edge + pp - ww + pxz,
        edge + pp - ww - pxz,
        edge - 2.0 * pp + pyz,
        edge - 2.0 * pp - pyz,
    ]
    odd = [
        -4.0 * kx,
        -4.0 * ky,
        -4.0 * kz,
        (kx + mx) + (ky - my),
        (kx + mx) - (ky - my),
        (kx - mx) + (kz + mz),
        (kx - mx) - (kz + mz),
        (ky + my) + (kz - mz),
        (ky + my) - (kz - mz),
    ]
    change = [12.0 * square - 30.0 * energy]
    for pair in range(9):
        change += [even[pair] + odd[pair], even[pair] - odd[pair]]
    fluid = solid != 1
    return [jnp.where(fluid, f[i] - change[i], f[i]) for i in range(19)]


def slots_to_row(value):
    owners, capacity = value.shape
    wide = jnp.concatenate([value, jnp.zeros((owners, LANES - capacity), value.dtype)], axis=1)
    return jnp.sum(pltpu.roll(wide, 0, 1, stride=capacity, stride_axis=0), axis=0, keepdims=True)


def membrane_start(pos_ref, rest_ref, tri_ref):
    nodes = pos_ref.shape[2]
    count = tri_ref.shape[2]
    wide = -(-count // LANES) * LANES
    patches = nodes // PATCH
    stretch = [pos_ref[a] - rest_ref[a] for a in range(3)]
    corners = [
        jnp.concatenate([tri_ref[t], jnp.full((1, wide - count), -1, jnp.int32)], axis=1) for t in range(3)
    ]
    patch = jnp.maximum(corners[0], 0) // PATCH
    local = [(corner - patch * PATCH).astype(jnp.float32) for corner in corners]
    node_ids = iota((PATCH, LANES), 0).astype(jnp.float32).astype(jnp.bfloat16)
    blocks = []
    for k in range(0, wide, LANES):
        block = jnp.zeros((PATCH, LANES), jnp.bfloat16)
        for corner in local:
            row = jnp.broadcast_to(corner[:, k : k + LANES], (16, LANES)).astype(jnp.bfloat16)
            row = jnp.concatenate([row] * (PATCH // 16), axis=0)
            block = block + jnp.where(node_ids == row, jnp.ones_like(block), jnp.zeros_like(block))
        blocks.append(block)
    hits = jnp.concatenate(blocks, axis=1)
    stretch8 = jnp.concatenate(stretch + [jnp.zeros((5, nodes), jnp.float32)], axis=0)
    pieces = [stacked3(stretch8[:, p * PATCH : (p + 1) * PATCH]) for p in range(patches)]
    sums = dot_nn(jnp.concatenate(pieces, axis=0), hits)
    total = jnp.zeros((8, wide), jnp.float32)
    for p in range(patches):
        total = jnp.where(patch == p, sum3(sums[p * 24 : (p + 1) * 24]), total)
    return stretch, hits, total, patch


def membrane_finish(parts, vel_ref, fab_ref):
    stretch, hits, total, patch = parts
    nodes = vel_ref.shape[2]
    patches = nodes // PATCH
    total = jnp.where(iota(total.shape, 0) == 3, 1.0, total)
    pieces = [stacked3(jnp.where(patch == p, total, 0.0)) for p in range(patches)]
    sums = dot_nt(jnp.concatenate(pieces, axis=0), hits)
    back = jnp.concatenate([sum3(sums[p * 24 : (p + 1) * 24]) for p in range(patches)], axis=1)
    for a in range(3):
        elastic = SPRING * back[a : a + 1] - 3.0 * SPRING * back[3:4] * stretch[a]
        base = (1.0 - DAMPING) * vel_ref[a] + elastic
        for k in range(nodes // LANES):
            row = 4 + a * (nodes // LANES) + k
            fab_ref[row : row + 1] = base[:, k * LANES : (k + 1) * LANES]


def z_face(tiles):
    up = jnp.zeros_like(next(t for t in tiles if t is not None))
    lane = iota(up.shape, 1)
    down = up
    for k in range(5):
        i, j = SIDES[2][0][k], SIDES[2][1][k]
        if tiles[i] is not None:
            up = jnp.where(lane == k, pltpu.roll(tiles[i], k + 1, 1), up)
        if tiles[j] is not None:
            down = jnp.where(lane == k, pltpu.roll(tiles[j], k, 1) if k else tiles[j], down)
    return jnp.where(lax.axis_index("gz") == 0, up, down)


def z_shift(tile, i, face):
    lane = iota(tile.shape, 1)
    low_end = lax.axis_index("gz") == 0
    if DIRECTIONS[i][2] == 1:
        k = SIDES[2][0].index(i)
        halo = pltpu.roll(face, LANES - k, 1) if k else face
        return jnp.where(lane == 0, jnp.where(low_end, WEIGHTS[i], halo), pltpu.roll(tile, 1, 1))
    if DIRECTIONS[i][2] == -1:
        k = SIDES[2][1].index(i)
        halo = pltpu.roll(face, LANES - 1 - k, 1)
        return jnp.where(lane == LANES - 1, jnp.where(low_end, halo, WEIGHTS[i]), pltpu.roll(tile, LANES - 1, 1))
    return tile


def open_kernel(
    pop_hbm, solid_hbm, cell_hbm, dir_hbm, node_hbm, wall_hbm, pos_hbm, vel_hbm, rest_hbm, tri_hbm,
    post_ref, up_ref, down_ref, seed_ref, kind_ref, back_ref, pos_ref,
    pop_ref, solid_ref, cell_ref, dir_ref, node_ref, wall_ref, vel_ref, rest_ref, tri_ref, sems,
):
    moves = [
        (pop_hbm, pop_ref), (solid_hbm, solid_ref),
        (tri_hbm, tri_ref), (pos_hbm, pos_ref), (rest_hbm, rest_ref), (vel_hbm, vel_ref),
        (cell_hbm, cell_ref), (dir_hbm, dir_ref), (node_hbm, node_ref), (wall_hbm, wall_ref),
    ]
    copies = [pltpu.make_async_copy(src, dst, sems.at[k]) for k, (src, dst) in enumerate(moves)]
    for copy in copies[6:] + copies[2:6] + copies[:2]:
        copy.start()
    for copy in copies[2:]:
        copy.wait()
    parts = membrane_start(pos_ref, rest_ref, tri_ref)
    size_x, size_y = post_ref.shape[1:3]
    rows = size_x * size_y
    cell = slots_to_row(cell_ref[0, 0, 0].astype(jnp.float32)).astype(jnp.int32)
    way = slots_to_row(dir_ref[0, 0, 0].astype(jnp.float32))
    node = slots_to_row(node_ref[0, 0, 0].astype(jnp.float32))
    live = node >= 0.0
    unit = []
    for a in range(3):
        u = jnp.zeros_like(way)
        for i in range(1, 19):
            if DIRECTIONS[i][a]:
                u = jnp.where(way == float(i), float(DIRECTIONS[i][a]), u)
        unit.append(u)
    weight = jnp.where(way >= 7.0, 6.0 / 36.0, 6.0 / 18.0)
    wall = [slots_to_row(wall_ref[0, 0, 0, a]) for a in range(3)]
    term = weight * (unit[0] * wall[0] + unit[1] * wall[1] + unit[2] * wall[2])
    at_row = jnp.where((iota((rows, LANES), 0) == (cell >> 7)) & live, 1.0, 0.0)
    at_lane = one_hot(iota((LANES, LANES), 0) == (cell & (LANES - 1)))
    left = jnp.concatenate([at_row * way] + [at_row * t for t in split3(term)], axis=0)
    maps = dot_nt(left.astype(jnp.bfloat16), at_lane)
    kind = maps[:rows]
    added = sum3(maps[rows:])
    for copy in copies[:2]:
        copy.wait()
    taken = []
    membrane_finish(parts, vel_ref, seed_ref)
    for x in range(size_x):
        post = collided([pop_ref[i, x] for i in range(19)], solid_ref[x])
        k = kind[x * size_y : (x + 1) * size_y]
        t = jnp.zeros_like(k)
        for i in range(19):
            post_ref[i, x] = post[i]
            if x == size_x - 1 and i in SIDES[0][0]:
                up_ref[SIDES[0][0].index(i)] = post[i]
            if x == 0 and i in SIDES[0][1]:
                down_ref[SIDES[0][1].index(i)] = post[i]
            if i:
                t = jnp.where(k == float(OPPOSITE[i]), post[i], t)
        seed_ref[FAB + x * size_y : FAB + (x + 1) * size_y] = z_face(post)
        taken.append(t)
        kind_ref[x] = k
        back_ref[x] = t + added[x * size_y : (x + 1) * size_y]
    strength = 2.0 * jnp.concatenate(taken, axis=0) + added
    at_link = sum3(dot_nn(stacked3(strength), at_lane))
    push = jnp.sum(at_row * at_link, axis=0, keepdims=True)
    seed_ref[0:1] = node
    for a in range(3):
        seed_ref[1 + a : 2 + a] = -unit[a] * push
    end = FAB + rows
    seed_ref[end:] = jnp.zeros((seed_ref.shape[0] - end, LANES), jnp.float32)


def source_tile(post_ref, low_ref, high_ref, i, x):
    size_x = post_ref.shape[1]
    from_x = x - DIRECTIONS[i][0]
    if from_x < 0:
        return low_ref.at[SIDES[0][0].index(i)]
    if from_x >= size_x:
        return high_ref.at[SIDES[0][1].index(i)]
    return post_ref.at[i, from_x]


def pair_kernel(seed_ref, other_ref, pair_ref):
    low = lax.axis_index("gz") == 0
    pair_ref[:FAB] = jnp.where(low, seed_ref[:FAB], other_ref[:FAB])
    pair_ref[FAB:] = jnp.where(low, other_ref[:FAB], seed_ref[:FAB])


def edge_tile(low_ref, high_ref):
    tiles = [None] * 19
    for i in range(19):
        if DIRECTIONS[i][0] and DIRECTIONS[i][2]:
            side = 0 if DIRECTIONS[i][0] == 1 else 1
            tiles[i] = (low_ref, high_ref)[side][SIDES[0][side].index(i)]
    return z_face(tiles)


def face_rows(post_ref, low_ref, high_ref, other_ref, out_ref, start, upward):
    size_x, size_y = post_ref.shape[1:3]
    for k in range(5):
        for x in range(size_x):
            at = start + k * size_x + x
            face = other_ref[FAB + x * size_y : FAB + (x + 1) * size_y]
            rows = []
            for side, row in ((0, size_y - 1), (1, 0)):
                i = SIDES[1][side][k]
                source = source_tile(post_ref, low_ref, high_ref, i, x)
                if DIRECTIONS[i][2]:
                    rows.append(z_shift(source[...], i, face)[row : row + 1])
                else:
                    rows.append(source[row : row + 1])
            out_ref[at : at + 1] = jnp.where(upward, rows[0], rows[1])
    end = start + 5 * size_x
    if out_ref.shape[0] > end:
        out_ref[end:] = jnp.zeros((out_ref.shape[0] - end, LANES), jnp.float32)


def middle_kernel(post_ref, low_ref, high_ref, other_ref, middle_ref):
    odd = lax.rem(lax.axis_index("gy"), 2) == 1
    face_rows(post_ref, low_ref, high_ref, other_ref, middle_ref, 0, odd)


def sides_kernel(post_ref, low_ref, high_ref, other_ref, middle_ref, beside_ref):
    size_y = post_ref.shape[2]
    odd = lax.rem(lax.axis_index("gy"), 2) == 1
    face_rows(post_ref, low_ref, high_ref, other_ref, middle_ref, 0, odd)
    face_rows(post_ref, low_ref, high_ref, other_ref, beside_ref, size_y, jnp.logical_not(odd))
    beside_ref[:size_y] = edge_tile(low_ref, high_ref)


def near_kernel(pair_ref, cross_ref, beside_ref, near_ref):
    near_ref[: 2 * FAB] = pair_ref[...]
    near_ref[2 * FAB : 4 * FAB] = cross_ref[...]
    near_ref[4 * FAB :] = beside_ref[beside_ref.shape[0] - (near_ref.shape[0] - 4 * FAB) :]


def shift_kernel(post_ref, low_ref, high_ref, other_ref, beside_ref, kind_ref, back_ref, rolled_ref):
    size_x, size_y = post_ref.shape[1:3]
    for i in range(19):
        for x in range(size_x):
            tile = source_tile(post_ref, low_ref, high_ref, i, x)[...]
            from_x = x - DIRECTIONS[i][0]
            if 0 <= from_x < size_x:
                face = other_ref[FAB + from_x * size_y : FAB + (from_x + 1) * size_y]
            else:
                face = beside_ref[:size_y]
            tile = z_shift(tile, i, face)
            if DIRECTIONS[i][1]:
                tile = pltpu.roll(tile, DIRECTIONS[i][1] % size_y, 0)
            rolled_ref[i, x] = jnp.where(kind_ref[x] == float(i), back_ref[x], tile) if i else tile


def fabric_part(pairs, chips, start, my_node, column, at_lane, nodes, capacity):
    parts = nodes // LANES
    me = lax.axis_index("gy") * 2 + lax.axis_index("gz")
    slot_owner = iota((1, LANES), 1) // capacity
    owner_base = (slot_owner * nodes).astype(jnp.float32)
    matches, forces, picked = [], [], jnp.zeros((8, LANES), jnp.float32)
    for m in range(2 * len(pairs)):
        tile = pairs[m // 2][m % 2 * FAB : m % 2 * FAB + 8]
        ids = tile[0:1]
        ids = jnp.where(ids >= 0.0, owner_base + ids, -1.0)
        matches.append(one_hot(column == ids))
        forces.append(tile)
        shift = lax.rem((start + m + LANES // capacity - me) * capacity, LANES)
        picked = jnp.where(slot_owner == start + m, pltpu.roll(tile, shift, 1), picked)
    pushed = sum3(dot_nt(stacked3(jnp.concatenate(forces, axis=1)), jnp.concatenate(matches, axis=1)))

    found = sum3(dot_nn(stacked3(jnp.concatenate(pairs, axis=0)), at_lane))
    row = iota((FAB, LANES), 0)
    fits = (row >= 4) & (row % parts == (my_node.astype(jnp.int32) >> 7))
    base = jnp.zeros((FAB, LANES), jnp.float32)
    for m in range(2 * len(pairs)):
        owner = chips[m // 2] * 2 + m % 2
        base = jnp.where(fits & (slot_owner == owner), found[m * FAB : (m + 1) * FAB], base)
    return jnp.concatenate([pushed, base, picked], axis=0)


def half_kernel(seed_ref, pair_ref, cross_ref, acc_ref, column_ref, lane_ref):
    place_y = lax.axis_index("gy")
    nodes, capacity = 4 * LANES, LANES // 8
    my_node = seed_ref[0:1]
    owner_base = (iota((1, LANES), 1) // capacity * nodes).astype(jnp.float32)
    my_id = jnp.where(my_node >= 0.0, owner_base + my_node, -2.0)
    column = jnp.transpose(jnp.broadcast_to(my_id, (LANES, LANES)))
    at_lane = one_hot(iota((LANES, LANES), 0) == (my_node.astype(jnp.int32) & (LANES - 1)))
    pairs, chips = [pair_ref[...], cross_ref[...]], [place_y, place_y ^ 2]
    acc_ref[...] = fabric_part(pairs, chips, 0, my_node, column, at_lane, nodes, capacity)
    column_ref[...] = column
    lane_ref[...] = at_lane


def final_kernel(
    rolled_ref, kind_ref, seed_ref, acc_ref, column_ref, lane_ref, near_ref, middle_ref, pos_ref,
    pop_hbm, pos_hbm, vel_hbm, wall_hbm,
    pop_ref, pos_out_ref, vel_out_ref, wall_out_ref, sems,
):
    size_x, size_y = rolled_ref.shape[1:3]
    place_y = lax.axis_index("gy")
    odd = lax.rem(place_y, 2) == 1
    first, top = place_y == 0, place_y == lax.axis_size("gy") - 1
    sub = iota((size_y, LANES), 0)
    owners, capacity = wall_out_ref.shape[4], wall_out_ref.shape[5]
    nodes = pos_ref.shape[2]
    parts = nodes // LANES
    mine = seed_ref[:FAB]
    pairs, chips = [near_ref[: 2 * FAB], near_ref[2 * FAB : 4 * FAB]], [place_y ^ 1, place_y ^ 3]
    acc = fabric_part(pairs, chips, 4, mine[0:1], column_ref[...], lane_ref[...], nodes, capacity) + acc_ref[...]
    copies = []
    for x in range(size_x):
        kind = kind_ref[x]
        for i in range(19):
            if not DIRECTIONS[i][1]:
                pop_ref[i, x] = rolled_ref[i, x]
                continue
            side = 0 if DIRECTIONS[i][1] == 1 else 1
            at = SIDES[1][side].index(i) * size_x + x
            by_near = near_ref[4 * FAB + at : 4 * FAB + at + 1]
            by_middle = middle_ref[at : at + 1]
            if side == 0:
                row = jnp.where(first, WEIGHTS[i], jnp.where(odd, by_near, by_middle))
                open_end = sub == 0
            else:
                row = jnp.where(top, WEIGHTS[i], jnp.where(odd, by_middle, by_near))
                open_end = sub == size_y - 1
            pop_ref[i, x] = jnp.where(open_end & (kind != float(i)), row, rolled_ref[i, x])

    pushed, found, picked = acc[:8], acc[8:24], acc[24:32]
    node = picked[0:1].astype(jnp.int32)
    row = iota((FAB, LANES), 0)
    spread = jnp.where(row < parts, picked[1:2], jnp.where(row < 2 * parts, picked[2:3], picked[3:4]))
    spread = jnp.where((row < 3 * parts) & (row % parts == (node >> 7)), spread, 0.0)
    at_node = one_hot(iota((LANES, LANES), 0) == (node & (LANES - 1)))
    fluid = sum3(dot_nt(stacked3(spread), at_node))
    my_live = mine[0:1] >= 0.0
    moved = []
    for a in range(3):
        for k in range(parts):
            r = a * parts + k
            new = mine[4 + r : 5 + r] + fluid[r : r + 1]
            at = slice(k * LANES, (k + 1) * LANES)
            vel_out_ref[a, :, at] = new
            pos_out_ref[a, :, at] = pos_ref[a, :, at] + new
        base = jnp.sum(found[4 + a * parts : 4 + (a + 1) * parts], axis=0, keepdims=True)
        moved.append(jnp.where(my_live, base + pushed[1 + a : 2 + a], 0.0))
    moved = jnp.concatenate(moved + [jnp.zeros((5, LANES), jnp.float32)], axis=0)
    for o in range(owners):
        turned = pltpu.roll(moved, LANES - o * capacity, 1) if o else moved
        for a in range(3):
            wall_out_ref[0, 0, 0, a, o : o + 1] = turned[a : a + 1, :capacity]
    copies.append(pltpu.make_async_copy(pop_ref, pop_hbm, sems.at[0]))
    copies[-1].start()
    for k, (src, dst) in enumerate(((vel_out_ref, vel_hbm), (pos_out_ref, pos_hbm), (wall_out_ref, wall_hbm))):
        copies.append(pltpu.make_async_copy(src, dst, sems.at[1 + k]))
        copies[-1].start()
    for copy in copies:
        copy.wait()


def ring(count, step):
    return [(i, (i + step) % count) for i in range(count)]


def body(
    populations,
    solid,
    link_cell,
    link_dir,
    link_node,
    link_velocity,
    fabric_position,
    fabric_velocity,
    fabric_rest,
    triangles,
):
    size_x, size_y, size_z = populations.shape[1:]
    owners, capacity = link_node.shape[3:]
    nodes = fabric_position.shape[2]
    count_x, count_y, count_z = (lax.axis_size(name) for name in ("gx", "gy", "gz"))
    folded = (
        (count_y, count_z) == (4, 2)
        and (size_y, size_z) == (8, LANES)
        and owners * capacity == LANES
        and nodes == 4 * LANES
    )
    if not folded:
        return general_body(
            populations, solid, link_cell, link_dir, link_node, link_velocity,
            fabric_position, fabric_velocity, fabric_rest, triangles,
        )
    f32 = jnp.float32
    on_chip = pl.BlockSpec(memory_space=pltpu.VMEM)

    def shape(*dims):
        return jax.ShapeDtypeStruct(dims, f32)

    def kept(*dims):
        return pltpu.VMEM(dims, f32)

    def run(kernel, outs, *args):
        args = [pltpu.with_memory_space_constraint(arg, pltpu.VMEM) for arg in args]
        return pl.pallas_call(
            kernel,
            out_shape=outs,
            in_specs=[on_chip] * len(args),
            out_specs=jax.tree.map(lambda _: on_chip, outs),
            name=kernel.__name__,
        )(*args)

    face_x = kept(5, size_y, size_z)
    map_shape = kept(size_x, size_y, size_z)
    given = (
        populations, solid, link_cell, link_dir, link_node, link_velocity,
        fabric_position, fabric_velocity, fabric_rest, triangles,
    )
    cells = size_x * size_y
    opened = (kept(*populations.shape), face_x, face_x, kept(max(SEED, FAB + cells), LANES), map_shape, map_shape, kept(*fabric_position.shape))
    post, up, down, seed, kind, back, position = pl.pallas_call(
        open_kernel,
        out_shape=opened,
        in_specs=[pl.BlockSpec(memory_space=pl.ANY)] * len(given),
        out_specs=(on_chip,) * len(opened),
        scratch_shapes=[pltpu.VMEM(arg.shape, arg.dtype) for arg in given if arg is not fabric_position]
        + [pltpu.SemaphoreType.DMA((len(given),))],
        name="open_kernel",
    )(*given)
    swap_z = [(0, 1), (1, 0)]
    other = lax.ppermute(seed, "gz", swap_z)
    xlow = lax.ppermute(up, "gx", ring(count_x, 1))
    xhigh = lax.ppermute(down, "gx", ring(count_x, -1))
    (pair,) = run(pair_kernel, (kept(2 * FAB, LANES),), seed, other)
    crossing = [(y * 2 + z, (y ^ 2) * 2 + 1 - z) for y in range(count_y) for z in range(2)]
    cross = lax.ppermute(pair, ("gy", "gz"), crossing)
    middling = []
    for y in range(count_y):
        to = y + 1 if y % 2 else y - 1
        for z in range(count_z):
            middling.append((y * 2 + z, to * 2 + z if 0 <= to < count_y else y * 2 + 1 - z))
    rows = -(-5 * size_x // 8) * 8
    middle, beside = run(
        sides_kernel, (kept(MID * rows, LANES), kept(size_y + rows, LANES)), post, xlow, xhigh, other
    )
    middle = lax.ppermute(middle, ("gy", "gz"), middling)
    beside = lax.ppermute(beside, "gz", swap_z)
    (near,) = run(near_kernel, (kept(4 * FAB + rows, LANES),), pair, cross, beside)
    nearing = [(y * 2 + z, (y ^ 1) * 2 + 1 - z) for y in range(count_y) for z in range(2)]
    near = lax.ppermute(near, ("gy", "gz"), nearing)
    (rolled,) = run(shift_kernel, (kept(*populations.shape),), post, xlow, xhigh, other, beside, kind, back)
    halves = (kept(32, LANES), kept(LANES, LANES), pltpu.VMEM((LANES, LANES), jnp.bfloat16))
    acc, column, at_lane = run(half_kernel, halves, seed, pair, cross)
    outs = (
        shape(*populations.shape),
        shape(*fabric_position.shape),
        shape(*fabric_velocity.shape),
        shape(*link_velocity.shape),
    )
    last = [rolled, kind, seed, acc, column, at_lane, near, middle, position]
    last = [pltpu.with_memory_space_constraint(arg, pltpu.VMEM) for arg in last]
    return pl.pallas_call(
        final_kernel,
        out_shape=outs,
        in_specs=[on_chip] * len(last),
        out_specs=(pl.BlockSpec(memory_space=pl.ANY),) * 4,
        scratch_shapes=[pltpu.VMEM(out.shape, f32) for out in outs] + [pltpu.SemaphoreType.DMA((4,))],
        name="final_kernel",
    )(*last)


def solution(mesh):
    placed = (
        P(None, "gx", "gy", "gz"),
        P("gx", "gy", "gz"),
        P("gx", "gy", "gz", None, None),
        P("gx", "gy", "gz", None, None),
        P("gx", "gy", "gz", None, None),
        P("gx", "gy", "gz", None, None, None),
        P(None, "gx", ("gy", "gz")),
        P(None, "gx", ("gy", "gz")),
        P(None, "gx", ("gy", "gz")),
        P(None, "gx", ("gy", "gz")),
    )
    return jax.shard_map(
        body,
        mesh=mesh,
        in_specs=placed,
        out_specs=(
            P(None, "gx", "gy", "gz"),
            P(None, "gx", ("gy", "gz")),
            P(None, "gx", ("gy", "gz")),
            P("gx", "gy", "gz", None, None, None),
        ),
        check_vma=False,
    )
```
